32 devices in a mesh: dp: 8 (over z, core), expert: 4 (over y, x).
Axes of the slice: x: 2, y: 2, z: 4, core: 2. Of those that a mesh axis runs over, the one named last changes fastest.
Arguments:
- patches: bfloat16 [8, 2048, 384], P('dp', 'expert'), may hold values from -6 to 6
- out_grad: bfloat16 [8, 2048, 384], P('dp', 'expert'), may hold values from -6 to 6
- image_of: int32 [8, 2048], P('dp'), may hold values from 0 to 2, never falling along the last dimension, each value on 1 to 1024 neighbouring positions
- task_of: int32 [8, 2048], P('dp', 'expert'), may hold values from 0 to 1
- routes: int32 [8, 2048, 4], P('dp', 'expert'), may hold values from 0 to 15, all different within a row; in each aligned block of 512 rows (0 to 511, 512 to 1023, ..., all dimensions but the last counted through in order) at most 256 rows name the same one
- norm_weight: float32 [4, 384], P(None, 'dp'), may hold values from -0.3 to 1.3, as said below
- norm_moment: float32 [4, 384], P(None, 'dp'), may hold values from -256 to 256
- norm_second: float32 [4, 384], P(None, 'dp'), may hold values from 147.456 to 589.824
- attend_weight: float32 [384, 1152], P('dp'), may hold values from -0.4375 to 0.4375
- attend_moment: float32 [384, 1152], P('dp'), may hold values from -128 to 128
- attend_second: float32 [384, 1152], P('dp'), may hold values from 36.864 to 147.456
- output_weight: float32 [384, 384], P('dp'), may hold values from -1.75 to 1.75
- output_moment: float32 [384, 384], P('dp'), may hold values from -24 to 24
- output_second: float32 [384, 384], P('dp'), may hold values from 1.47456 to 5.89824
- router_weight: float32 [2, 16, 384], P(None, None, 'dp'), may hold values from -0.15625 to 0.15625
- router_moment: float32 [2, 16, 384], P(None, None, 'dp'), may hold values from -320 to 320
- router_second: float32 [2, 16, 384], P(None, None, 'dp'), may hold values from 200.704 to 802.816
- expand_weight: float32 [16, 384, 1536], P('expert'), may hold values from -0.3125 to 0.3125
- expand_moment: float32 [16, 384, 1536], P('expert'), may hold values from -12 to 12
- expand_second: float32 [16, 384, 1536], P('expert'), may hold values from 0.36864 to 1.47456
- reduce_weight: float32 [16, 1536, 384], P('expert'), may hold values from -0.625 to 0.625
- reduce_moment: float32 [16, 1536, 384], P('expert'), may hold values from -4 to 4
- reduce_second: float32 [16, 1536, 384], P('expert'), may hold values from 0.1048576 to 0.4194304
Outputs:
- block_out: bfloat16 [8, 2048, 384], P('dp', 'expert')
- input_grad: float32 [8, 2048, 384], P('dp', 'expert')
- norm_weight_new: float32 [4, 384], P(None, 'dp')
- norm_moment_new: float32 [4, 384], P(None, 'dp')
- norm_second_new: float32 [4, 384], P(None, 'dp')
- attend_weight_new: float32 [384, 1152], P('dp')
- attend_moment_new: float32 [384, 1152], P('dp')
- attend_second_new: float32 [384, 1152], P('dp')
- output_weight_new: float32 [384, 384], P('dp')
- output_moment_new: float32 [384, 384], P('dp')
- output_second_new: float32 [384, 384], P('dp')
- router_weight_new: float32 [2, 16, 384], P(None, None, 'dp')
- router_moment_new: float32 [2, 16, 384], P(None, None, 'dp')
- router_second_new: float32 [2, 16, 384], P(None, None, 'dp')
- expand_weight_new: float32 [16, 384, 1536], P('expert')
- expand_moment_new: float32 [16, 384, 1536], P('expert')
- expand_second_new: float32 [16, 384, 1536], P('expert')
- reduce_weight_new: float32 [16, 1536, 384], P('expert')
- reduce_moment_new: float32 [16, 1536, 384], P('expert')
- reduce_second_new: float32 [16, 1536, 384], P('expert')
The draws below stay inside these ranges and needn't reach their ends.
Inputs may be any that keep to these rules, and one draw needn't show every extreme that they name: `image_of`: in each row, 3 images of consecutive patches numbered in order from 0, each of 1 to 1024 patches; one has exactly 1024. `routes`: A patch names 4 different experts. Within the rows of one device no expert is named by more than 256 rows, a bound that some block reaches. `norm_weight`: rows 0 and 2 are gains, rows 1 and 3 offsets.
All inputs are finite; a program needn't handle non-finite values.
Results may differ from the reference program's by a relative error of at most 0.024.
Values may be sent and summed in bfloat16 or wider, within the bound.
No kernel may reach another device: no remote copies, remote signals or barrier semaphores. Data moves between devices by JAX's collectives and lax.ppermute only.
A program may use at most 320 MiB of HBM per device.

```python
import math
import jax
import jax.numpy as jnp
import numpy as np
from jax import lax

D = 384
HEADS = 6
HEAD_DIM = 64
FFN = 1536
EXPERTS = 16
TASKS = 2
TOP = 4
STEP = 10
TOK_DEV = 512
GROUP = 2048
TOKENS = 16384
IMAGES = 3
IMG_MOST = 1024
CAP = 256
N_DP = 8
N_EXPERT = 4


def draw_norm_weight(key, part):
    key_gain = jax.random.fold_in(key, 11)
    key_shift = jax.random.fold_in(key, 23)
    gain_rows = 1.0 + 0.1 * jnp.clip(jax.random.normal(key_gain, (2, D), jnp.float32), -3.0, 3.0)
    shift_rows = 0.1 * jnp.clip(jax.random.normal(key_shift, (2, D), jnp.float32), -3.0, 3.0)
    return jnp.stack([gain_rows[0], shift_rows[0], gain_rows[1], shift_rows[1]]).astype(jnp.float32)


def with_ends(values, key, smallest, high):
    extent = values.shape
    place = [jax.random.randint(jax.random.fold_in(key, axis), (), 0, extent[axis]) for axis in range(len(extent))]
    values = values.at[tuple(place)].set(smallest)
    longest = extent.index(max(extent))
    place[longest] = (place[longest] + 1) % extent[longest]
    return values.at[tuple(place)].set(high)


def level_of(stream_key, dims, cuts, least, top_value):
    loudness = 1.0
    for dim, shards_of in cuts:
        steps = jax.random.uniform(jax.random.fold_in(jax.random.fold_in(stream_key, 6), dim), (shards_of,), jnp.float32, least / len(cuts), top_value / len(cuts))
        loudness = loudness * jnp.repeat(jnp.exp(steps), dims[dim] // shards_of).reshape((-1,) + (1,) * (len(dims) - 1 - dim))
    return loudness


def profile(amount, total, bound, lean):
    portions = [(1 << 20) // math.isqrt(standing ** lean) + 1 for standing in range(2, amount + 1)]
    rest, given = total - bound - (amount - 1), [1] * (amount - 1)
    while rest > 0:
        free = [i for i in range(amount - 1) if given[i] < bound]
        whole, left = sum([portions[i] for i in free]), rest
        for i in free:
            extra = min(bound - given[i], max(1, left * portions[i] // whole), rest)
            given[i] = given[i] + extra
            rest = rest - extra
    return np.array([bound] + given)


def uneven(key, count, total, limit, lean):
    if count == 2:
        one = jax.random.randint(key, (), max(1, total - limit), min(limit, total - 1) + 1)
        return jnp.stack([one, total - one])
    tallies = jnp.asarray(profile(count, total, limit, lean), jnp.int32)
    pairs = (count - 1) // 2
    giver, sink = tallies[1:1 + 2 * pairs:2], tallies[2:2 + 2 * pairs:2]
    room = jnp.minimum(giver - 1, limit - sink)
    shifted = jax.random.randint(jax.random.fold_in(key, 1), (pairs,), 0, 1 << 20) % (room + 1)
    tallies = tallies.at[1:1 + 2 * pairs:2].set(giver - shifted).at[2:2 + 2 * pairs:2].set(sink + shifted)
    return tallies[jax.random.permutation(jax.random.fold_in(key, 2), count)]


def deal_out(rng, own, number, rows, amount, top, reach, lean):
    ranking = jax.random.permutation(rng, amount)
    heavy_load, common = portions_of(amount, rows * top, reach, lean, True), portions_of(amount, rows * top, reach, lean, False)
    places = jnp.arange(amount)

    def named(sizes, rotation):
        used = int((sizes > 0).sum())
        fixed = max(1, used // 4)
        shifted = fixed + (places - fixed + rotation * (used - fixed)) % max(1, amount - fixed)
        return jnp.zeros((amount,), jnp.int32).at[ranking[jnp.where(places < fixed, places, shifted)]].set(jnp.asarray(sizes, jnp.int32))

    sizes = jnp.where(number % 4 == 0, named(heavy_load, number // 4), named(common, number - number // 4 - 1))
    mixed = jax.random.permutation(jax.random.fold_in(own, 3), amount)
    donor, receiver = mixed[0:amount // 2 * 2:2], mixed[1:amount // 2 * 2:2]
    slack = jnp.minimum(sizes[donor] - 1, reach - sizes[receiver]) // 2
    slack = jnp.where((donor == ranking[0]) | (receiver == ranking[0]) | (sizes[receiver] == 0), 0, jnp.maximum(slack, 0))
    shifted = jax.random.randint(jax.random.fold_in(own, 4), (amount // 2,), 0, 1 << 20) % (slack + 1)
    sizes = sizes.at[donor].add(-shifted).at[receiver].add(shifted)
    labels = jnp.searchsorted(jnp.cumsum(sizes), jnp.arange(rows * top), side="right").astype(jnp.int32)
    listing = labels.reshape(top, rows).T
    listing = listing[jax.random.permutation(jax.random.fold_in(own, 1), rows)]
    rotation = jax.random.randint(jax.random.fold_in(own, 2), (rows, 1), 0, top)
    return jnp.take_along_axis(listing, (jnp.arange(top)[None, :] + rotation) % top, axis=1)


def portions_of(number_of, total, limit, skew, full):
    loads = [(1 << 20) // math.isqrt(standing ** skew) + 1 for standing in range(1, number_of + 1)]
    largest = limit if full else min(limit, max(-(-total // number_of), total * loads[0] // sum(loads)))
    least = 1 if total - largest >= number_of - 1 else 0
    counts, rest = [largest] + [least] * (number_of - 1), total - largest - least * (number_of - 1)
    while rest > 0:
        movable = [i for i in range(1, number_of) if counts[i] < largest] or [i for i in range(1, number_of) if counts[i] < limit]
        mass, budget = sum([loads[i] for i in movable]), rest
        for i in movable:
            more = min(limit - counts[i], max(1, budget * loads[i] // mass), rest)
            counts[i] = counts[i] + more
            rest = rest - more
    return np.array(counts)


def noise(stream_key, shape, deviation, reach, cuts=(), kind=jnp.bfloat16):
    array = jax.random.normal(stream_key, shape, jnp.float32) * deviation
    if len(cuts) > 0:
        array = level_of(stream_key, shape, cuts, -0.22, 0.18) * array
    return jnp.clip(array, min=-reach, max=reach).astype(kind)


def setup_inputs(seed: int = 0) -> dict:
    arg_keys = jax.random.split(jax.random.key(seed), 24)
    patches = noise(arg_keys[0], (N_DP, GROUP, D), 1.0, 6.0, ((0, 8), (1, 4)))
    out_grad = noise(arg_keys[1], (N_DP, GROUP, D), 1.0, 6.0, ((0, 8), (1, 4)))
    image_of = jax.vmap(lambda own: jnp.searchsorted(jnp.cumsum(uneven(own, IMAGES, GROUP, IMG_MOST, 1)), jnp.arange(GROUP), side="right"))(jax.random.split(arg_keys[2], N_DP)).reshape((N_DP, GROUP)).astype(jnp.int32)
    task_of = with_ends(jax.random.randint(arg_keys[3], (N_DP, GROUP), 0, TASKS), jax.random.fold_in(arg_keys[3], 1), 0, TASKS - 1).astype(jnp.int32)
    routes_keys = jax.random.split(jax.random.fold_in(arg_keys[4], 1), N_DP * GROUP // TOK_DEV)
    routes_turns = jax.random.permutation(jax.random.fold_in(arg_keys[4], 3), N_DP * GROUP // TOK_DEV)
    routes = jax.vmap(lambda own, number: deal_out(jax.random.fold_in(arg_keys[4], 2), own, number, TOK_DEV, EXPERTS, TOP, CAP, 2))(routes_keys, routes_turns).reshape((N_DP, GROUP, TOP))
    norm_weight = draw_norm_weight(jax.random.fold_in(arg_keys[23], 71), 0)
    norm_moment = noise(arg_keys[6], (4, D), (0.333 * TOKENS ** 0.5), 256.0, ((1, 8),), jnp.float32)
    norm_second = jnp.clip(jnp.exp(math.log(589.824) - 1.3862944 * jax.random.uniform(arg_keys[7], (4, D), jnp.float32) ** level_of(arg_keys[7], (4, D), ((1, 8),), -0.2, 0.2)), 147.456, 589.824)
    attend_weight = noise(arg_keys[8], (D, 3 * D), (D // 2) ** -0.5, 0.4375, ((0, 8),), jnp.float32)
    attend_moment = noise(arg_keys[9], (D, 3 * D), (0.167 * TOKENS ** 0.5), 128.0, ((0, 8),), jnp.float32)
    attend_second = jnp.clip(jnp.exp(math.log(147.456) - 1.3862944 * jax.random.uniform(arg_keys[10], (D, 3 * D), jnp.float32) ** level_of(arg_keys[10], (D, 3 * D), ((0, 8),), -0.2, 0.2)), 36.864, 147.456)
    output_weight = noise(arg_keys[11], (D, D), (D // 32) ** -0.5, 1.75, ((0, 8),), jnp.float32)
    output_moment = noise(arg_keys[12], (D, D), (0.033 * TOKENS ** 0.5), 24.0, ((0, 8),), jnp.float32)
    output_second = jnp.clip(jnp.exp(math.log(5.89824) - 1.3862944 * jax.random.uniform(arg_keys[13], (D, D), jnp.float32) ** level_of(arg_keys[13], (D, D), ((0, 8),), -0.2, 0.2)), 1.47456, 5.89824)
    router_weight = noise(arg_keys[14], (TASKS, EXPERTS, D), (4 * D) ** -0.5, 0.15625, ((2, 8),), jnp.float32)
    router_moment = noise(arg_keys[15], (TASKS, EXPERTS, D), (0.389 * TOKENS ** 0.5), 320.0, ((2, 8),), jnp.float32)
    router_second = jnp.clip(jnp.exp(math.log(802.816) - 1.3862944 * jax.random.uniform(arg_keys[16], (TASKS, EXPERTS, D), jnp.float32) ** level_of(arg_keys[16], (TASKS, EXPERTS, D), ((2, 8),), -0.2, 0.2)), 200.704, 802.816)
    expand_weight = noise(arg_keys[17], (EXPERTS, D, FFN), D ** -0.5, 0.3125, ((0, 4),), jnp.float32)
    expand_moment = noise(arg_keys[18], (EXPERTS, D, FFN), (0.0167 * TOKENS ** 0.5), 12.0, ((0, 4),), jnp.float32)
    expand_second = jnp.clip(jnp.exp(math.log(1.47456) - 1.3862944 * jax.random.uniform(arg_keys[19], (EXPERTS, D, FFN), jnp.float32) ** level_of(arg_keys[19], (EXPERTS, D, FFN), ((0, 4),), -0.2, 0.2)), 0.36864, 1.47456)
    reduce_weight = noise(arg_keys[20], (EXPERTS, FFN, D), (FFN // 16) ** -0.5, 0.625, ((0, 4),), jnp.float32)
    reduce_moment = noise(arg_keys[21], (EXPERTS, FFN, D), (0.0089 * TOKENS ** 0.5), 4.0, ((0, 4),), jnp.float32)
    reduce_second = jnp.clip(jnp.exp(math.log(0.4194304) - 1.3862944 * jax.random.uniform(arg_keys[22], (EXPERTS, FFN, D), jnp.float32) ** level_of(arg_keys[22], (EXPERTS, FFN, D), ((0, 4),), -0.2, 0.2)), 0.1048576, 0.4194304)
    return dict(patches=patches, out_grad=out_grad, image_of=image_of, task_of=task_of, routes=routes, norm_weight=norm_weight, norm_moment=norm_moment, norm_second=norm_second, attend_weight=attend_weight, attend_moment=attend_moment, attend_second=attend_second, output_weight=output_weight, output_moment=output_moment, output_second=output_second, router_weight=router_weight, router_moment=router_moment, router_second=router_second, expand_weight=expand_weight, expand_moment=expand_moment, expand_second=expand_second, reduce_weight=reduce_weight, reduce_moment=reduce_moment, reduce_second=reduce_second)


@jax.custom_vjp
def low(v):
    return lax.optimization_barrier(v.astype(jnp.bfloat16)).astype(jnp.float32)

@jax.custom_vjp
def low_back(v):
    return v

def low_keep(v):
    return (low(v), None)

def low_pass(kept, grad):
    return (grad,)

def back_keep(v):
    return (v, None)

def back_low(kept, grad):
    return (low(grad),)
low.defvjp(low_keep, low_pass)
low_back.defvjp(back_keep, back_low)
NORM_EPS = 1e-06
ADAM_EPS = 1e-08
BETA_FIRST = 0.9
BETA_SECOND = 0.999
DECAY = 0.05
RATE_NORM = 0.5
RATE_ATTEND = 0.2
RATE_OUTPUT = 0.7
RATE_ROUTER = 0.06
RATE_EXPAND = 0.13
RATE_REDUCE = 0.25
MASKED = -1e+30

def gelu_exact(values):
    return 0.5 * values * (1.0 + lax.erf(values * 0.7071067811865476))

def norm_rows(values, gain_row, offset):
    average = lax.optimization_barrier(jnp.mean(values, axis=-1, keepdims=True))
    centred = values - average
    spread = lax.optimization_barrier(jnp.mean(centred * centred, axis=-1, keepdims=True))
    return centred * lax.rsqrt(spread + NORM_EPS) * gain_row + offset

def adamw(weight, moment, second, gradient, step_rate):
    moment = BETA_FIRST * moment + (1.0 - BETA_FIRST) * gradient
    second = BETA_SECOND * second + (1.0 - BETA_SECOND) * gradient * gradient
    first_hat = moment / (1.0 - BETA_FIRST ** STEP)
    second_hat = second / (1.0 - BETA_SECOND ** STEP)
    weight = weight - step_rate * (first_hat / (jnp.sqrt(second_hat) + ADAM_EPS) + DECAY * weight)
    return (weight, moment, second)

def gating(hidden, router, task_hot, route_hot):
    logits = jnp.einsum('td,ced->tce', hidden, router, precision=lax.Precision.HIGHEST)
    task_logits = jnp.einsum('tc,tce->te', task_hot, logits, precision=lax.Precision.HIGHEST)
    chosen = jnp.einsum('te,tke->tk', task_logits, route_hot, precision=lax.Precision.HIGHEST)
    highest = lax.optimization_barrier(jnp.max(chosen, axis=-1, keepdims=True))
    raised = jnp.exp(chosen - highest)
    return raised / lax.optimization_barrier(jnp.sum(raised, axis=-1, keepdims=True))

def slots_of(route_group):
    pair_expert = route_group.reshape(-1).astype(jnp.int32)
    pair_hot = (pair_expert[:, None] == jnp.arange(EXPERTS, dtype=jnp.int32)[None, :]).astype(jnp.int32)
    slot_index = lax.optimization_barrier(jnp.sum((jnp.cumsum(pair_hot, axis=0) - pair_hot) * pair_hot, axis=1))
    return (pair_expert * (N_EXPERT * CAP) + slot_index).astype(jnp.int32)

def forward(weights, inputs, image_row, task_hot, route_hot, flat_slot):
    norm_values, attend_full, output_full, router_full, expand_full, reduce_full = weights
    group_rows = inputs.shape[0]
    precise = lax.Precision.HIGHEST
    score_scale = HEAD_DIM ** (-0.5)
    normed_one = low(norm_rows(inputs, norm_values[0], norm_values[1]))
    packed = low_back(low(jnp.dot(normed_one, attend_full, precision=precise)))
    queries = packed[:, :D].reshape(group_rows, HEADS, HEAD_DIM)
    keys_all = packed[:, D:2 * D].reshape(group_rows, HEADS, HEAD_DIM)
    values_all = packed[:, 2 * D:].reshape(group_rows, HEADS, HEAD_DIM)
    block_rows = min(512, group_rows)
    count_blocks = group_rows // block_rows

    def one_block(carry_in, block_in):
        query_part, image_part = block_in
        raw = low_back(jnp.einsum('thd,khd->htk', query_part, keys_all, precision=precise) * score_scale)
        same_image = image_part[:, None] == image_row[None, :]
        masked = jnp.where(same_image[None], raw, MASKED)
        highest = lax.optimization_barrier(jnp.max(masked, axis=-1, keepdims=True))
        raised = jnp.exp(masked - highest)
        soft_part = low(raised / lax.optimization_barrier(jnp.sum(raised, axis=-1, keepdims=True)))
        return (carry_in, jnp.einsum('htk,khd->thd', soft_part, values_all, precision=precise))
    attended = lax.scan(jax.checkpoint(one_block), None, (queries.reshape(count_blocks, block_rows, HEADS, HEAD_DIM), image_row.reshape(count_blocks, block_rows)))[1]
    attended = low(low_back(attended.reshape(group_rows, D)))
    branch = low_back(jnp.dot(attended, output_full, precision=precise))
    middle = inputs + branch
    mixed = low(norm_rows(middle, norm_values[2], norm_values[3]))
    gate_values = gating(mixed, router_full, task_hot, route_hot)
    pair_rows = low_back(jnp.repeat(mixed, TOP, axis=0))
    group_cap = N_EXPERT * CAP
    buffer = jnp.zeros((EXPERTS * group_cap, D), jnp.float32).at[flat_slot].set(pair_rows).reshape(EXPERTS, group_cap, D)
    hidden_pre = low_back(jnp.einsum('ecd,edh->ech', buffer, expand_full, precision=precise))
    active = low(gelu_exact(hidden_pre))
    expert_out = low_back(low(jnp.einsum('ech,ehd->ecd', active, reduce_full, precision=precise)))
    pair_out = expert_out.reshape(EXPERTS * group_cap, D)[flat_slot].reshape(group_rows, TOP, D)
    expert_mix = jnp.einsum('tk,tkd->td', gate_values, pair_out, precision=precise)
    return middle + expert_mix

def reference(patches, out_grad, image_of, task_of, routes, norm_weight, norm_moment, norm_second, attend_weight, attend_moment, attend_second, output_weight, output_moment, output_second, router_weight, router_moment, router_second, expand_weight, expand_moment, expand_second, reduce_weight, reduce_moment, reduce_second):
    masters = (norm_weight, attend_weight, output_weight, router_weight, expand_weight, reduce_weight)
    weights = tuple((low(master) for master in masters))

    def group_step(totals, group_in):
        patch_group, grad_group, image_row, task_row, route_group = group_in
        task_hot = (task_row[:, None] == jnp.arange(TASKS, dtype=jnp.int32)[None, :]).astype(jnp.float32)
        route_hot = (route_group[:, :, None] == jnp.arange(EXPERTS, dtype=jnp.int32)[None, None, :]).astype(jnp.float32)
        flat_slot = slots_of(route_group)

        def run_group(params, inputs):
            return forward(params, inputs, image_row, task_hot, route_hot, flat_slot)
        result, pullback = jax.vjp(run_group, weights, patch_group.astype(jnp.float32))
        param_grads, input_grad = pullback(grad_group.astype(jnp.float32))
        totals = jax.tree.map(jnp.add, totals, param_grads)
        return (totals, (result.astype(jnp.bfloat16), input_grad))
    initial = tuple((jnp.zeros_like(master) for master in weights))
    totals, outputs = lax.scan(group_step, initial, (patches, out_grad, image_of, task_of, routes))
    block_out, input_grad = outputs
    norm_sum, attend_sum, output_sum, router_sum, expand_sum, reduce_sum = totals
    norm_new = adamw(norm_weight, norm_moment, norm_second, norm_sum, RATE_NORM)
    attend_new = adamw(attend_weight, attend_moment, attend_second, attend_sum, RATE_ATTEND)
    output_new = adamw(output_weight, output_moment, output_second, output_sum, RATE_OUTPUT)
    router_new = adamw(router_weight, router_moment, router_second, router_sum, RATE_ROUTER)
    expand_new = adamw(expand_weight, expand_moment, expand_second, expand_sum, RATE_EXPAND)
    reduce_new = adamw(reduce_weight, reduce_moment, reduce_second, reduce_sum, RATE_REDUCE)
    return (block_out, input_grad, norm_new[0], norm_new[1], norm_new[2], attend_new[0], attend_new[1], attend_new[2], output_new[0], output_new[1], output_new[2], router_new[0], router_new[1], router_new[2], expand_new[0], expand_new[1], expand_new[2], reduce_new[0], reduce_new[1], reduce_new[2])
```

```python
import functools

import jax
import jax.numpy as jnp
from jax import lax
from jax.experimental import pallas as pl
from jax.experimental.pallas import tpu as pltpu
from jax.sharding import PartitionSpec as P

D = 384
HEADS = 6
HEAD_DIM = 64
FFN = 1536
EXPERTS = 16
TASKS = 2
TOP = 4
STEP = 10
CAP = 256
PAIRS = HEADS // 2
LANES = 128
WCOLS = 4 * D + LANES
INFO = 16
NORM_AT = 2 * EXPERTS
EXTRA = 64

NORM_EPS = 1e-06
ADAM_EPS = 1e-08
BETA_FIRST = 0.9
BETA_SECOND = 0.999
DECAY = 0.05
RATE_NORM = 0.5
RATE_ATTEND = 0.2
RATE_OUTPUT = 0.7
RATE_ROUTER = 0.06
RATE_EXPAND = 0.13
RATE_REDUCE = 0.25
MASKED = -1e30
F32 = jnp.float32
BF16 = jnp.bfloat16


def dot_nn(a, b):
    return lax.dot_general(a, b, (((1,), (0,)), ((), ())), preferred_element_type=F32)


def dot_nt(a, b):
    return lax.dot_general(a, b, (((1,), (1,)), ((), ())), preferred_element_type=F32)


def dot_tn(a, b):
    return lax.dot_general(a, b, (((0,), (0,)), ((), ())), preferred_element_type=F32)


def unit_rows(values):
    average = jnp.mean(values, axis=-1, keepdims=True)
    centred = values - average
    spread = jnp.mean(centred * centred, axis=-1, keepdims=True)
    scale = lax.rsqrt(spread + NORM_EPS)
    return centred * scale, scale


def eye(n):
    rows = lax.broadcasted_iota(jnp.int32, (n, n), 0)
    cols = lax.broadcasted_iota(jnp.int32, (n, n), 1)
    return (rows == cols).astype(F32).astype(BF16)


def norm_rows_of(full_ref):
    return dot_nt(eye(LANES), full_ref[:, 4 * D :])[NORM_AT : NORM_AT + 8]


def vmem():
    return pl.BlockSpec(memory_space=pltpu.VMEM)


def smem():
    return pl.BlockSpec(memory_space=pltpu.SMEM)


def route_kernel(meta, i0, i1, i2, i3, row_out, col_out, plan_out):
    base = meta[0]
    rows = i0.shape[1] + LANES
    later = lax.broadcasted_iota(jnp.int32, (rows, rows), 0)
    token = lax.broadcasted_iota(jnp.int32, (rows, rows), 1)
    before = (later < token).astype(F32).astype(BF16)
    one = (later == token).astype(F32).astype(BF16)
    local = row_out.shape[0]
    which = lax.broadcasted_iota(jnp.int32, (local, rows), 0)
    slot_names = (which + base).astype(F32)
    every = lax.broadcasted_iota(jnp.int32, (EXPERTS, rows), 0).astype(F32)
    experts = plan_out.shape[0] // 8
    starts = [jnp.int32(0)] * experts
    for d, ref in enumerate((i0, i1, i2, i3)):
        info = ref[...].astype(F32)

        def line(k):
            return jnp.concatenate([info[2 * k : 2 * k + 1], info[2 * k + 1 : 2 * k + 2, :LANES]], axis=1)

        mine = jnp.zeros((local, rows), jnp.bool_)
        chosen = jnp.zeros((EXPERTS, rows), jnp.bool_)
        for k in range(TOP):
            named = line(k)
            mine = mine | (slot_names == named)
            chosen = chosen | (every == named)
        mine = jnp.where(mine & (which < experts), 1.0, 0.0)
        chosen = jnp.where(chosen, 1.0, 0.0)
        rank = dot_nn(mine.astype(BF16), before)
        spot = jnp.where(mine > 0.5, rank, -1.0)
        row_out[:, d * rows : (d + 1) * rows] = spot
        tasks = jnp.broadcast_to(line(TOP), (8, rows))
        table = jnp.concatenate(
            [spot, jnp.zeros((16 - local, rows), F32), chosen, tasks, jnp.zeros((LANES - 40, rows), F32)],
            axis=0,
        )
        col_out[d * rows : (d + 1) * rows, :] = dot_nt(one, table.astype(BF16))
        for e in range(experts):
            held = jnp.sum(mine[e : e + 1, :]).astype(jnp.int32)
            plan_out[e * 8 + d] = starts[e]
            starts[e] = starts[e] + (held + 15) // 16 * 16
    for e in range(experts):
        plan_out[e * 8 + 4] = starts[e]
        plan_out[e * 8 + 5] = (starts[e] + CAP - 1) // CAP


def route_call(meta, pieces, experts):
    rows = pieces[0].shape[0] - INFO
    return pl.pallas_call(
        route_kernel,
        grid=(1,),
        in_specs=[smem()] + [pl.BlockSpec((INFO, D), lambda i: (rows // INFO, 0))] * 4,
        out_specs=(
            pl.BlockSpec((8, 4 * rows), lambda i: (0, 0)),
            pl.BlockSpec((4 * rows, LANES), lambda i: (0, 0)),
            smem(),
        ),
        out_shape=(
            jax.ShapeDtypeStruct((8, 4 * rows), F32),
            jax.ShapeDtypeStruct((4 * rows, LANES), F32),
            jax.ShapeDtypeStruct((experts * 8,), jnp.int32),
        ),
        name="routing",
    )(meta, *pieces)


def front_kernel(
    meta, image, p0, p1, p2, p3, w0, w1, w2, w3, w4, w5, w6, w7,
    qkv, full, att, lse_col, lse_row, middle, mixed,
    everything, scores, top, total, out_acc,
):
    rows = att.shape[0]
    for j, ref in enumerate((w0, w1, w2, w3, w4, w5, w6, w7)):
        full[pl.ds(pl.multiple_of(meta[16 + j], 16), ref.shape[0]), :] = ref[...]
    for d, ref in enumerate((p0, p1, p2, p3)):
        everything[d * rows : (d + 1) * rows, :] = ref[:rows, :]
    norms = norm_rows_of(full)
    tile = 256

    def project(i, carry):
        at = pl.ds(pl.multiple_of(i * tile, tile), tile)
        unit, _ = unit_rows(everything[at, :].astype(F32))
        normed = (unit * norms[0:1] + norms[1:2]).astype(BF16)
        for third in range(3):
            made = dot_nn(normed, full[:, third * D : (third + 1) * D]).astype(BF16)
            if third == 0:
                made = made * jnp.asarray(HEAD_DIM ** (-0.5), BF16)
            for part in range(PAIRS):
                qkv[third * PAIRS + part, at, :] = made[:, part * LANES : (part + 1) * LANES]
        return carry

    lax.fori_loop(0, 4 * rows // tile, project, 0)
    own_row = image[pl.ds(meta[4], 1), :].astype(F32)
    own_col = jnp.transpose(jnp.broadcast_to(own_row, (LANES, rows)))[:, :1]
    lane = lax.broadcasted_iota(jnp.int32, (rows, LANES), 1)
    lse_col[...] = jnp.zeros_like(lse_col)

    def pair_of_heads(pair, carry):
        done = []
        for half in range(2):
            held = (lane < HEAD_DIM) if half == 0 else (lane >= HEAD_DIM)
            query = jnp.where(held, qkv[pair, 0:rows, :], jnp.zeros((), BF16))
            top[...] = jnp.full_like(top, MASKED)

            def score(d, c):
                @pl.when(meta[8 + d] > 0)
                def _():
                    key = qkv[PAIRS + pair, pl.ds(pl.multiple_of(d * rows, rows), rows), :]
                    same = own_col == image[pl.ds(meta[4 + d], 1), :].astype(F32)
                    raw = jnp.where(same, dot_nt(query, key), MASKED)
                    scores[d] = raw
                    top[...] = jnp.maximum(top[...], jnp.max(raw, axis=1, keepdims=True))

                return c

            lax.fori_loop(0, 4, score, 0)
            total[...] = jnp.zeros_like(total)
            out_acc[...] = jnp.zeros_like(out_acc)
            peak = top[:, :1]

            def weigh(d, c):
                @pl.when(meta[8 + d] > 0)
                def _():
                    value = qkv[2 * PAIRS + pair, pl.ds(pl.multiple_of(d * rows, rows), rows), :]
                    shares = jnp.exp(scores[d] - peak)
                    total[...] += jnp.sum(shares, axis=1, keepdims=True)
                    out_acc[...] += dot_nn(shares.astype(BF16), value)

                return c

            lax.fori_loop(0, 4, weigh, 0)
            done.append(out_acc[...] / total[:, :1])
            lse_col[...] = jnp.where(lane == 2 * pair + half, peak + jnp.log(total[:, :1]), lse_col[...])
        att[:, pl.ds(pl.multiple_of(pair * LANES, LANES), LANES)] = jnp.where(lane < HEAD_DIM, done[0], done[1])
        return carry

    lax.fori_loop(0, PAIRS, pair_of_heads, 0)
    lse_row[...] = jnp.transpose(lse_col[...])[:8]
    branch = dot_nn(att[...].astype(BF16), full[:, 3 * D : 4 * D])
    centre = everything[0:rows, :].astype(F32) + branch
    middle[...] = centre
    unit, _ = unit_rows(centre)
    mixed[...] = (unit * norms[2:3] + norms[3:4]).astype(BF16)


def front_call(meta, image, pieces, shards):
    rows = pieces[0].shape[0] - INFO
    return pl.pallas_call(
        front_kernel,
        in_specs=[smem()] + [vmem()] * 13,
        out_specs=(vmem(),) * 7,
        out_shape=(
            jax.ShapeDtypeStruct((3 * PAIRS, 4 * rows, LANES), BF16),
            jax.ShapeDtypeStruct((D, WCOLS), BF16),
            jax.ShapeDtypeStruct((rows, D), F32),
            jax.ShapeDtypeStruct((rows, LANES), F32),
            jax.ShapeDtypeStruct((8, rows), F32),
            jax.ShapeDtypeStruct((rows, D), F32),
            jax.ShapeDtypeStruct((rows, D), BF16),
        ),
        scratch_shapes=[
            pltpu.VMEM((4 * rows, D), BF16),
            pltpu.VMEM((4, rows, rows), F32),
            pltpu.VMEM((rows, 1), F32),
            pltpu.VMEM((rows, 1), F32),
            pltpu.VMEM((rows, LANES), F32),
        ],
        name="front",
    )(meta, image, *pieces, *shards)


def expert_kernel(
    plan, meta, m0, m1, m2, m3, g0, g1, g2, g3, spot_row, spot_col, full, up, down,
    mine, other, back_out, mix_out, router_out,
    gates, terms, back_acc, mix_acc, hidden, upstream, results, low_up, low_down, sum_up, sum_down,
):
    step = pl.program_id(0)
    last = pl.num_programs(0) - 1
    base, core = meta[0], meta[1]
    rows = m0.shape[0]
    lane = lax.broadcasted_iota(jnp.int32, (rows, LANES), 1)

    @pl.when(step == 0)
    def _():
        hidden[...] = jnp.zeros_like(hidden)
        upstream[...] = jnp.zeros_like(upstream)
        results[...] = jnp.zeros_like(results)
        terms[...] = jnp.zeros_like(terms)
        back_acc[...] = jnp.zeros_like(back_acc)
        mix_acc[...] = jnp.zeros_like(mix_acc)
        for d, ref in enumerate((m0, m1, m2, m3)):
            at = slice(d * rows, (d + 1) * rows)
            both = dot_nn(ref[...], full[:, 4 * D :])
            info = spot_col[at, :]
            task = info[:, 32:33]
            logits = jnp.where(task < 0.5, both, pltpu.roll(both, LANES - EXPERTS, 1))
            chosen = pltpu.roll(info, LANES - 16, 1)
            open_ = (lane < EXPERTS) & (chosen > 0.5)
            logits = jnp.where(open_, logits, MASKED)
            raised = jnp.where(open_, jnp.exp(logits - jnp.max(logits, axis=1, keepdims=True)), 0.0)
            gates[at, :] = raised / jnp.sum(raised, axis=1, keepdims=True)

    low_up[...] = up[0].astype(BF16)
    low_down[...] = down[0].astype(BF16)
    expert = base + step
    slot_at = lax.broadcasted_iota(jnp.int32, (CAP, rows), 0).astype(F32)
    slot_along = lax.broadcasted_iota(jnp.int32, (rows, CAP), 1).astype(F32)
    mixes = (m0, m1, m2, m3)
    grads = (g0, g1, g2, g3)
    for d in range(4):
        at = slice(d * rows, (d + 1) * rows)
        spots = spot_row[pl.ds(step, 1), at]
        pick = jnp.where(slot_at == spots, 1.0, 0.0).astype(BF16)
        gate = jnp.sum(jnp.where(lane == expert, gates[at, :], 0.0), axis=1, keepdims=True)
        scaled = (gate * grads[d][...].astype(F32)).astype(BF16)
        start = pl.multiple_of(plan[step * 8 + d], 16)
        hidden[pl.ds(start, CAP), :] = dot_nn(pick, mixes[d][...]).astype(BF16)
        upstream[pl.ds(start, CAP), :] = dot_nn(pick, scaled).astype(BF16)
    ending = pl.multiple_of(plan[step * 8 + 4], 16)
    hidden[pl.ds(ending, CAP), :] = jnp.zeros((CAP, D), BF16)
    upstream[pl.ds(ending, CAP), :] = jnp.zeros((CAP, D), BF16)
    sum_up[...] = jnp.zeros_like(sum_up)
    sum_down[...] = jnp.zeros_like(sum_down)
    wide = 512

    def tile(i, carry):
        at = pl.ds(pl.multiple_of(i * CAP, CAP), CAP)
        x = hidden[at, :]
        g = upstream[at, :]
        x_t = jnp.transpose(x)
        g_t = jnp.transpose(g)
        made = jnp.zeros((CAP, D), F32)
        back = jnp.zeros((CAP, D), F32)
        for j in range(FFN // wide):
            cols = slice(j * wide, (j + 1) * wide)
            pre = dot_nn(x, low_up[:, cols])
            pull = dot_nt(g, low_down[cols, :])
            share = 0.5 + 0.5 * lax.erf(pre * 0.7071067811865476)
            active = (pre * share).astype(BF16)
            slope = share + pre * (0.3989422804014327 * jnp.exp(-0.5 * pre * pre))
            pre_grad = (slope * pull).astype(BF16)
            made = made + dot_nn(active, low_down[cols, :])
            back = back + dot_nt(pre_grad, low_up[:, cols])
            sum_up[:, cols] += dot_nn(x_t, pre_grad)
            sum_down[:, cols] += dot_nn(g_t, active)
        results[at, :D] = made.astype(BF16)
        results[at, D:] = back.astype(BF16)
        return carry

    lax.fori_loop(0, plan[step * 8 + 5], tile, 0)
    for d in range(4):
        at = slice(d * rows, (d + 1) * rows)
        info = spot_col[at, :]
        spots = jnp.sum(jnp.where(lane == step, info, 0.0), axis=1, keepdims=True)
        put = jnp.where(slot_along == spots, 1.0, 0.0).astype(BF16)
        start = pl.multiple_of(plan[step * 8 + d], 16)
        got = dot_nn(put, results[pl.ds(start, CAP), :])
        gate = jnp.sum(jnp.where(lane == expert, gates[at, :], 0.0), axis=1, keepdims=True)
        out = got[:, :D]
        gained = jnp.sum(grads[d][...].astype(F32) * out, axis=1, keepdims=True)
        terms[at, :] = jnp.where(lane == expert, gate * gained, terms[at, :])
        mix_acc[at, :] += gate * out
        back_acc[at, :] += got[:, D:]
    half = FFN // 2
    for b in range(2):
        for ref, side in ((mine, core), (other, 1 - core)):
            cols = pl.ds(pl.multiple_of(side * half + b * D, LANES), D)
            ref[0, b * D : (b + 1) * D, :] = sum_down[:, cols].astype(BF16)
            ref[0, (2 + b) * D : (3 + b) * D, :] = sum_up[:, cols].astype(BF16)

    @pl.when(step == last)
    def _():
        total = jnp.zeros((D, LANES), F32)
        for d, ref in enumerate((m0, m1, m2, m3)):
            at = slice(d * rows, (d + 1) * rows)
            held = terms[at, :]
            change = held - jnp.sum(held, axis=1, keepdims=True) * gates[at, :]
            task = spot_col[at, 32:33]
            first = jnp.where((lane < EXPERTS) & (task < 0.5), change, 0.0)
            second = jnp.where(
                (lane >= EXPERTS) & (lane < 2 * EXPERTS) & (task > 0.5), pltpu.roll(change, EXPERTS, 1), 0.0
            )
            both = first + second
            high = both.astype(BF16)
            low = (both - high.astype(F32)).astype(BF16)
            routers = full[:, 4 * D :]
            pulled = dot_nt(high, routers) + dot_nt(low, routers)
            total = total + dot_tn(ref[...], high) + dot_tn(ref[...], low)
            back_out[d] = (back_acc[at, :] + pulled).astype(BF16)
            mix_out[d] = mix_acc[at, :].astype(BF16)
        router_out[...] = total


def expert_call(plan, meta, mixes, grads, spot_row, spot_col, full, up, down):
    rows = mixes[0].shape[0]
    count = up.shape[0]
    slots = 4 * CAP + CAP

    def whole(shape):
        return pl.BlockSpec(shape, lambda e, *_: (0,) * len(shape), pipeline_mode=pl.Buffered(1))

    return pl.pallas_call(
        expert_kernel,
        grid_spec=pltpu.PrefetchScalarGridSpec(
            num_scalar_prefetch=2,
            grid=(count,),
            in_specs=[whole((rows, D))] * 8
            + [
                whole((8, 4 * rows)),
                whole((4 * rows, LANES)),
                whole((D, WCOLS)),
                pl.BlockSpec((1, D, FFN), lambda e, *_: (e, 0, 0)),
                pl.BlockSpec((1, FFN, D), lambda e, *_: (e, 0, 0)),
            ],
            out_specs=(
                pl.BlockSpec((1, 4 * D, D), lambda e, *_: (e, 0, 0)),
                pl.BlockSpec((1, 4 * D, D), lambda e, *_: (e, 0, 0)),
                whole((4, rows, D)),
                whole((4, rows, D)),
                whole((D, LANES)),
            ),
            scratch_shapes=[
                pltpu.VMEM((4 * rows, LANES), F32),
                pltpu.VMEM((4 * rows, LANES), F32),
                pltpu.VMEM((4 * rows, D), F32),
                pltpu.VMEM((4 * rows, D), F32),
                pltpu.VMEM((slots, D), BF16),
                pltpu.VMEM((slots, D), BF16),
                pltpu.VMEM((slots, 2 * D), BF16),
                pltpu.VMEM((D, FFN), BF16),
                pltpu.VMEM((FFN, D), BF16),
                pltpu.VMEM((D, FFN), F32),
                pltpu.VMEM((D, FFN), F32),
            ],
        ),
        out_shape=(
            jax.ShapeDtypeStruct((count, 4 * D, D), BF16),
            jax.ShapeDtypeStruct((count, 4 * D, D), BF16),
            jax.ShapeDtypeStruct((4, rows, D), BF16),
            jax.ShapeDtypeStruct((4, rows, D), BF16),
            jax.ShapeDtypeStruct((D, LANES), F32),
        ),
        name="experts",
    )(plan, meta, *mixes, *grads, spot_row, spot_col, full, up, down)


def turn_kernel(b0, r1, r2, r3, middle, grad, full, att, lse_row, middle_grad, sent, dots_col, output_grad, norm_two):
    rows = middle.shape[0]
    norms = norm_rows_of(full)
    mixed_grad = b0[0].astype(F32) + r1[...].astype(F32) + r2[...].astype(F32) + r3[...].astype(F32)
    unit, scale = unit_rows(middle[...])
    norm_two[...] = jnp.zeros_like(norm_two)
    norm_two[0:1, :] = jnp.sum(mixed_grad * unit, axis=0, keepdims=True)
    norm_two[1:2, :] = jnp.sum(mixed_grad, axis=0, keepdims=True)
    pulled = mixed_grad * norms[2:3]
    through = pulled - jnp.mean(pulled, axis=1, keepdims=True)
    through = scale * (through - unit * jnp.mean(pulled * unit, axis=1, keepdims=True))
    whole = through + grad[...].astype(F32)
    middle_grad[...] = whole
    branch = whole.astype(BF16)
    output_grad[...] = dot_tn(att[...].astype(BF16), branch).astype(BF16)
    pulled = dot_nt(branch, full[:, 3 * D : 4 * D]).astype(BF16)
    sent[0:rows, :] = pulled
    product = pulled.astype(F32) * att[...]
    high = product.astype(BF16)
    low = (product - high.astype(F32)).astype(BF16)
    heads = (
        lax.broadcasted_iota(jnp.int32, (D, LANES), 0) // HEAD_DIM
        == lax.broadcasted_iota(jnp.int32, (D, LANES), 1)
    )
    heads = heads.astype(F32).astype(BF16)
    dots = dot_nn(high, heads) + dot_nn(low, heads)
    dots_col[...] = dots
    lines = jnp.concatenate([lse_row[...], jnp.transpose(dots)[:8]], axis=0)
    high = lines.astype(BF16).astype(F32)
    table = jnp.concatenate([high, lines - high], axis=0).astype(BF16)
    half = EXTRA // 2
    sent[rows : rows + half, :] = table[:, :D]
    sent[rows + half : rows + EXTRA, :] = jnp.zeros((half, D), BF16)
    sent[rows + half : rows + EXTRA, : rows - D] = table[:, D:]


def turn_call(back, received, middle, grad, full, att, lse_row):
    rows = middle.shape[0]
    return pl.pallas_call(
        turn_kernel,
        grid=(1,),
        in_specs=[pl.BlockSpec((1, rows, D), lambda i: (0, 0, 0))] + [vmem()] * 8,
        out_specs=(vmem(),) * 5,
        out_shape=(
            jax.ShapeDtypeStruct((rows, D), F32),
            jax.ShapeDtypeStruct((rows + EXTRA, D), BF16),
            jax.ShapeDtypeStruct((rows, LANES), F32),
            jax.ShapeDtypeStruct((D, D), BF16),
            jax.ShapeDtypeStruct((8, D), F32),
        ),
        name="turn",
    )(back, *received, middle, grad, full, att, lse_row)


def attention_back_kernel(
    meta, image, qkv, s0, s1, s2, s3, lse_col, dots_col, own, full, middle_grad, output_grad, norm_two, routers,
    input_grad, shared,
    lines, grads, packed, acc_one, acc_two,
):
    rows = input_grad.shape[0]
    half_extra = EXTRA // 2
    for d, ref in enumerate((s0, s1, s2, s3)):
        grads[d] = ref[0:rows, :]
        table = jnp.concatenate(
            [ref[rows : rows + half_extra, :], ref[rows + half_extra : rows + EXTRA, : rows - D]], axis=1
        ).astype(F32)
        lines[d] = table[:16] + table[16:]
    own_row = image[pl.ds(meta[4], 1), :].astype(F32)
    own_col = jnp.transpose(jnp.broadcast_to(own_row, (LANES, rows)))[:, :1]
    lane = lax.broadcasted_iota(jnp.int32, (rows, LANES), 1)
    none = jnp.zeros((), BF16)
    here = slice(0, rows)

    def pair_of_heads(pair, carry):
        lanes = pl.ds(pl.multiple_of(pair * LANES, LANES), LANES)
        made = []
        for half in range(2):
            head = 2 * pair + half
            held = (lane < HEAD_DIM) if half == 0 else (lane >= HEAD_DIM)
            query = jnp.where(held, qkv[pair, here, :], none)
            pull = jnp.where(held, grads[0, :, lanes], none)
            log_total = jnp.sum(jnp.where(lane == head, lse_col[...], 0.0), axis=1, keepdims=True)
            dots = jnp.sum(jnp.where(lane == head, dots_col[...], 0.0), axis=1, keepdims=True)
            acc_one[...] = jnp.zeros_like(acc_one)

            def over_keys(d, c):
                @pl.when(meta[8 + d] > 0)
                def _():
                    at = pl.ds(pl.multiple_of(d * rows, rows), rows)
                    key = qkv[PAIRS + pair, at, :]
                    same = own_col == image[pl.ds(meta[4 + d], 1), :].astype(F32)
                    shares = jnp.where(same, jnp.exp(dot_nt(query, key) - log_total), 0.0)
                    change = dot_nt(pull, qkv[2 * PAIRS + pair, at, :]) - dots
                    acc_one[...] += dot_nn((shares * change).astype(BF16), key)

                return c

            lax.fori_loop(0, 4, over_keys, 0)
            made.append(acc_one[...])
        packed[:, lanes] = jnp.where(lane < HEAD_DIM, made[0], made[1]) * (HEAD_DIM ** (-0.5))
        made = []
        for half in range(2):
            head = 2 * pair + half
            held = (lane < HEAD_DIM) if half == 0 else (lane >= HEAD_DIM)
            key = jnp.where(held, qkv[PAIRS + pair, here, :], none)
            value = jnp.where(held, qkv[2 * PAIRS + pair, here, :], none)
            acc_one[...] = jnp.zeros_like(acc_one)
            acc_two[...] = jnp.zeros_like(acc_two)

            def over_queries(d, c):
                @pl.when(meta[8 + d] > 0)
                def _():
                    at = pl.ds(pl.multiple_of(d * rows, rows), rows)
                    query = qkv[pair, at, :]
                    pull = grads[d, :, lanes]
                    same = own_col == image[pl.ds(meta[4 + d], 1), :].astype(F32)
                    log_total = lines[d, pl.ds(head, 1), :]
                    dots = lines[d, pl.ds(8 + head, 1), :]
                    shares = jnp.where(same, jnp.exp(dot_nt(key, query) - log_total), 0.0)
                    change = dot_nt(value, pull) - dots
                    acc_two[...] += dot_nn(shares.astype(BF16), pull)
                    acc_one[...] += dot_nn((shares * change).astype(BF16), query)

                return c

            lax.fori_loop(0, 4, over_queries, 0)
            made.append((acc_one[...], acc_two[...]))
        shift = pl.ds(pl.multiple_of(D + pair * LANES, LANES), LANES)
        packed[:, shift] = jnp.where(lane < HEAD_DIM, made[0][0], made[1][0])
        shift = pl.ds(pl.multiple_of(2 * D + pair * LANES, LANES), LANES)
        packed[:, shift] = jnp.where(lane < HEAD_DIM, made[0][1], made[1][1])
        return carry

    lax.fori_loop(0, PAIRS, pair_of_heads, 0)
    norms = norm_rows_of(full)
    unit, scale = unit_rows(own[0:rows, :].astype(F32))
    normed = (unit * norms[0:1] + norms[1:2]).astype(BF16)
    normed_grad = jnp.zeros((rows, D), F32)
    for third in range(3):
        part = packed[:, third * D : (third + 1) * D].astype(BF16)
        normed_grad = normed_grad + dot_nt(part, full[:, third * D : (third + 1) * D])
        weight_grad = dot_tn(normed, part).astype(BF16)
        for j in range(PAIRS):
            block = third * PAIRS + j
            shared[meta[24 + block // 4], :, block % 4 * LANES : (block % 4 + 1) * LANES] = weight_grad[
                :, j * LANES : (j + 1) * LANES
            ]
    pulled = normed_grad * norms[0:1]
    through = pulled - jnp.mean(pulled, axis=1, keepdims=True)
    through = scale * (through - unit * jnp.mean(pulled * unit, axis=1, keepdims=True))
    input_grad[...] = through + middle_grad[...]
    for j in range(PAIRS):
        block = 3 * PAIRS + j
        shared[meta[24 + block // 4], :, block % 4 * LANES : (block % 4 + 1) * LANES] = output_grad[
            :, j * LANES : (j + 1) * LANES
        ]
    lines_norm = jnp.concatenate(
        [
            jnp.zeros((NORM_AT, D), F32),
            jnp.sum(normed_grad * unit, axis=0, keepdims=True),
            jnp.sum(normed_grad, axis=0, keepdims=True),
            norm_two[0:2, :],
            jnp.zeros((LANES - NORM_AT - 4, D), F32),
        ],
        axis=0,
    )
    small = routers[...] + jnp.transpose(lines_norm)
    shared[meta[27], :, 0:LANES] = small.astype(BF16)
    shared[meta[27], :, LANES:] = jnp.zeros((D, 3 * LANES), BF16)


def attention_back_call(meta, image, qkv, sent, lse_col, dots_col, own, full, middle_grad, output_grad, norm_two, routers):
    rows = middle_grad.shape[0]
    return pl.pallas_call(
        attention_back_kernel,
        in_specs=[smem()] + [vmem()] * 14,
        out_specs=(vmem(),) * 2,
        out_shape=(
            jax.ShapeDtypeStruct((rows, D), F32),
            jax.ShapeDtypeStruct((4, D, 4 * LANES), BF16),
        ),
        scratch_shapes=[
            pltpu.VMEM((4, 16, rows), F32),
            pltpu.VMEM((4, rows, D), BF16),
            pltpu.VMEM((rows, 3 * D), F32),
            pltpu.VMEM((rows, LANES), F32),
            pltpu.VMEM((rows, LANES), F32),
        ],
        name="attention_back",
    )(meta, image, qkv, *sent, lse_col, dots_col, own, full, middle_grad, output_grad, norm_two, routers)


def adamw(weight, moment, second, gradient, step_rate):
    moment = BETA_FIRST * moment + (1.0 - BETA_FIRST) * gradient
    second = BETA_SECOND * second + (1.0 - BETA_SECOND) * gradient * gradient
    first_hat = moment / (1.0 - BETA_FIRST**STEP)
    second_hat = second / (1.0 - BETA_SECOND**STEP)
    weight = weight - step_rate * (first_hat / (jnp.sqrt(second_hat) + ADAM_EPS) + DECAY * weight)
    return (weight, moment, second)


def adam_kernel(meta, ready, passed, ready_two, passed_two, w1, m1, v1, w2, m2, v2, *rest):
    outs = rest[-6:]
    mine = (pl.program_id(0) // (FFN // 2 // LANES)) == meta[1]
    down = jnp.where(mine, ready[...], passed[...]).astype(F32)
    up = jnp.where(mine, ready_two[...], passed_two[...]).astype(F32)
    for k, value in enumerate(adamw(w1[0], m1[0], v1[0], up, RATE_EXPAND)):
        outs[k][0] = value
    for k, value in enumerate(adamw(w2[0], m2[0], v2[0], jnp.transpose(down), RATE_REDUCE)):
        outs[3 + k][0] = value


def adam_call(expert, meta, ready, passed, states, previous):
    steps = FFN // LANES
    per = D // LANES

    def part(first):
        return pl.BlockSpec((D, LANES), lambda i, *_: (first + i // per % 2, i % per))

    up = pl.BlockSpec((1, D, LANES), lambda i, *_: (expert, 0, i))
    down = pl.BlockSpec((1, LANES, D), lambda i, *_: (expert, i, 0))
    specs = [part(0), part(0), part(2), part(2)] + [up] * 3 + [down] * 3
    args = [ready, passed, ready, passed, *states]
    aliases = {}
    if previous is not None:
        for k, value in enumerate(previous):
            aliases[1 + len(args)] = k
            args.append(value)
            specs.append(pl.BlockSpec(memory_space=pl.ANY))
    return pl.pallas_call(
        adam_kernel,
        grid_spec=pltpu.PrefetchScalarGridSpec(
            num_scalar_prefetch=1,
            grid=(steps,),
            in_specs=specs,
            out_specs=(up,) * 3 + (down,) * 3,
        ),
        out_shape=tuple(jax.ShapeDtypeStruct(s.shape, F32) for s in states),
        input_output_aliases=aliases,
        name="adam",
    )(meta, *args)


def swap_expert(value, d):
    return lax.ppermute(value, "expert", [(i, i ^ d) for i in range(4)])


def swap_tall(value, d):
    return lax.ppermute(value, "dp", [(2 * a + c, 2 * (a ^ d) + c) for a in range(4) for c in range(2)])


def swap_core(value):
    return lax.ppermute(value, "dp", [(i, i ^ 1) for i in range(8)])


def send_tall(value, hops):
    return lax.ppermute(value, "dp", [(2 * a + c, 2 * b + c) for a, b in hops for c in range(2)])


def reduce_line(mine, other, inner):
    half = mine + swap_core(other)
    pair = half + send_tall(half, ((0, 1), (3, 2)))
    whole = pair + send_tall(pair, ((1, 2), (2, 1)))
    returned = send_tall(whole, ((1, 0), (2, 3)))
    ready = jnp.where(inner, whole, returned)
    return ready, swap_core(ready)


def fast_body(
    patches, out_grad, image_of, task_of, routes,
    norm_weight, norm_moment, norm_second,
    attend_weight, attend_moment, attend_second,
    output_weight, output_moment, output_second,
    router_weight, router_moment, router_second,
    expand_weight, expand_moment, expand_second,
    reduce_weight, reduce_moment, reduce_second,
):
    member = lax.axis_index("expert")
    place = lax.axis_index("dp")
    tall, core = place // 2, place % 2
    rows = patches.shape[1]
    count = expand_weight.shape[0]
    shard_rows = attend_weight.shape[0]

    lists = jnp.concatenate([routes[0].T, task_of], axis=0).astype(BF16)
    lists = jnp.stack([lists[:, :D], jnp.pad(lists[:, D:], ((0, 0), (0, 2 * D - rows)))], axis=1)
    lists = jnp.pad(lists.reshape(2 * (TOP + TASKS - 1), D), ((0, INFO - 2 * (TOP + TASKS - 1)), (0, 0)))
    own = jnp.concatenate([patches[0], lists], axis=0)
    pieces = [own] + [swap_expert(own, d) for d in (1, 2, 3)]
    shard = jnp.concatenate(
        [
            attend_weight.astype(BF16),
            output_weight.astype(BF16),
            router_weight.reshape(TASKS * EXPERTS, shard_rows).T.astype(BF16),
            norm_weight.T.astype(BF16),
            jnp.zeros((shard_rows, LANES - NORM_AT - 4), BF16),
        ],
        axis=1,
    )
    shards = [shard] + [swap_tall(shard, d) for d in (1, 2, 3)]
    shards = shards + [swap_core(s) for s in shards]
    grad = out_grad[0]
    grads = [grad] + [swap_expert(grad, d) for d in (1, 2, 3)]

    image = image_of.reshape(4, rows)
    order = [member ^ d for d in range(4)]
    opens, closes = image[:, 0], image[:, rows - 1]
    first, final = opens[member], closes[member]
    needed = [((opens[o] <= final) & (closes[o] >= first)).astype(jnp.int32) for o in order]
    spots = [shard_rows * (2 * (tall ^ d) + core) for d in range(4)]
    spots = spots + [shard_rows * (2 * (tall ^ d) + 1 - core) for d in range(4)]
    zero = jnp.int32(0)
    meta = jnp.stack(
        [member * count, core, zero, zero] + order + needed + [zero] * 4 + spots + order
    ).astype(jnp.int32)

    spot_row, spot_col, plan = route_call(meta, pieces, count)
    qkv, full, att, lse_col, lse_row, middle, mixed = front_call(meta, image, pieces, shards)
    mixes = [mixed] + [swap_expert(mixed, d) for d in (1, 2, 3)]
    mine, other, back, mix, routers = expert_call(
        plan, meta, mixes, grads, spot_row, spot_col, full, expand_weight, reduce_weight
    )
    inner = (tall == 1) | (tall == 2)
    returned = [swap_expert(back[d], d) for d in (1, 2, 3)]
    middle_grad, sent, dots_col, output_grad, norm_two = turn_call(
        back, returned, middle, grad, full, att, lse_row
    )
    sents = [sent] + [swap_expert(sent, d) for d in (1, 2, 3)]
    input_grad, shared = attention_back_call(
        meta, image, qkv, sents, lse_col, dots_col, own, full, middle_grad, output_grad, norm_two, routers
    )
    states = (expand_weight, expand_moment, expand_second, reduce_weight, reduce_moment, reduce_second)
    news = None
    for e in range(count):
        ready, passed = reduce_line(mine[e], other[e], inner)
        news = adam_call(e, meta, ready, passed, states, news)
    parts = [swap_expert(mix[d], d) for d in (1, 2, 3)]
    block_out = middle + mix[0].astype(F32)
    for part in parts:
        block_out = block_out + part.astype(F32)
    block_out = block_out.astype(BF16)[None]

    quarter = shared[0].astype(F32)
    for d in (1, 2, 3):
        quarter = quarter + swap_expert(shared[d], d).astype(F32)
    quarter = quarter.astype(BF16).reshape(4, 2, shard_rows, 4 * LANES)
    kept = lax.dynamic_index_in_dim(quarter, core, 1, False)
    gone = lax.dynamic_index_in_dim(quarter, 1 - core, 1, False)
    kept = kept + swap_core(gone)
    piece = lax.dynamic_index_in_dim(kept, tall, 0, False).astype(F32)
    for d in (1, 2, 3):
        piece = piece + swap_tall(lax.dynamic_index_in_dim(kept, tall ^ d, 0, False), d).astype(F32)
    piece = piece.astype(BF16)
    quarters = jnp.stack([piece] + [swap_expert(piece, d) for d in (1, 2, 3)])
    quarters = jnp.concatenate([quarters[o] for o in order], axis=1).astype(F32)
    attend_sum = quarters[:, : 3 * D]
    output_sum = quarters[:, 3 * D : 4 * D]
    router_sum = quarters[:, 4 * D : 4 * D + NORM_AT].T.reshape(router_weight.shape)
    norm_sum = quarters[:, 4 * D + NORM_AT : 4 * D + NORM_AT + 4].T
    norm_new = adamw(norm_weight, norm_moment, norm_second, norm_sum, RATE_NORM)
    attend_new = adamw(attend_weight, attend_moment, attend_second, attend_sum, RATE_ATTEND)
    output_new = adamw(output_weight, output_moment, output_second, output_sum, RATE_OUTPUT)
    router_new = adamw(router_weight, router_moment, router_second, router_sum, RATE_ROUTER)
    return (
        block_out, input_grad[None],
        *norm_new, *attend_new, *output_new, *router_new, *news,
    )


def gelu_exact(values):
    return 0.5 * values * (1.0 + lax.erf(values * 0.7071067811865476))


def norm_rows(values, gain_row, offset):
    average = jnp.mean(values, axis=-1, keepdims=True)
    centred = values - average
    spread = jnp.mean(centred * centred, axis=-1, keepdims=True)
    return centred * lax.rsqrt(spread + NORM_EPS) * gain_row + offset


def body(
    patches,
    out_grad,
    image_of,
    task_of,
    routes,
    norm_weight,
    norm_moment,
    norm_second,
    attend_weight,
    attend_moment,
    attend_second,
    output_weight,
    output_moment,
    output_second,
    router_weight,
    router_moment,
    router_second,
    expand_weight,
    expand_moment,
    expand_second,
    reduce_weight,
    reduce_moment,
    reduce_second,
):
    precise = lax.Precision.HIGHEST
    member = lax.axis_index("expert")
    tokens = patches.shape[1]
    group_rows = image_of.shape[1]
    key_rows = min(512, group_rows)
    score_scale = HEAD_DIM ** (-0.5)
    norm_full, attend_full, output_full, router_full = (
        lax.all_gather(norm_weight.astype(jnp.bfloat16), "dp", axis=1, tiled=True),
        lax.all_gather(attend_weight.astype(jnp.bfloat16), "dp", axis=0, tiled=True),
        lax.all_gather(output_weight.astype(jnp.bfloat16), "dp", axis=0, tiled=True),
        lax.all_gather(router_weight.astype(jnp.bfloat16), "dp", axis=2, tiled=True),
    )
    norm_values = norm_full.astype(jnp.float32)
    router_values = router_full.astype(jnp.float32)
    expand_low = expand_weight.astype(jnp.bfloat16)
    reduce_low = reduce_weight.astype(jnp.bfloat16)
    inputs = patches[0].astype(jnp.float32)
    image_row = image_of[0]
    my_image = lax.dynamic_slice_in_dim(image_row, member * tokens, tokens)
    task_row = task_of[0]
    route_rows = routes[0]
    first_image = my_image[0]
    last_image = my_image[tokens - 1]
    first_key = jnp.sum((image_row < first_image).astype(jnp.int32))
    last_key = jnp.sum((image_row <= last_image).astype(jnp.int32)) - 1
    first_block = first_key // key_rows
    end_block = last_key // key_rows + 1
    normed_one, first_back = jax.vjp(norm_rows, inputs, norm_values[0], norm_values[1])
    normed_low = normed_one.astype(jnp.bfloat16)
    packed = jnp.dot(normed_low, attend_full, preferred_element_type=jnp.float32).astype(
        jnp.bfloat16
    )
    queries = packed[:, :D].reshape(tokens, HEADS, HEAD_DIM)
    key_value = packed[:, D:]
    key_value_all = lax.all_gather(key_value, "expert", axis=0, tiled=True)
    keys_all = key_value_all[:, :D].reshape(group_rows, HEADS, HEAD_DIM)
    values_all = key_value_all[:, D:].reshape(group_rows, HEADS, HEAD_DIM)

    def scores_of(query_part, key_part, same_image):
        raw = (
            jnp.einsum("thd,khd->htk", query_part, key_part, preferred_element_type=jnp.float32)
            * score_scale
        )
        return jnp.where(same_image[None], raw, MASKED)

    def block_at(block_index):
        first_row = block_index * key_rows
        key_part = lax.dynamic_slice_in_dim(keys_all, first_row, key_rows, 0)
        value_part = lax.dynamic_slice_in_dim(values_all, first_row, key_rows, 0)
        same_image = (
            my_image[:, None]
            == lax.dynamic_slice_in_dim(image_row, first_row, key_rows, 0)[None, :]
        )
        return (key_part, value_part, same_image)

    def max_step(block_index, state_in):
        highest, totals = state_in
        key_part, value_part, same_image = block_at(block_index)
        scores = scores_of(queries, key_part, same_image)
        raised = jnp.maximum(highest, jnp.max(scores, axis=-1))
        shares = jnp.where(same_image[None], jnp.exp(scores - raised[..., None]), 0.0)
        return (raised, totals * jnp.exp(highest - raised) + jnp.sum(shares, axis=-1))

    start_max = jnp.full((HEADS, tokens), MASKED, jnp.float32)
    highest, totals = lax.fori_loop(
        first_block, end_block, max_step, (start_max, jnp.zeros((HEADS, tokens), jnp.float32))
    )
    log_total = highest + jnp.log(totals)

    def value_step(block_index, accum):
        key_part, value_part, same_image = block_at(block_index)
        scores = scores_of(queries, key_part, same_image)
        soft_part = jnp.where(same_image[None], jnp.exp(scores - log_total[..., None]), 0.0).astype(
            jnp.bfloat16
        )
        return accum + jnp.einsum(
            "htk,khd->thd", soft_part, value_part, preferred_element_type=jnp.float32
        )

    attended = lax.fori_loop(
        first_block, end_block, value_step, jnp.zeros((tokens, HEADS, HEAD_DIM), jnp.float32)
    )
    attended_low = attended.reshape(tokens, D).astype(jnp.bfloat16)
    branch = jnp.dot(attended_low, output_full, preferred_element_type=jnp.float32)
    middle = inputs + branch
    normed_two, second_back = jax.vjp(norm_rows, middle, norm_values[2], norm_values[3])
    mixed_low = normed_two.astype(jnp.bfloat16)
    task_hot = (task_row[:, None] == jnp.arange(TASKS, dtype=jnp.int32)[None, :]).astype(
        jnp.float32
    )
    route_hot = (
        route_rows[:, :, None] == jnp.arange(EXPERTS, dtype=jnp.int32)[None, None, :]
    ).astype(jnp.float32)

    def gating(hidden, router):
        logits = jnp.einsum("td,ced->tce", hidden, router, precision=precise)
        task_logits = jnp.einsum("tc,tce->te", task_hot, logits, precision=precise)
        chosen = jnp.einsum("te,tke->tk", task_logits, route_hot, precision=precise)
        peak = jnp.max(chosen, axis=-1, keepdims=True)
        raised = jnp.exp(chosen - peak)
        return raised / jnp.sum(raised, axis=-1, keepdims=True)

    gate_values, gate_back = jax.vjp(gating, mixed_low.astype(jnp.float32), router_values)
    pair_expert = route_rows.reshape(-1)
    pair_hot = (pair_expert[:, None] == jnp.arange(EXPERTS, dtype=jnp.int32)[None, :]).astype(
        jnp.int32
    )
    slot_index = jnp.sum((jnp.cumsum(pair_hot, axis=0) - pair_hot) * pair_hot, axis=1)
    flat_slot = pair_expert * CAP + slot_index

    def scatter_pairs(pair_values):
        return (
            jnp.zeros((EXPERTS * CAP, D), pair_values.dtype)
            .at[flat_slot]
            .set(pair_values)
            .reshape(EXPERTS, CAP, D)
        )

    def gather_pairs(buffer):
        return (
            buffer.reshape(EXPERTS * CAP, D)[flat_slot].astype(jnp.float32).reshape(tokens, TOP, D)
        )

    received = lax.all_to_all(
        scatter_pairs(jnp.repeat(mixed_low, TOP, axis=0)),
        "expert",
        split_axis=0,
        concat_axis=1,
        tiled=True,
    )
    hidden_pre = jnp.einsum(
        "ecd,edh->ech", received, expand_low, preferred_element_type=jnp.float32
    )
    active, gelu_back = jax.vjp(gelu_exact, hidden_pre)
    active_low = active.astype(jnp.bfloat16)
    expert_out = jnp.einsum(
        "ech,ehd->ecd", active_low, reduce_low, preferred_element_type=jnp.float32
    ).astype(jnp.bfloat16)
    returned = lax.all_to_all(expert_out, "expert", split_axis=1, concat_axis=0, tiled=True)
    pair_out = gather_pairs(returned)
    expert_mix = jnp.einsum("tk,tkd->td", gate_values, pair_out, precision=precise)
    block_out = (middle + expert_mix).astype(jnp.bfloat16)[None]
    upstream = out_grad[0].astype(jnp.float32)
    gate_grad = jnp.sum(upstream[:, None, :] * pair_out, axis=-1)
    pair_grad = (
        (gate_values[:, :, None] * upstream[:, None, :])
        .astype(jnp.bfloat16)
        .reshape(tokens * TOP, D)
    )
    grad_in = lax.all_to_all(
        scatter_pairs(pair_grad), "expert", split_axis=0, concat_axis=1, tiled=True
    )
    reduce_grad = jnp.einsum(
        "ech,ecd->ehd", active_low, grad_in, preferred_element_type=jnp.float32
    )
    active_grad = jnp.einsum(
        "ecd,ehd->ech", grad_in, reduce_low, preferred_element_type=jnp.float32
    )
    pre_grad = gelu_back(active_grad)[0].astype(jnp.bfloat16)
    expand_grad = jnp.einsum("ecd,ech->edh", received, pre_grad, preferred_element_type=jnp.float32)
    back_rows = jnp.einsum(
        "ech,edh->ecd", pre_grad, expand_low, preferred_element_type=jnp.float32
    ).astype(jnp.bfloat16)
    expand_sum, reduce_sum = (
        lax.psum(expand_grad.astype(jnp.bfloat16), "dp").astype(jnp.float32),
        lax.psum(reduce_grad.astype(jnp.bfloat16), "dp").astype(jnp.float32),
    )
    came_back = lax.all_to_all(back_rows, "expert", split_axis=1, concat_axis=0, tiled=True)
    routed_grad = jnp.sum(gather_pairs(came_back), axis=1)
    hidden_gate_grad, router_grad = gate_back(gate_grad)
    middle_part, gain_two, offset_two = second_back(routed_grad + hidden_gate_grad)
    middle_grad = middle_part + upstream
    branch_grad = middle_grad.astype(jnp.bfloat16)
    output_grad = jnp.einsum(
        "td,te->de", attended_low, branch_grad, preferred_element_type=jnp.float32
    )
    attended_grad = (
        jnp.einsum("te,de->td", branch_grad, output_full, preferred_element_type=jnp.float32)
        .astype(jnp.bfloat16)
        .reshape(tokens, HEADS, HEAD_DIM)
    )
    row_dots = jnp.einsum(
        "thd,thd->ht", attended_grad.astype(jnp.float32), attended, precision=precise
    )

    def score_grad(query_part, key_part, value_part, grad_part, same_image, log_part, dots_part):
        scores = scores_of(query_part, key_part, same_image)
        soft_part = jnp.where(same_image[None], jnp.exp(scores - log_part[..., None]), 0.0)
        soft_grad = jnp.einsum(
            "thd,khd->htk", grad_part, value_part, preferred_element_type=jnp.float32
        )
        return (soft_part, (soft_part * (soft_grad - dots_part[..., None])).astype(jnp.bfloat16))

    def pair_step(block_index, state_in):
        query_acc, terms_acc = state_in
        key_part, value_part, same_image = block_at(block_index)
        soft_part, dscore = score_grad(
            queries, key_part, value_part, attended_grad, same_image, log_total, row_dots
        )
        query_acc = query_acc + jnp.einsum(
            "htk,khd->thd", dscore, key_part, preferred_element_type=jnp.float32
        )
        key_term = (
            jnp.einsum("htk,thd->khd", dscore, queries, preferred_element_type=jnp.float32)
            * score_scale
        )
        value_term = jnp.einsum(
            "htk,thd->khd",
            soft_part.astype(jnp.bfloat16),
            attended_grad,
            preferred_element_type=jnp.float32,
        )
        terms = jnp.concatenate(
            [key_term.reshape(key_rows, D), value_term.reshape(key_rows, D)], axis=1
        )
        terms_acc = lax.dynamic_update_slice_in_dim(terms_acc, terms, block_index * key_rows, 0)
        return (query_acc, terms_acc)

    query_acc, key_value_terms = lax.fori_loop(
        first_block,
        end_block,
        pair_step,
        (
            jnp.zeros((tokens, HEADS, HEAD_DIM), jnp.float32),
            jnp.zeros((group_rows, 2 * D), jnp.float32),
        ),
    )
    key_value_grad = lax.psum_scatter(
        key_value_terms.astype(jnp.bfloat16), "expert", scatter_dimension=0, tiled=True
    ).astype(jnp.float32)
    query_grad = (query_acc * score_scale).reshape(tokens, D)
    packed_grad = jnp.concatenate([query_grad, key_value_grad], axis=1).astype(jnp.bfloat16)
    attend_grad = jnp.einsum(
        "td,te->de", normed_low, packed_grad, preferred_element_type=jnp.float32
    )
    normed_grad = jnp.einsum(
        "te,de->td", packed_grad, attend_full, preferred_element_type=jnp.float32
    )
    input_part, gain_one, offset_one = first_back(normed_grad)
    input_grad = (middle_grad + input_part)[None]
    norm_grad = jnp.stack([gain_one, offset_one, gain_two, offset_two])
    shared = (norm_grad, attend_grad, output_grad, router_grad)
    summed = (
        lax.psum(shared[0].astype(jnp.bfloat16), "expert").astype(jnp.float32),
        lax.psum(shared[1].astype(jnp.bfloat16), "expert").astype(jnp.float32),
        lax.psum(shared[2].astype(jnp.bfloat16), "expert").astype(jnp.float32),
        lax.psum(shared[3].astype(jnp.bfloat16), "expert").astype(jnp.float32),
    )
    norm_sum, attend_sum, output_sum, router_sum = (
        lax.psum_scatter(
            summed[0].astype(jnp.bfloat16), "dp", scatter_dimension=1, tiled=True
        ).astype(jnp.float32),
        lax.psum_scatter(
            summed[1].astype(jnp.bfloat16), "dp", scatter_dimension=0, tiled=True
        ).astype(jnp.float32),
        lax.psum_scatter(
            summed[2].astype(jnp.bfloat16), "dp", scatter_dimension=0, tiled=True
        ).astype(jnp.float32),
        lax.psum_scatter(
            summed[3].astype(jnp.bfloat16), "dp", scatter_dimension=2, tiled=True
        ).astype(jnp.float32),
    )
    norm_new = adamw(norm_weight, norm_moment, norm_second, norm_sum, RATE_NORM)
    attend_new = adamw(attend_weight, attend_moment, attend_second, attend_sum, RATE_ATTEND)
    output_new = adamw(output_weight, output_moment, output_second, output_sum, RATE_OUTPUT)
    router_new = adamw(router_weight, router_moment, router_second, router_sum, RATE_ROUTER)
    expand_new = adamw(expand_weight, expand_moment, expand_second, expand_sum, RATE_EXPAND)
    reduce_new = adamw(reduce_weight, reduce_moment, reduce_second, reduce_sum, RATE_REDUCE)
    return (
        block_out,
        input_grad,
        norm_new[0],
        norm_new[1],
        norm_new[2],
        attend_new[0],
        attend_new[1],
        attend_new[2],
        output_new[0],
        output_new[1],
        output_new[2],
        router_new[0],
        router_new[1],
        router_new[2],
        expand_new[0],
        expand_new[1],
        expand_new[2],
        reduce_new[0],
        reduce_new[1],
        reduce_new[2],
    )


def solution(mesh):
    placed = (
        P("dp", "expert", None),
        P("dp", "expert", None),
        P("dp", None),
        P("dp", "expert"),
        P("dp", "expert", None),
        P(None, "dp"),
        P(None, "dp"),
        P(None, "dp"),
        P("dp", None),
        P("dp", None),
        P("dp", None),
        P("dp", None),
        P("dp", None),
        P("dp", None),
        P(None, None, "dp"),
        P(None, None, "dp"),
        P(None, None, "dp"),
        P("expert", None, None),
        P("expert", None, None),
        P("expert", None, None),
        P("expert", None, None),
        P("expert", None, None),
        P("expert", None, None),
    )
    fits = mesh.shape["dp"] == 8 and mesh.shape["expert"] == 4
    return jax.shard_map(
        fast_body if fits else body,
        mesh=mesh,
        in_specs=placed,
        out_specs=(
            P("dp", "expert", None),
            P("dp", "expert", None),
            P(None, "dp"),
            P(None, "dp"),
            P(None, "dp"),
            P("dp", None),
            P("dp", None),
            P("dp", None),
            P("dp", None),
            P("dp", None),
            P("dp", None),
            P(None, None, "dp"),
            P(None, None, "dp"),
            P(None, None, "dp"),
            P("expert", None, None),
            P("expert", None, None),
            P("expert", None, None),
            P("expert", None, None),
            P("expert", None, None),
            P("expert", None, None),
        ),
        check_vma=False,
    )
```

```python
import functools

import jax
import jax.numpy as jnp
import numpy as np
from jax import lax
from jax.experimental import pallas as pl
from jax.experimental.pallas import tpu as pltpu
from jax.sharding import PartitionSpec as P

D = 384
HEADS = 6
HEAD_DIM = 64
FFN = 1536
EXPERTS = 16
TASKS = 2
TOP = 4
STEP = 10
CAP = 256
PAIRS = HEADS // 2
LANES = 128
WCOLS = 4 * D + LANES
INFO = 16
NORM_AT = 2 * EXPERTS
EXTRA = 64

NORM_EPS = 1e-06
ADAM_EPS = 1e-08
BETA_FIRST = 0.9
BETA_SECOND = 0.999
DECAY = 0.05
RATE_NORM = 0.5
RATE_ATTEND = 0.2
RATE_OUTPUT = 0.7
RATE_ROUTER = 0.06
RATE_EXPAND = 0.13
RATE_REDUCE = 0.25
MASKED = -1e30
F32 = jnp.float32
BF16 = jnp.bfloat16
LIGHT = pl.CostEstimate(flops=1, transcendentals=0, bytes_accessed=1)


def dot_nn(a, b):
    return lax.dot_general(a, b, (((1,), (0,)), ((), ())), preferred_element_type=F32)


def dot_nt(a, b):
    return lax.dot_general(a, b, (((1,), (1,)), ((), ())), preferred_element_type=F32)


def dot_tn(a, b):
    return lax.dot_general(a, b, (((0,), (0,)), ((), ())), preferred_element_type=F32)


def unit_rows(values):
    average = jnp.mean(values, axis=-1, keepdims=True)
    centred = values - average
    spread = jnp.mean(centred * centred, axis=-1, keepdims=True)
    scale = lax.rsqrt(spread + NORM_EPS)
    return centred * scale, scale


def eye(n):
    rows = lax.broadcasted_iota(jnp.int32, (n, n), 0)
    cols = lax.broadcasted_iota(jnp.int32, (n, n), 1)
    return (rows == cols).astype(F32).astype(BF16)


def norm_rows_of(full_ref):
    return dot_nt(eye(LANES), full_ref[:, 4 * D :])[NORM_AT : NORM_AT + 8]


def vmem():
    return pl.BlockSpec(memory_space=pltpu.VMEM)


def smem():
    return pl.BlockSpec(memory_space=pltpu.SMEM)


def room(mebibytes):
    return pltpu.CompilerParams(vmem_limit_bytes=mebibytes * 2**20)


def whole(shape):
    return pl.BlockSpec(shape, lambda *_: (0,) * len(shape), pipeline_mode=pl.Buffered(1))


def once(kernel, scalars, arrays, outs, name, mebibytes, scratch=()):
    return pl.pallas_call(
        kernel,
        grid=(1,),
        in_specs=[smem()] * len(scalars) + [whole(a.shape) for a in arrays],
        out_specs=tuple(whole(o[0]) for o in outs),
        out_shape=tuple(jax.ShapeDtypeStruct(*o) for o in outs),
        scratch_shapes=[pltpu.VMEM(*held) for held in scratch],
        compiler_params=room(mebibytes),
        cost_estimate=LIGHT,
        name=name,
    )(*scalars, *arrays)


def place_table(count, shard_rows):
    table = np.zeros((32, 48), np.int32)
    for place in range(8):
        for member in range(4):
            tall, core = place // 2, place % 2
            row = table[place * 4 + member]
            row[0:3] = member * count, core, tall in (1, 2)
            for d in range(4):
                row[4 + d] = member ^ d
                row[16 + d] = shard_rows * (2 * (tall ^ d) + core)
                row[20 + d] = shard_rows * (2 * (tall ^ d) + 1 - core)
            for owner in range(8):
                row[28 + owner] = shard_rows * ((owner % 2 ^ core) * 4 + (owner // 2 ^ tall))
    return table


def wanted(meta, ends, d):
    rows = ends.shape[1] // 4
    here, there = meta[4] * rows, meta[4 + d] * rows
    return (ends[0, there] <= ends[0, here + rows - 1]) & (ends[0, there + rows - 1] >= ends[0, here])


def images_of(meta, image, d):
    rows = image.shape[1] // 4
    return image[0:1, pl.ds(pl.multiple_of(meta[4 + d] * rows, LANES), rows)].astype(F32)


def pack_kernel(
    patches, routes, tasks, attend, output, router, norm, own, shard, wide, square,
):
    rows = patches.shape[1]
    shard_rows = attend.shape[0]
    shard[:, 0 : 3 * D] = attend[...].astype(BF16)
    shard[:, 3 * D : 4 * D] = output[...].astype(BF16)
    square[...] = jnp.zeros_like(square)
    for t in range(TASKS):
        square[t * EXPERTS : (t + 1) * EXPERTS, 0:shard_rows] = router[t]
    square[NORM_AT : NORM_AT + 4, 0:shard_rows] = norm[...]
    shard[:, 4 * D :] = jnp.transpose(square[...])[:shard_rows].astype(BF16)
    own[0:rows, :] = patches[0]
    wide[...] = jnp.zeros_like(wide)
    wide[:, 0:TOP] = routes[0].astype(F32)
    lists = jnp.concatenate([jnp.transpose(wide[...])[:TOP], tasks[...].astype(F32)], axis=0)
    rest = jnp.concatenate([lists[:, D:], jnp.zeros((TOP + 1, 2 * D - rows), F32)], axis=1)
    lines = []
    for k in range(TOP + 1):
        lines = lines + [lists[k : k + 1, :D], rest[k : k + 1]]
    lines = lines + [jnp.zeros((INFO - 2 * (TOP + 1), D), F32)]
    own[rows : rows + INFO, :] = jnp.concatenate(lines, axis=0).astype(BF16)


def pack_call(patches, routes, tasks, attend, output, router, norm):
    rows = patches.shape[1]
    return once(
        pack_kernel, (), (patches, routes, tasks, attend, output, router, norm),
        (((rows + INFO, D), BF16), ((attend.shape[0], WCOLS), BF16)),
        "pack", 12, (((rows, LANES), F32), ((LANES, LANES), F32)),
    )


def route_kernel(meta, i0, i1, i2, i3, row_out, pick_out, col_out, plan_out):
    base = meta[0]
    rows = i0.shape[1] + LANES
    later = lax.broadcasted_iota(jnp.int32, (rows, rows), 0)
    token = lax.broadcasted_iota(jnp.int32, (rows, rows), 1)
    before = (later < token).astype(F32).astype(BF16)
    one = (later == token).astype(F32).astype(BF16)
    local = row_out.shape[0]
    which = lax.broadcasted_iota(jnp.int32, (local, rows), 0)
    slot_names = (which + base).astype(F32)
    every = lax.broadcasted_iota(jnp.int32, (EXPERTS, rows), 0).astype(F32)
    experts = plan_out.shape[0] // 8
    starts = [jnp.int32(0)] * experts
    for d, ref in enumerate((i0, i1, i2, i3)):
        info = ref[...].astype(F32)

        def line(k):
            return jnp.concatenate([info[2 * k : 2 * k + 1], info[2 * k + 1 : 2 * k + 2, :LANES]], axis=1)

        mine = jnp.zeros((local, rows), jnp.bool_)
        chosen = jnp.zeros((EXPERTS, rows), jnp.bool_)
        for k in range(TOP):
            named = line(k)
            mine = mine | (slot_names == named)
            chosen = chosen | (every == named)
        mine = jnp.where(mine & (which < experts), 1.0, 0.0)
        chosen = jnp.where(chosen, 1.0, 0.0)
        rank = dot_nn(mine.astype(BF16), before)
        spot = jnp.where(mine > 0.5, rank, -1.0)
        at = slice(d * rows, (d + 1) * rows)
        row_out[:, at] = spot
        tasks = jnp.broadcast_to(line(TOP), (8, rows))
        pick_out[0:EXPERTS, at] = chosen
        pick_out[EXPERTS:, at] = tasks
        table = jnp.concatenate(
            [spot, jnp.zeros((16 - local, rows), F32), chosen, tasks, jnp.zeros((LANES - 40, rows), F32)],
            axis=0,
        )
        col_out[d * rows : (d + 1) * rows, :] = dot_nt(one, table.astype(BF16))
        for e in range(experts):
            held = jnp.sum(mine[e : e + 1, :]).astype(jnp.int32)
            plan_out[e * 8 + d] = starts[e]
            starts[e] = starts[e] + (held + 15) // 16 * 16
    for e in range(experts):
        plan_out[e * 8 + 4] = starts[e]
        plan_out[e * 8 + 5] = (starts[e] + CAP - 1) // CAP


def route_call(meta, pieces, experts):
    rows = pieces[0].shape[0] - INFO
    return pl.pallas_call(
        route_kernel,
        grid=(1,),
        in_specs=[smem()] + [pl.BlockSpec((INFO, D), lambda i: (rows // INFO, 0))] * 4,
        out_specs=(
            pl.BlockSpec((8, 4 * rows), lambda i: (0, 0)),
            pl.BlockSpec((EXPERTS + 8, 4 * rows), lambda i: (0, 0)),
            pl.BlockSpec((4 * rows, LANES), lambda i: (0, 0)),
            smem(),
        ),
        out_shape=(
            jax.ShapeDtypeStruct((8, 4 * rows), F32),
            jax.ShapeDtypeStruct((EXPERTS + 8, 4 * rows), F32),
            jax.ShapeDtypeStruct((4 * rows, LANES), F32),
            jax.ShapeDtypeStruct((experts * 8,), jnp.int32),
        ),
        compiler_params=room(24),
        cost_estimate=LIGHT,
        name="routing",
    )(meta, *pieces)


def front_kernel(
    meta, ends, image, p0, p1, p2, p3, w0, w1, w2, w3, w4, w5, w6, w7,
    qkv, full, att, lse_col, lse_row, middle, mixed,
    everything, scores, top, total, out_acc,
):
    rows = att.shape[0]
    for j, ref in enumerate((w0, w1, w2, w3, w4, w5, w6, w7)):
        full[pl.ds(pl.multiple_of(meta[16 + j], 16), ref.shape[0]), :] = ref[...]
    for d, ref in enumerate((p0, p1, p2, p3)):
        everything[d * rows : (d + 1) * rows, :] = ref[:rows, :]
    norms = norm_rows_of(full)
    tile = 256

    def project(i, carry):
        at = pl.ds(pl.multiple_of(i * tile, tile), tile)
        unit, _ = unit_rows(everything[at, :].astype(F32))
        normed = (unit * norms[0:1] + norms[1:2]).astype(BF16)
        for third in range(3):
            made = dot_nn(normed, full[:, third * D : (third + 1) * D]).astype(BF16)
            if third == 0:
                made = made * jnp.asarray(HEAD_DIM ** (-0.5), BF16)
            for part in range(PAIRS):
                qkv[third * PAIRS + part, at, :] = made[:, part * LANES : (part + 1) * LANES]
        return carry

    lax.fori_loop(0, 4 * rows // tile, project, 0)
    own_row = images_of(meta, image, 0)
    own_col = jnp.transpose(jnp.broadcast_to(own_row, (LANES, rows)))[:, :1]
    lane = lax.broadcasted_iota(jnp.int32, (rows, LANES), 1)
    lse_col[...] = jnp.zeros_like(lse_col)

    def pair_of_heads(pair, carry):
        done = []
        for half in range(2):
            held = (lane < HEAD_DIM) if half == 0 else (lane >= HEAD_DIM)
            query = jnp.where(held, qkv[pair, 0:rows, :], jnp.zeros((), BF16))
            top[...] = jnp.full_like(top, MASKED)

            def score(d, c):
                @pl.when(wanted(meta, ends, d))
                def _():
                    key = qkv[PAIRS + pair, pl.ds(pl.multiple_of(d * rows, rows), rows), :]
                    same = own_col == images_of(meta, image, d)
                    raw = jnp.where(same, dot_nt(query, key), MASKED)
                    scores[d] = raw
                    top[...] = jnp.maximum(top[...], jnp.max(raw, axis=1, keepdims=True))

                return c

            lax.fori_loop(0, 4, score, 0)
            total[...] = jnp.zeros_like(total)
            out_acc[...] = jnp.zeros_like(out_acc)
            peak = top[:, :1]

            def weigh(d, c):
                @pl.when(wanted(meta, ends, d))
                def _():
                    value = qkv[2 * PAIRS + pair, pl.ds(pl.multiple_of(d * rows, rows), rows), :]
                    shares = jnp.exp(scores[d] - peak)
                    total[...] += jnp.sum(shares, axis=1, keepdims=True)
                    out_acc[...] += dot_nn(shares.astype(BF16), value)

                return c

            lax.fori_loop(0, 4, weigh, 0)
            done.append(out_acc[...] / total[:, :1])
            lse_col[...] = jnp.where(lane == 2 * pair + half, peak + jnp.log(total[:, :1]), lse_col[...])
        att[:, pl.ds(pl.multiple_of(pair * LANES, LANES), LANES)] = jnp.where(lane < HEAD_DIM, done[0], done[1])
        return carry

    lax.fori_loop(0, PAIRS, pair_of_heads, 0)
    lse_row[...] = jnp.transpose(lse_col[...])[:8]
    branch = dot_nn(att[...].astype(BF16), full[:, 3 * D : 4 * D])
    centre = everything[0:rows, :].astype(F32) + branch
    middle[...] = centre
    unit, _ = unit_rows(centre)
    mixed[...] = (unit * norms[2:3] + norms[3:4]).astype(BF16)


def front_call(meta, image, pieces, shards):
    rows = pieces[0].shape[0] - INFO
    return once(
        front_kernel, (meta, image), (image, *pieces, *shards),
        (
            ((3 * PAIRS, 4 * rows, LANES), BF16), ((D, WCOLS), BF16), ((rows, D), F32), ((rows, LANES), F32),
            ((8, rows), F32), ((rows, D), F32), ((rows, D), BF16),
        ),
        "front", 40,
        (((4 * rows, D), BF16), ((4, rows, rows), F32), ((rows, 1), F32), ((rows, 1), F32), ((rows, LANES), F32)),
    )


def gate_rows(mix, router_rows, choice):
    both = dot_nt(router_rows, mix)
    open_ = choice[:EXPERTS] > 0.5
    logits = jnp.where(choice[EXPERTS : EXPERTS + 1] < 0.5, both[:EXPERTS], both[EXPERTS : 2 * EXPERTS])
    logits = jnp.where(open_, logits, MASKED)
    raised = jnp.where(open_, jnp.exp(logits - jnp.max(logits, axis=0, keepdims=True)), 0.0)
    return raised / jnp.sum(raised, axis=0, keepdims=True)


def expert_kernel(
    first, plan, meta, m0, m1, m2, m3, g0, g1, g2, g3, spot_row, choice, given, up, down,
    mine0, other0, mine1, other1, results, gates_out,
    gates, hidden, upstream, gate_slots, sum_up, sum_down,
):
    step = pl.program_id(0)
    core = meta[1]
    low_up, low_down = up.at[0], down.at[0]
    local = first + step
    expert = meta[0] + local
    rows = m0.shape[0]
    mixes = (m0, m1, m2, m3)
    grads = (g0, g1, g2, g3)

    @pl.when(step == 0)
    def _():
        if first == 0:
            router_rows = jnp.transpose(given[:, 4 * D :])
            for d in range(4):
                at = slice(d * rows, (d + 1) * rows)
                gates[:, at] = gate_rows(mixes[d][...], router_rows, choice[:, at])
            gates_out[...] = gates[...]
        else:
            gates[...] = given[...]
            gates_out[...] = jnp.zeros_like(gates_out)

    slot_at = lax.broadcasted_iota(jnp.int32, (CAP, rows), 0).astype(F32)
    lane = lax.broadcasted_iota(jnp.int32, (CAP, LANES), 1)
    for d in range(4):
        at = slice(d * rows, (d + 1) * rows)
        hit = slot_at == spot_row[pl.ds(local, 1), at]
        pick = jnp.where(hit, 1.0, 0.0).astype(BF16)
        gate = jnp.sum(jnp.where(hit, gates[pl.ds(expert, 1), at], 0.0), axis=1, keepdims=True)
        start = pl.multiple_of(plan[local * 8 + d], 16)
        hidden[pl.ds(start, CAP), :] = dot_nn(pick, mixes[d][...]).astype(BF16)
        upstream[pl.ds(start, CAP), :] = (gate * dot_nn(pick, grads[d][...])).astype(BF16)
        gate_slots[pl.ds(start, CAP), :] = jnp.broadcast_to(gate, (CAP, LANES))
    ending = pl.multiple_of(plan[local * 8 + 4], 16)
    hidden[pl.ds(ending, CAP), :] = jnp.zeros((CAP, D), BF16)
    upstream[pl.ds(ending, CAP), :] = jnp.zeros((CAP, D), BF16)
    gate_slots[pl.ds(ending, CAP), :] = jnp.zeros((CAP, LANES), F32)
    sum_up[...] = jnp.zeros_like(sum_up)
    sum_down[...] = jnp.zeros_like(sum_down)
    wide = 512

    def tile(i, carry):
        at = pl.ds(pl.multiple_of(i * CAP, CAP), CAP)
        x = hidden[at, :]
        g = upstream[at, :]
        x_t = jnp.transpose(x)
        g_t = jnp.transpose(g)
        made = jnp.zeros((CAP, D), F32)
        back = jnp.zeros((CAP, D), F32)
        for j in range(FFN // wide):
            cols = slice(j * wide, (j + 1) * wide)
            pre = dot_nn(x, low_up[:, cols])
            pull = dot_nt(g, low_down[cols, :])
            share = 0.5 + 0.5 * lax.erf(pre * 0.7071067811865476)
            active = (pre * share).astype(BF16)
            slope = share + pre * (0.3989422804014327 * jnp.exp(-0.5 * pre * pre))
            pre_grad = (slope * pull).astype(BF16)
            made = made + dot_nn(active, low_down[cols, :])
            back = back + dot_nt(pre_grad, low_up[:, cols])
            sum_up[:, cols] += dot_nn(x_t, pre_grad)
            sum_down[:, cols] += dot_nn(g_t, active)
        results[0, at, 0:D] = (gate_slots[at, 0:1] * made).astype(BF16)
        results[0, at, D : 2 * D] = back.astype(BF16)
        term = jnp.sum(g.astype(F32) * made, axis=1, keepdims=True)
        high = term.astype(BF16).astype(F32)
        ends = jnp.where(lane == expert, high, 0.0) + jnp.where(lane == 32 + expert, term - high, 0.0)
        results[0, at, 2 * D :] = ends.astype(BF16)
        return carry

    count = plan[local * 8 + 5]
    lax.fori_loop(0, count, tile, 0)
    results[0, pl.ds(pl.multiple_of(count * CAP, CAP), CAP), :] = jnp.zeros((CAP, 2 * D + LANES), BF16)
    half = FFN // 2
    quarter = D // 2

    def write(pair):
        for ref, side in zip(pair, (core, 1 - core)):
            for b in range(2):
                cols = pl.ds(pl.multiple_of(side * half + b * D, LANES), D)
                ref[b * D : (b + 1) * D, :] = sum_down[:, cols].astype(BF16)
            held = sum_up[pl.ds(pl.multiple_of(side * quarter, 16), quarter), :].astype(BF16)
            for b in range(4):
                ref[half + b * quarter : half + (b + 1) * quarter, :] = held[:, b * D : (b + 1) * D]

    @pl.when(step == 0)
    def _():
        write((mine0, other0))

    @pl.when(step == 1)
    def _():
        write((mine1, other1))


def expert_call(first, plan, meta, mixes, grads, spot_row, choice, given, up, down):
    rows = mixes[0].shape[0]
    slots = 4 * CAP + CAP
    return pl.pallas_call(
        functools.partial(expert_kernel, first),
        grid_spec=pltpu.PrefetchScalarGridSpec(
            num_scalar_prefetch=2,
            grid=(2,),
            in_specs=[whole((rows, D))] * 8
            + [
                whole((8, 4 * rows)),
                whole((EXPERTS + 8, 4 * rows)),
                whole(given.shape),
                pl.BlockSpec((1, D, FFN), lambda e, *_: (first + e, 0, 0)),
                pl.BlockSpec((1, FFN, D), lambda e, *_: (first + e, 0, 0)),
            ],
            out_specs=(whole((4 * D, D)),) * 4
            + (
                pl.BlockSpec((1, slots, 2 * D + LANES), lambda e, *_: (e, 0, 0)),
                whole((EXPERTS, 4 * rows)),
            ),
            scratch_shapes=[
                pltpu.VMEM((EXPERTS, 4 * rows), F32),
                pltpu.VMEM((slots, D), BF16),
                pltpu.VMEM((slots, D), BF16),
                pltpu.VMEM((slots, LANES), F32),
                pltpu.VMEM((D, FFN), F32),
                pltpu.VMEM((D, FFN), F32),
            ],
        ),
        out_shape=(jax.ShapeDtypeStruct((4 * D, D), BF16),) * 4
        + (
            jax.ShapeDtypeStruct((2, slots, 2 * D + LANES), BF16),
            jax.ShapeDtypeStruct((EXPERTS, 4 * rows), F32),
        ),
        compiler_params=room(48),
        cost_estimate=LIGHT,
        name="experts",
    )(plan, meta, *mixes, *grads, spot_row, choice, given, up, down)


def combine_kernel(
    plan, m0, m1, m2, m3, spot_col, gates, full, res0, res1,
    b0, b1, b2, b3, x0, x1, x2, x3, router_out,
    stack,
):
    rows = m0.shape[0]
    lane = lax.broadcasted_iota(jnp.int32, (rows, LANES), 1)
    slot_along = lax.broadcasted_iota(jnp.int32, (rows, CAP), 1).astype(F32)
    routers = jnp.concatenate([full[:, 4 * D :], full[:, 4 * D :]], axis=1)
    total = jnp.zeros((D, 2 * LANES), F32)
    for d, (mix, back_out, mix_out) in enumerate(((m0, b0, x0), (m1, b1, x1), (m2, b2, x2), (m3, b3, x3))):
        at = slice(d * rows, (d + 1) * rows)
        info = spot_col[at, :]
        puts = []
        for e in range(4):
            start = pl.multiple_of(plan[e * 8 + d], 16)
            stack[e * CAP : (e + 1) * CAP, :] = (res0, res1)[e // 2][e % 2, pl.ds(start, CAP), :]
            puts.append(jnp.where(slot_along == info[:, e : e + 1], 1.0, 0.0).astype(BF16))
        got = dot_nn(jnp.concatenate(puts, axis=1), stack[...])
        mix_out[...] = got[:, :D].astype(BF16)
        ends = got[:, 2 * D :]
        held = jnp.where(lane < EXPERTS, ends + pltpu.roll(ends, LANES - 32, 1), 0.0)
        gate = jnp.transpose(
            jnp.concatenate([gates[:, at], jnp.zeros((LANES - EXPERTS, rows), F32)], axis=0)
        )
        change = held - jnp.sum(held, axis=1, keepdims=True) * gate
        task = info[:, 32:33]
        early = jnp.where((lane < EXPERTS) & (task < 0.5), change, 0.0)
        late = jnp.where(
            (lane >= EXPERTS) & (lane < 2 * EXPERTS) & (task > 0.5), pltpu.roll(change, EXPERTS, 1), 0.0
        )
        both = early + late
        high = both.astype(BF16)
        low = (both - high.astype(F32)).astype(BF16)
        parts = jnp.concatenate([high, low], axis=1)
        pulled = dot_nt(parts, routers)
        total = total + dot_tn(mix[...], parts)
        back_out[...] = (got[:, D : 2 * D] + pulled).astype(BF16)
    router_out[...] = total[:, :LANES] + total[:, LANES:]


def combine_call(plan, mixes, spot_col, gates, full, results):
    rows = mixes[0].shape[0]
    return once(
        combine_kernel, (plan,), (*mixes, spot_col, gates, full, *results),
        (((rows, D), BF16),) * 8 + (((D, LANES), F32),),
        "combine", 40, (((4 * CAP, 2 * D + LANES), BF16),),
    )


def turn_kernel(b0, r1, r2, r3, middle, grad, full, att, lse_row, middle_grad, sent, dots_col, output_grad, norm_two):
    rows = middle.shape[0]
    norms = norm_rows_of(full)
    mixed_grad = b0[...].astype(F32) + r1[...].astype(F32) + r2[...].astype(F32) + r3[...].astype(F32)
    unit, scale = unit_rows(middle[...])
    norm_two[...] = jnp.zeros_like(norm_two)
    norm_two[0:1, :] = jnp.sum(mixed_grad * unit, axis=0, keepdims=True)
    norm_two[1:2, :] = jnp.sum(mixed_grad, axis=0, keepdims=True)
    pulled = mixed_grad * norms[2:3]
    through = pulled - jnp.mean(pulled, axis=1, keepdims=True)
    through = scale * (through - unit * jnp.mean(pulled * unit, axis=1, keepdims=True))
    whole = through + grad[...].astype(F32)
    middle_grad[...] = whole
    branch = whole.astype(BF16)
    output_grad[...] = dot_tn(att[...].astype(BF16), branch).astype(BF16)
    pulled = dot_nt(branch, full[:, 3 * D : 4 * D]).astype(BF16)
    sent[0:rows, :] = pulled
    product = pulled.astype(F32) * att[...]
    high = product.astype(BF16)
    low = (product - high.astype(F32)).astype(BF16)
    heads = (
        lax.broadcasted_iota(jnp.int32, (D, LANES), 0) // HEAD_DIM
        == lax.broadcasted_iota(jnp.int32, (D, LANES), 1)
    )
    heads = heads.astype(F32).astype(BF16)
    dots = dot_nn(high, heads) + dot_nn(low, heads)
    dots_col[...] = dots
    lines = jnp.concatenate([lse_row[...], jnp.transpose(dots)[:8]], axis=0)
    high = lines.astype(BF16).astype(F32)
    table = jnp.concatenate([high, lines - high], axis=0).astype(BF16)
    half = EXTRA // 2
    sent[rows : rows + half, :] = table[:, :D]
    sent[rows + half : rows + EXTRA, :] = jnp.zeros((half, D), BF16)
    sent[rows + half : rows + EXTRA, : rows - D] = table[:, D:]


def turn_call(back, received, middle, grad, full, att, lse_row):
    rows = middle.shape[0]
    return once(
        turn_kernel, (), (back, *received, middle, grad, full, att, lse_row),
        (((rows, D), F32), ((rows + EXTRA, D), BF16), ((rows, LANES), F32), ((D, D), BF16), ((8, D), F32)),
        "turn", 24,
    )


def attention_back_kernel(
    meta, ends, image, qkv, s0, s1, s2, s3, lse_col, dots_col, own, full, middle_grad, output_grad, norm_two, routers,
    input_grad, to0, to1, to2, to3,
    lines, grads, packed, acc_one, acc_two, shared,
):
    rows = input_grad.shape[0]
    half_extra = EXTRA // 2
    for d, ref in enumerate((s0, s1, s2, s3)):
        grads[d] = ref[0:rows, :]
        table = jnp.concatenate(
            [ref[rows : rows + half_extra, :], ref[rows + half_extra : rows + EXTRA, : rows - D]], axis=1
        ).astype(F32)
        lines[d] = table[:16] + table[16:]
    own_row = images_of(meta, image, 0)
    own_col = jnp.transpose(jnp.broadcast_to(own_row, (LANES, rows)))[:, :1]
    lane = lax.broadcasted_iota(jnp.int32, (rows, LANES), 1)
    none = jnp.zeros((), BF16)
    here = slice(0, rows)

    def pair_of_heads(pair, carry):
        lanes = pl.ds(pl.multiple_of(pair * LANES, LANES), LANES)
        made = []
        for half in range(2):
            head = 2 * pair + half
            held = (lane < HEAD_DIM) if half == 0 else (lane >= HEAD_DIM)
            query = jnp.where(held, qkv[pair, here, :], none)
            pull = jnp.where(held, grads[0, :, lanes], none)
            log_total = jnp.sum(jnp.where(lane == head, lse_col[...], 0.0), axis=1, keepdims=True)
            dots = jnp.sum(jnp.where(lane == head, dots_col[...], 0.0), axis=1, keepdims=True)
            acc_one[...] = jnp.zeros_like(acc_one)

            def over_keys(d, c):
                @pl.when(wanted(meta, ends, d))
                def _():
                    at = pl.ds(pl.multiple_of(d * rows, rows), rows)
                    key = qkv[PAIRS + pair, at, :]
                    same = own_col == images_of(meta, image, d)
                    shares = jnp.where(same, jnp.exp(dot_nt(query, key) - log_total), 0.0)
                    change = dot_nt(pull, qkv[2 * PAIRS + pair, at, :]) - dots
                    acc_one[...] += dot_nn((shares * change).astype(BF16), key)

                return c

            lax.fori_loop(0, 4, over_keys, 0)
            made.append(acc_one[...])
        packed[:, lanes] = jnp.where(lane < HEAD_DIM, made[0], made[1]) * (HEAD_DIM ** (-0.5))
        made = []
        for half in range(2):
            head = 2 * pair + half
            held = (lane < HEAD_DIM) if half == 0 else (lane >= HEAD_DIM)
            key = jnp.where(held, qkv[PAIRS + pair, here, :], none)
            value = jnp.where(held, qkv[2 * PAIRS + pair, here, :], none)
            acc_one[...] = jnp.zeros_like(acc_one)
            acc_two[...] = jnp.zeros_like(acc_two)

            def over_queries(d, c):
                @pl.when(wanted(meta, ends, d))
                def _():
                    at = pl.ds(pl.multiple_of(d * rows, rows), rows)
                    query = qkv[pair, at, :]
                    pull = grads[d, :, lanes]
                    same = own_col == images_of(meta, image, d)
                    log_total = lines[d, pl.ds(head, 1), :]
                    dots = lines[d, pl.ds(8 + head, 1), :]
                    shares = jnp.where(same, jnp.exp(dot_nt(key, query) - log_total), 0.0)
                    change = dot_nt(value, pull) - dots
                    acc_two[...] += dot_nn(shares.astype(BF16), pull)
                    acc_one[...] += dot_nn((shares * change).astype(BF16), query)

                return c

            lax.fori_loop(0, 4, over_queries, 0)
            made.append((acc_one[...], acc_two[...]))
        shift = pl.ds(pl.multiple_of(D + pair * LANES, LANES), LANES)
        packed[:, shift] = jnp.where(lane < HEAD_DIM, made[0][0], made[1][0])
        shift = pl.ds(pl.multiple_of(2 * D + pair * LANES, LANES), LANES)
        packed[:, shift] = jnp.where(lane < HEAD_DIM, made[0][1], made[1][1])
        return carry

    lax.fori_loop(0, PAIRS, pair_of_heads, 0)
    norms = norm_rows_of(full)
    unit, scale = unit_rows(own[0:rows, :].astype(F32))
    normed = (unit * norms[0:1] + norms[1:2]).astype(BF16)
    normed_grad = jnp.zeros((rows, D), F32)
    for third in range(3):
        part = packed[:, third * D : (third + 1) * D].astype(BF16)
        normed_grad = normed_grad + dot_nt(part, full[:, third * D : (third + 1) * D])
        weight_grad = dot_tn(normed, part).astype(BF16)
        for j in range(PAIRS):
            block = third * PAIRS + j
            shared[meta[4 + block // 4], :, block % 4 * LANES : (block % 4 + 1) * LANES] = weight_grad[
                :, j * LANES : (j + 1) * LANES
            ]
    pulled = normed_grad * norms[0:1]
    through = pulled - jnp.mean(pulled, axis=1, keepdims=True)
    through = scale * (through - unit * jnp.mean(pulled * unit, axis=1, keepdims=True))
    input_grad[...] = through + middle_grad[...]
    for j in range(PAIRS):
        block = 3 * PAIRS + j
        shared[meta[4 + block // 4], :, block % 4 * LANES : (block % 4 + 1) * LANES] = output_grad[
            :, j * LANES : (j + 1) * LANES
        ]
    lines_norm = jnp.concatenate(
        [
            jnp.zeros((NORM_AT, D), F32),
            jnp.sum(normed_grad * unit, axis=0, keepdims=True),
            jnp.sum(normed_grad, axis=0, keepdims=True),
            norm_two[0:2, :],
            jnp.zeros((LANES - NORM_AT - 4, D), F32),
        ],
        axis=0,
    )
    small = routers[...] + jnp.transpose(lines_norm)
    shared[meta[7], :, 0:LANES] = small.astype(BF16)
    shared[meta[7], :, LANES:] = jnp.zeros((D, 3 * LANES), BF16)
    part = D // 8
    for d, ref in enumerate((to0, to1, to2, to3)):
        for owner in range(8):
            at = pl.ds(pl.multiple_of(meta[28 + owner], 16), part)
            ref[at, :] = shared[d, owner * part : (owner + 1) * part, :]


def attention_back_call(meta, image, qkv, sent, lse_col, dots_col, own, full, middle_grad, output_grad, norm_two, routers):
    rows = middle_grad.shape[0]
    return once(
        attention_back_kernel, (meta, image),
        (image, qkv, *sent, lse_col, dots_col, own, full, middle_grad, output_grad, norm_two, routers),
        (((rows, D), F32),) + (((D, 4 * LANES), BF16),) * 4,
        "attention_back", 40,
        (
            ((4, 16, rows), F32), ((4, rows, D), BF16), ((rows, 3 * D), F32), ((rows, LANES), F32),
            ((rows, LANES), F32), ((4, D, 4 * LANES), BF16),
        ),
    )


def adamw(weight, moment, second, gradient, step_rate):
    moment = BETA_FIRST * moment + (1.0 - BETA_FIRST) * gradient
    second = BETA_SECOND * second + (1.0 - BETA_SECOND) * gradient * gradient
    first_hat = moment / (1.0 - BETA_FIRST**STEP)
    second_hat = second / (1.0 - BETA_SECOND**STEP)
    weight = weight - step_rate * (first_hat / (jnp.sqrt(second_hat) + ADAM_EPS) + DECAY * weight)
    return (weight, moment, second)


def adam_kernel(meta, ready, passed, w1, m1, v1, w2, m2, v2, *rest):
    outs = rest[-6:]
    step = pl.program_id(0)
    half_steps = pl.num_programs(0) // 2
    mine = (step // half_steps) == meta[1]
    inner = step % half_steps
    up_rows, down_rows = w1.shape[1], w2.shape[1]
    half = FFN // 2
    quarter = D // 2

    def pick(rows_at, lanes_at):
        return jnp.where(mine, ready[rows_at, lanes_at], passed[rows_at, lanes_at]).astype(F32)

    per = D // down_rows
    down = pick(
        pl.ds(pl.multiple_of(inner // per * D, D), D), pl.ds(pl.multiple_of(inner % per * down_rows, LANES), down_rows)
    )
    up = jnp.concatenate(
        [
            pick(pl.ds(pl.multiple_of(half + b * quarter + inner * up_rows, 16), up_rows), slice(0, D))
            for b in range(4)
        ],
        axis=1,
    )
    for k, value in enumerate(adamw(w1[0], m1[0], v1[0], up, RATE_EXPAND)):
        outs[k][0] = value
    for k, value in enumerate(adamw(w2[0], m2[0], v2[0], jnp.transpose(down), RATE_REDUCE)):
        outs[3 + k][0] = value


def adam_call(expert, meta, ready, passed, states, previous):
    steps = FFN // LANES
    up = pl.BlockSpec((1, D // steps, FFN), lambda i, *_: (expert, i, 0))
    down = pl.BlockSpec((1, LANES, D), lambda i, *_: (expert, i, 0))
    specs = [whole(ready.shape)] * 2 + [up] * 3 + [down] * 3
    args = [ready, passed, *states]
    aliases = {}
    if previous is not None:
        for k, value in enumerate(previous):
            aliases[1 + len(args)] = k
            args.append(value)
            specs.append(pl.BlockSpec(memory_space=pl.ANY))
    return pl.pallas_call(
        adam_kernel,
        grid_spec=pltpu.PrefetchScalarGridSpec(
            num_scalar_prefetch=1,
            grid=(steps,),
            in_specs=specs,
            out_specs=(up,) * 3 + (down,) * 3,
        ),
        out_shape=tuple(jax.ShapeDtypeStruct(s.shape, F32) for s in states),
        input_output_aliases=aliases,
        compiler_params=room(56),
        cost_estimate=LIGHT,
        name="adam",
    )(meta, *args)


def fold_kernel(a, b, c, d, kept, gone):
    rows = kept.shape[0]
    for ref, at in ((kept, slice(0, rows)), (gone, slice(rows, 2 * rows))):
        ref[...] = (
            a[at, :].astype(F32) + b[at, :].astype(F32) + c[at, :].astype(F32) + d[at, :].astype(F32)
        ).astype(BF16)


def fold_call(parts):
    rows, cols = parts[0].shape
    return once(fold_kernel, (), parts, (((rows // 2, cols), BF16),) * 2, "fold", 8)


def split_kernel(kept, came, *outs):
    for k, ref in enumerate(outs):
        at = slice(k * ref.shape[0], (k + 1) * ref.shape[0])
        ref[...] = (kept[at, :].astype(F32) + came[at, :].astype(F32)).astype(BF16)


def split_call(kept, came):
    rows, cols = kept.shape
    return once(split_kernel, (), (kept, came), (((rows // 4, cols), BF16),) * 4, "split", 8)


def settle_kernel(meta, *refs):
    pieces, states, outs, (buffer, square) = refs[:4], refs[4:16], refs[16:28], refs[28:]
    rows = pieces[0].shape[0]
    for d in range(4):
        buffer[meta[4 + d]] = pieces[d][...].astype(F32)
    square[...] = jnp.zeros_like(square)
    square[0:rows, :] = buffer[3, :, 0:LANES]
    turned = jnp.transpose(square[...])
    attend_sum = jnp.concatenate([buffer[0], buffer[1], buffer[2, :, 0:LANES]], axis=1)
    sums = (turned[NORM_AT : NORM_AT + 4, :rows], attend_sum, buffer[2, :, LANES:])
    for k, (total, rate) in enumerate(zip(sums, (RATE_NORM, RATE_ATTEND, RATE_OUTPUT))):
        held = [ref[...] for ref in states[3 * k : 3 * k + 3]]
        for ref, value in zip(outs[3 * k : 3 * k + 3], adamw(*held, total, rate)):
            ref[...] = value
    for t in range(TASKS):
        held = [ref[t] for ref in states[9:12]]
        total = turned[t * EXPERTS : (t + 1) * EXPERTS, :rows]
        for ref, value in zip(outs[9:12], adamw(*held, total, RATE_ROUTER)):
            ref[t] = value


def settle_call(meta, pieces, states):
    rows, cols = pieces[0].shape
    return once(
        settle_kernel, (meta,), (*pieces, *states), tuple((s.shape, F32) for s in states),
        "settle", 12, (((4, rows, cols), F32), ((LANES, LANES), F32)),
    )


def swap_expert(value, d):
    return lax.ppermute(value, "expert", [(i, i ^ d) for i in range(4)])


def swap_tall(value, d):
    return lax.ppermute(value, "dp", [(2 * a + c, 2 * (a ^ d) + c) for a in range(4) for c in range(2)])


def swap_core(value):
    return lax.ppermute(value, "dp", [(i, i ^ 1) for i in range(8)])


def send_tall(value, hops):
    return lax.ppermute(value, "dp", [(2 * a + c, 2 * b + c) for a, b in hops for c in range(2)])


def tie(value, *others):
    flat, tree = jax.tree.flatten((value, others))
    return jax.tree.unflatten(tree, lax.optimization_barrier(flat))[0]


def fast_body(
    patches, out_grad, image_of, task_of, routes,
    norm_weight, norm_moment, norm_second,
    attend_weight, attend_moment, attend_second,
    output_weight, output_moment, output_second,
    router_weight, router_moment, router_second,
    expand_weight, expand_moment, expand_second,
    reduce_weight, reduce_moment, reduce_second,
):
    member = lax.axis_index("expert")
    place = lax.axis_index("dp")
    rows = patches.shape[1]
    count = expand_weight.shape[0]
    table = place_table(count, attend_weight.shape[0])
    meta = lax.dynamic_index_in_dim(jnp.asarray(table), place * 4 + member, 0, False)
    inner = (place >= 2) & (place < 6)
    image = image_of

    own, shard = pack_call(patches, routes, task_of, attend_weight, output_weight, router_weight, norm_weight)
    shards = [shard] + [swap_tall(shard, d) for d in (1, 2, 3)]
    pieces = [own] + [swap_expert(own, d) for d in (1, 2, 3)]
    shards = shards + [swap_core(s) for s in shards]
    grad = out_grad[0]
    grads = [grad] + [swap_expert(grad, d) for d in (1, 2, 3)]

    qkv, full, att, lse_col, lse_row, middle, mixed = front_call(meta, image, pieces, shards)
    mixes = [mixed] + [swap_expert(mixed, d) for d in (1, 2, 3)]
    spot_row, choice, spot_col, plan = route_call(meta, pieces, count)

    up_low = tie(expand_weight, mixed).astype(BF16)
    down_low = tie(reduce_weight, mixed).astype(BF16)

    def first_hop(value):
        return send_tall(value, ((0, 1), (3, 2)))

    def second_hop(value):
        return send_tall(value, ((1, 2), (2, 1)))

    def third_hop(value):
        return send_tall(value, ((1, 0), (2, 3)))

    def settled(value, came):
        return jnp.where(inner, value, came)

    mine0, other0, mine1, other1, res0, gates = expert_call(
        0, plan, meta, mixes, grads, spot_row, choice, full, up_low, down_low
    )
    half0 = mine0 + swap_core(other0)
    half1 = mine1 + swap_core(other1)
    came_a0, came_a1 = first_hop(half0), first_hop(half1)
    mine2, other2, mine3, other3, res1, _ = expert_call(
        2, plan, meta, mixes, grads, spot_row, choice, tie(gates, half0, half1), up_low, down_low
    )
    pair0 = half0 + tie(came_a0, mine2)
    came_b0 = second_hop(pair0)
    got2, got3 = swap_core(other2), swap_core(other3)
    *outs, routers = combine_call(plan, mixes, spot_col, tie(gates, pair0), full, (res0, res1))
    back, mix = outs[:4], outs[4:]
    returned = [swap_expert(back[d], d) for d in (1, 2, 3)]
    half2 = mine2 + tie(got2, routers)
    half3 = mine3 + tie(got3, routers)
    came_a2, came_a3 = first_hop(half2), first_hop(half3)
    pair1 = half1 + tie(came_a1, half3)
    came_b1 = second_hop(pair1)
    whole0 = pair0 + tie(came_b0, half3)
    came_c0 = third_hop(whole0)
    middle_grad, sent, dots_col, output_grad, norm_two = turn_call(
        tie(back[0], pair1, whole0), returned, middle, grad, full, att, lse_row
    )
    sents = [sent] + [swap_expert(sent, d) for d in (1, 2, 3)]
    pair2 = half2 + tie(came_a2, norm_two)
    came_b2 = second_hop(pair2)
    whole1 = pair1 + tie(came_b1, norm_two)
    came_c1 = third_hop(whole1)
    ready0 = settled(whole0, tie(came_c0, norm_two))
    passed0 = swap_core(ready0)
    input_grad, *shared = attention_back_call(
        meta, image, qkv, sents, tie(lse_col, pair2, whole1, ready0), dots_col, own, full, middle_grad,
        output_grad, norm_two, routers,
    )
    shared = [shared[0]] + [swap_expert(shared[d], d) for d in (1, 2, 3)]
    pair3 = half3 + tie(came_a3, input_grad)
    came_b3 = second_hop(pair3)
    whole2 = pair2 + tie(came_b2, input_grad)
    came_c2 = third_hop(whole2)
    ready1 = settled(whole1, tie(came_c1, input_grad))
    passed1 = swap_core(ready1)
    states = (expand_weight, expand_moment, expand_second, reduce_weight, reduce_moment, reduce_second)
    news = adam_call(0, meta, tie(ready0, pair3, whole2, ready1), passed0, states, None)
    kept, gone = fold_call([tie(shared[0], news[0])] + shared[1:])
    gone = swap_core(gone)
    parts = [swap_expert(tie(mix[d], kept), d) for d in (1, 2, 3)]
    news = adam_call(1, meta, tie(ready1, kept), passed1, states, news)
    whole3 = pair3 + tie(came_b3, news[0])
    came_c3 = third_hop(whole3)
    ready2 = settled(whole2, tie(came_c2, news[0]))
    passed2 = swap_core(ready2)
    piece, *away = split_call(tie(kept, news[0]), gone)
    away = [swap_tall(away[d - 1], d) for d in (1, 2, 3)]
    news = adam_call(2, meta, tie(ready2, whole3, piece), passed2, states, news)
    piece = tie(piece, news[0]) + away[0] + away[1] + away[2]
    quarters = [piece] + [swap_expert(piece, d) for d in (1, 2, 3)]
    block_out = middle + tie(mix[0], news[0]).astype(F32)
    for part in parts:
        block_out = block_out + part.astype(F32)
    block_out = block_out.astype(BF16)[None]
    ready3 = settled(whole3, tie(came_c3, block_out))
    passed3 = swap_core(ready3)
    small = settle_call(
        meta, [tie(quarters[0], ready3)] + quarters[1:],
        (
            norm_weight, norm_moment, norm_second, attend_weight, attend_moment, attend_second,
            output_weight, output_moment, output_second, router_weight, router_moment, router_second,
        ),
    )
    news = adam_call(3, meta, tie(ready3, small[0]), passed3, states, news)
    return (block_out, input_grad[None], *small, *news)


def gelu_exact(values):
    return 0.5 * values * (1.0 + lax.erf(values * 0.7071067811865476))


def norm_rows(values, gain_row, offset):
    average = jnp.mean(values, axis=-1, keepdims=True)
    centred = values - average
    spread = jnp.mean(centred * centred, axis=-1, keepdims=True)
    return centred * lax.rsqrt(spread + NORM_EPS) * gain_row + offset


def body(
    patches,
    out_grad,
    image_of,
    task_of,
    routes,
    norm_weight,
    norm_moment,
    norm_second,
    attend_weight,
    attend_moment,
    attend_second,
    output_weight,
    output_moment,
    output_second,
    router_weight,
    router_moment,
    router_second,
    expand_weight,
    expand_moment,
    expand_second,
    reduce_weight,
    reduce_moment,
    reduce_second,
):
    precise = lax.Precision.HIGHEST
    member = lax.axis_index("expert")
    tokens = patches.shape[1]
    group_rows = image_of.shape[1]
    key_rows = min(512, group_rows)
    score_scale = HEAD_DIM ** (-0.5)
    norm_full, attend_full, output_full, router_full = (
        lax.all_gather(norm_weight.astype(jnp.bfloat16), "dp", axis=1, tiled=True),
        lax.all_gather(attend_weight.astype(jnp.bfloat16), "dp", axis=0, tiled=True),
        lax.all_gather(output_weight.astype(jnp.bfloat16), "dp", axis=0, tiled=True),
        lax.all_gather(router_weight.astype(jnp.bfloat16), "dp", axis=2, tiled=True),
    )
    norm_values = norm_full.astype(jnp.float32)
    router_values = router_full.astype(jnp.float32)
    expand_low = expand_weight.astype(jnp.bfloat16)
    reduce_low = reduce_weight.astype(jnp.bfloat16)
    inputs = patches[0].astype(jnp.float32)
    image_row = image_of[0]
    my_image = lax.dynamic_slice_in_dim(image_row, member * tokens, tokens)
    task_row = task_of[0]
    route_rows = routes[0]
    first_image = my_image[0]
    last_image = my_image[tokens - 1]
    first_key = jnp.sum((image_row < first_image).astype(jnp.int32))
    last_key = jnp.sum((image_row <= last_image).astype(jnp.int32)) - 1
    first_block = first_key // key_rows
    end_block = last_key // key_rows + 1
    normed_one, first_back = jax.vjp(norm_rows, inputs, norm_values[0], norm_values[1])
    normed_low = normed_one.astype(jnp.bfloat16)
    packed = jnp.dot(normed_low, attend_full, preferred_element_type=jnp.float32).astype(
        jnp.bfloat16
    )
    queries = packed[:, :D].reshape(tokens, HEADS, HEAD_DIM)
    key_value = packed[:, D:]
    key_value_all = lax.all_gather(key_value, "expert", axis=0, tiled=True)
    keys_all = key_value_all[:, :D].reshape(group_rows, HEADS, HEAD_DIM)
    values_all = key_value_all[:, D:].reshape(group_rows, HEADS, HEAD_DIM)

    def scores_of(query_part, key_part, same_image):
        raw = (
            jnp.einsum("thd,khd->htk", query_part, key_part, preferred_element_type=jnp.float32)
            * score_scale
        )
        return jnp.where(same_image[None], raw, MASKED)

    def block_at(block_index):
        first_row = block_index * key_rows
        key_part = lax.dynamic_slice_in_dim(keys_all, first_row, key_rows, 0)
        value_part = lax.dynamic_slice_in_dim(values_all, first_row, key_rows, 0)
        same_image = (
            my_image[:, None]
            == lax.dynamic_slice_in_dim(image_row, first_row, key_rows, 0)[None, :]
        )
        return (key_part, value_part, same_image)

    def max_step(block_index, state_in):
        highest, totals = state_in
        key_part, value_part, same_image = block_at(block_index)
        scores = scores_of(queries, key_part, same_image)
        raised = jnp.maximum(highest, jnp.max(scores, axis=-1))
        shares = jnp.where(same_image[None], jnp.exp(scores - raised[..., None]), 0.0)
        return (raised, totals * jnp.exp(highest - raised) + jnp.sum(shares, axis=-1))

    start_max = jnp.full((HEADS, tokens), MASKED, jnp.float32)
    highest, totals = lax.fori_loop(
        first_block, end_block, max_step, (start_max, jnp.zeros((HEADS, tokens), jnp.float32))
    )
    log_total = highest + jnp.log(totals)

    def value_step(block_index, accum):
        key_part, value_part, same_image = block_at(block_index)
        scores = scores_of(queries, key_part, same_image)
        soft_part = jnp.where(same_image[None], jnp.exp(scores - log_total[..., None]), 0.0).astype(
            jnp.bfloat16
        )
        return accum + jnp.einsum(
            "htk,khd->thd", soft_part, value_part, preferred_element_type=jnp.float32
        )

    attended = lax.fori_loop(
        first_block, end_block, value_step, jnp.zeros((tokens, HEADS, HEAD_DIM), jnp.float32)
    )
    attended_low = attended.reshape(tokens, D).astype(jnp.bfloat16)
    branch = jnp.dot(attended_low, output_full, preferred_element_type=jnp.float32)
    middle = inputs + branch
    normed_two, second_back = jax.vjp(norm_rows, middle, norm_values[2], norm_values[3])
    mixed_low = normed_two.astype(jnp.bfloat16)
    task_hot = (task_row[:, None] == jnp.arange(TASKS, dtype=jnp.int32)[None, :]).astype(
        jnp.float32
    )
    route_hot = (
        route_rows[:, :, None] == jnp.arange(EXPERTS, dtype=jnp.int32)[None, None, :]
    ).astype(jnp.float32)

    def gating(hidden, router):
        logits = jnp.einsum("td,ced->tce", hidden, router, precision=precise)
        task_logits = jnp.einsum("tc,tce->te", task_hot, logits, precision=precise)
        chosen = jnp.einsum("te,tke->tk", task_logits, route_hot, precision=precise)
        peak = jnp.max(chosen, axis=-1, keepdims=True)
        raised = jnp.exp(chosen - peak)
        return raised / jnp.sum(raised, axis=-1, keepdims=True)

    gate_values, gate_back = jax.vjp(gating, mixed_low.astype(jnp.float32), router_values)
    pair_expert = route_rows.reshape(-1)
    pair_hot = (pair_expert[:, None] == jnp.arange(EXPERTS, dtype=jnp.int32)[None, :]).astype(
        jnp.int32
    )
    slot_index = jnp.sum((jnp.cumsum(pair_hot, axis=0) - pair_hot) * pair_hot, axis=1)
    flat_slot = pair_expert * CAP + slot_index

    def scatter_pairs(pair_values):
        return (
            jnp.zeros((EXPERTS * CAP, D), pair_values.dtype)
            .at[flat_slot]
            .set(pair_values)
            .reshape(EXPERTS, CAP, D)
        )

    def gather_pairs(buffer):
        return (
            buffer.reshape(EXPERTS * CAP, D)[flat_slot].astype(jnp.float32).reshape(tokens, TOP, D)
        )

    received = lax.all_to_all(
        scatter_pairs(jnp.repeat(mixed_low, TOP, axis=0)),
        "expert",
        split_axis=0,
        concat_axis=1,
        tiled=True,
    )
    hidden_pre = jnp.einsum(
        "ecd,edh->ech", received, expand_low, preferred_element_type=jnp.float32
    )
    active, gelu_back = jax.vjp(gelu_exact, hidden_pre)
    active_low = active.astype(jnp.bfloat16)
    expert_out = jnp.einsum(
        "ech,ehd->ecd", active_low, reduce_low, preferred_element_type=jnp.float32
    ).astype(jnp.bfloat16)
    returned = lax.all_to_all(expert_out, "expert", split_axis=1, concat_axis=0, tiled=True)
    pair_out = gather_pairs(returned)
    expert_mix = jnp.einsum("tk,tkd->td", gate_values, pair_out, precision=precise)
    block_out = (middle + expert_mix).astype(jnp.bfloat16)[None]
    upstream = out_grad[0].astype(jnp.float32)
    gate_grad = jnp.sum(upstream[:, None, :] * pair_out, axis=-1)
    pair_grad = (
        (gate_values[:, :, None] * upstream[:, None, :])
        .astype(jnp.bfloat16)
        .reshape(tokens * TOP, D)
    )
    grad_in = lax.all_to_all(
        scatter_pairs(pair_grad), "expert", split_axis=0, concat_axis=1, tiled=True
    )
    reduce_grad = jnp.einsum(
        "ech,ecd->ehd", active_low, grad_in, preferred_element_type=jnp.float32
    )
    active_grad = jnp.einsum(
        "ecd,ehd->ech", grad_in, reduce_low, preferred_element_type=jnp.float32
    )
    pre_grad = gelu_back(active_grad)[0].astype(jnp.bfloat16)
    expand_grad = jnp.einsum("ecd,ech->edh", received, pre_grad, preferred_element_type=jnp.float32)
    back_rows = jnp.einsum(
        "ech,edh->ecd", pre_grad, expand_low, preferred_element_type=jnp.float32
    ).astype(jnp.bfloat16)
    expand_sum, reduce_sum = (
        lax.psum(expand_grad.astype(jnp.bfloat16), "dp").astype(jnp.float32),
        lax.psum(reduce_grad.astype(jnp.bfloat16), "dp").astype(jnp.float32),
    )
    came_back = lax.all_to_all(back_rows, "expert", split_axis=1, concat_axis=0, tiled=True)
    routed_grad = jnp.sum(gather_pairs(came_back), axis=1)
    hidden_gate_grad, router_grad = gate_back(gate_grad)
    middle_part, gain_two, offset_two = second_back(routed_grad + hidden_gate_grad)
    middle_grad = middle_part + upstream
    branch_grad = middle_grad.astype(jnp.bfloat16)
    output_grad = jnp.einsum(
        "td,te->de", attended_low, branch_grad, preferred_element_type=jnp.float32
    )
    attended_grad = (
        jnp.einsum("te,de->td", branch_grad, output_full, preferred_element_type=jnp.float32)
        .astype(jnp.bfloat16)
        .reshape(tokens, HEADS, HEAD_DIM)
    )
    row_dots = jnp.einsum(
        "thd,thd->ht", attended_grad.astype(jnp.float32), attended, precision=precise
    )

    def score_grad(query_part, key_part, value_part, grad_part, same_image, log_part, dots_part):
        scores = scores_of(query_part, key_part, same_image)
        soft_part = jnp.where(same_image[None], jnp.exp(scores - log_part[..., None]), 0.0)
        soft_grad = jnp.einsum(
            "thd,khd->htk", grad_part, value_part, preferred_element_type=jnp.float32
        )
        return (soft_part, (soft_part * (soft_grad - dots_part[..., None])).astype(jnp.bfloat16))

    def pair_step(block_index, state_in):
        query_acc, terms_acc = state_in
        key_part, value_part, same_image = block_at(block_index)
        soft_part, dscore = score_grad(
            queries, key_part, value_part, attended_grad, same_image, log_total, row_dots
        )
        query_acc = query_acc + jnp.einsum(
            "htk,khd->thd", dscore, key_part, preferred_element_type=jnp.float32
        )
        key_term = (
            jnp.einsum("htk,thd->khd", dscore, queries, preferred_element_type=jnp.float32)
            * score_scale
        )
        value_term = jnp.einsum(
            "htk,thd->khd",
            soft_part.astype(jnp.bfloat16),
            attended_grad,
            preferred_element_type=jnp.float32,
        )
        terms = jnp.concatenate(
            [key_term.reshape(key_rows, D), value_term.reshape(key_rows, D)], axis=1
        )
        terms_acc = lax.dynamic_update_slice_in_dim(terms_acc, terms, block_index * key_rows, 0)
        return (query_acc, terms_acc)

    query_acc, key_value_terms = lax.fori_loop(
        first_block,
        end_block,
        pair_step,
        (
            jnp.zeros((tokens, HEADS, HEAD_DIM), jnp.float32),
            jnp.zeros((group_rows, 2 * D), jnp.float32),
        ),
    )
    key_value_grad = lax.psum_scatter(
        key_value_terms.astype(jnp.bfloat16), "expert", scatter_dimension=0, tiled=True
    ).astype(jnp.float32)
    query_grad = (query_acc * score_scale).reshape(tokens, D)
    packed_grad = jnp.concatenate([query_grad, key_value_grad], axis=1).astype(jnp.bfloat16)
    attend_grad = jnp.einsum(
        "td,te->de", normed_low, packed_grad, preferred_element_type=jnp.float32
    )
    normed_grad = jnp.einsum(
        "te,de->td", packed_grad, attend_full, preferred_element_type=jnp.float32
    )
    input_part, gain_one, offset_one = first_back(normed_grad)
    input_grad = (middle_grad + input_part)[None]
    norm_grad = jnp.stack([gain_one, offset_one, gain_two, offset_two])
    shared = (norm_grad, attend_grad, output_grad, router_grad)
    summed = (
        lax.psum(shared[0].astype(jnp.bfloat16), "expert").astype(jnp.float32),
        lax.psum(shared[1].astype(jnp.bfloat16), "expert").astype(jnp.float32),
        lax.psum(shared[2].astype(jnp.bfloat16), "expert").astype(jnp.float32),
        lax.psum(shared[3].astype(jnp.bfloat16), "expert").astype(jnp.float32),
    )
    norm_sum, attend_sum, output_sum, router_sum = (
        lax.psum_scatter(
            summed[0].astype(jnp.bfloat16), "dp", scatter_dimension=1, tiled=True
        ).astype(jnp.float32),
        lax.psum_scatter(
            summed[1].astype(jnp.bfloat16), "dp", scatter_dimension=0, tiled=True
        ).astype(jnp.float32),
        lax.psum_scatter(
            summed[2].astype(jnp.bfloat16), "dp", scatter_dimension=0, tiled=True
        ).astype(jnp.float32),
        lax.psum_scatter(
            summed[3].astype(jnp.bfloat16), "dp", scatter_dimension=2, tiled=True
        ).astype(jnp.float32),
    )
    norm_new = adamw(norm_weight, norm_moment, norm_second, norm_sum, RATE_NORM)
    attend_new = adamw(attend_weight, attend_moment, attend_second, attend_sum, RATE_ATTEND)
    output_new = adamw(output_weight, output_moment, output_second, output_sum, RATE_OUTPUT)
    router_new = adamw(router_weight, router_moment, router_second, router_sum, RATE_ROUTER)
    expand_new = adamw(expand_weight, expand_moment, expand_second, expand_sum, RATE_EXPAND)
    reduce_new = adamw(reduce_weight, reduce_moment, reduce_second, reduce_sum, RATE_REDUCE)
    return (
        block_out,
        input_grad,
        norm_new[0],
        norm_new[1],
        norm_new[2],
        attend_new[0],
        attend_new[1],
        attend_new[2],
        output_new[0],
        output_new[1],
        output_new[2],
        router_new[0],
        router_new[1],
        router_new[2],
        expand_new[0],
        expand_new[1],
        expand_new[2],
        reduce_new[0],
        reduce_new[1],
        reduce_new[2],
    )


def solution(mesh):
    placed = (
        P("dp", "expert", None),
        P("dp", "expert", None),
        P("dp", None),
        P("dp", "expert"),
        P("dp", "expert", None),
        P(None, "dp"),
        P(None, "dp"),
        P(None, "dp"),
        P("dp", None),
        P("dp", None),
        P("dp", None),
        P("dp", None),
        P("dp", None),
        P("dp", None),
        P(None, None, "dp"),
        P(None, None, "dp"),
        P(None, None, "dp"),
        P("expert", None, None),
        P("expert", None, None),
        P("expert", None, None),
        P("expert", None, None),
        P("expert", None, None),
        P("expert", None, None),
    )
    fits = mesh.shape["dp"] == 8 and mesh.shape["expert"] == 4
    return jax.shard_map(
        fast_body if fits else body,
        mesh=mesh,
        in_specs=placed,
        out_specs=(
            P("dp", "expert", None),
            P("dp", "expert", None),
            P(None, "dp"),
            P(None, "dp"),
            P(None, "dp"),
            P("dp", None),
            P("dp", None),
            P("dp", None),
            P("dp", None),
            P("dp", None),
            P("dp", None),
            P(None, None, "dp"),
            P(None, None, "dp"),
            P(None, None, "dp"),
            P("expert", None, None),
            P("expert", None, None),
            P("expert", None, None),
            P("expert", None, None),
            P("expert", None, None),
            P("expert", None, None),
        ),
        check_vma=False,
    )
```

```python
import functools

import jax
import jax.numpy as jnp
import numpy as np
from jax import lax
from jax.experimental import pallas as pl
from jax.experimental.pallas import tpu as pltpu
from jax.sharding import PartitionSpec as P

D = 384
HEADS = 6
HEAD_DIM = 64
FFN = 1536
EXPERTS = 16
TASKS = 2
TOP = 4
STEP = 10
CAP = 256
PAIRS = HEADS // 2
LANES = 128
WCOLS = 4 * D + LANES
INFO = 16
NORM_AT = 2 * EXPERTS
EXTRA = 64

NORM_EPS = 1e-06
ADAM_EPS = 1e-08
BETA_FIRST = 0.9
BETA_SECOND = 0.999
DECAY = 0.05
RATE_NORM = 0.5
RATE_ATTEND = 0.2
RATE_OUTPUT = 0.7
RATE_ROUTER = 0.06
RATE_EXPAND = 0.13
RATE_REDUCE = 0.25
MASKED = -1e30
F32 = jnp.float32
BF16 = jnp.bfloat16
LIGHT = pl.CostEstimate(flops=1, transcendentals=0, bytes_accessed=1)


def dot_nn(a, b):
    return lax.dot_general(a, b, (((1,), (0,)), ((), ())), preferred_element_type=F32)


def dot_nt(a, b):
    return lax.dot_general(a, b, (((1,), (1,)), ((), ())), preferred_element_type=F32)


def dot_tn(a, b):
    return lax.dot_general(a, b, (((0,), (0,)), ((), ())), preferred_element_type=F32)


def unit_rows(values):
    average = jnp.mean(values, axis=-1, keepdims=True)
    centred = values - average
    spread = jnp.mean(centred * centred, axis=-1, keepdims=True)
    scale = lax.rsqrt(spread + NORM_EPS)
    return centred * scale, scale


def eye(n):
    rows = lax.broadcasted_iota(jnp.int32, (n, n), 0)
    cols = lax.broadcasted_iota(jnp.int32, (n, n), 1)
    return (rows == cols).astype(F32).astype(BF16)


def norm_rows_of(full_ref):
    return dot_nt(eye(LANES), full_ref[:, 4 * D :])[NORM_AT : NORM_AT + 8]


def vmem():
    return pl.BlockSpec(memory_space=pltpu.VMEM)


def smem():
    return pl.BlockSpec(memory_space=pltpu.SMEM)


def room(mebibytes):
    return pltpu.CompilerParams(vmem_limit_bytes=mebibytes * 2**20)


def whole(shape):
    return pl.BlockSpec(shape, lambda *_: (0,) * len(shape), pipeline_mode=pl.Buffered(1))


def far(value):
    return pltpu.with_memory_space_constraint(value, pltpu.HBM)


def once(kernel, scalars, arrays, outs, name, mebibytes, scratch=()):
    return pl.pallas_call(
        kernel,
        grid=(1,),
        in_specs=[smem()] * len(scalars) + [whole(a.shape) for a in arrays],
        out_specs=tuple(whole(o[0]) for o in outs),
        out_shape=tuple(jax.ShapeDtypeStruct(*o) for o in outs),
        scratch_shapes=[pltpu.VMEM(*held) for held in scratch],
        compiler_params=room(mebibytes),
        cost_estimate=LIGHT,
        name=name,
    )(*scalars, *arrays)


def place_table(count, shard_rows):
    table = np.zeros((32, 48), np.int32)
    for place in range(8):
        for member in range(4):
            tall, core = place // 2, place % 2
            row = table[place * 4 + member]
            row[0:3] = member * count, core, tall in (1, 2)
            for d in range(4):
                row[4 + d] = member ^ d
                row[16 + d] = shard_rows * (2 * (tall ^ d) + core)
                row[20 + d] = shard_rows * (2 * (tall ^ d) + 1 - core)
            for owner in range(8):
                row[28 + owner] = shard_rows * ((owner % 2 ^ core) * 4 + (owner // 2 ^ tall))
    return table


def wanted(meta, ends, d):
    rows = ends.shape[1] // 4
    here, there = meta[4] * rows, meta[4 + d] * rows
    return (ends[0, there] <= ends[0, here + rows - 1]) & (ends[0, there + rows - 1] >= ends[0, here])


def images_of(meta, image, d):
    rows = image.shape[1] // 4
    return image[0:1, pl.ds(pl.multiple_of(meta[4 + d] * rows, LANES), rows)].astype(F32)


def pack_kernel(
    patches, routes, tasks, attend, output, router, norm, own, shard, wide, square,
):
    rows = patches.shape[1]
    shard_rows = attend.shape[0]
    shard[:, 0 : 3 * D] = attend[...].astype(BF16)
    shard[:, 3 * D : 4 * D] = output[...].astype(BF16)
    square[...] = jnp.zeros_like(square)
    for t in range(TASKS):
        square[t * EXPERTS : (t + 1) * EXPERTS, 0:shard_rows] = router[t]
    square[NORM_AT : NORM_AT + 4, 0:shard_rows] = norm[...]
    shard[:, 4 * D :] = jnp.transpose(square[...])[:shard_rows].astype(BF16)
    own[0:rows, :] = patches[0]
    wide[...] = jnp.zeros_like(wide)
    wide[:, 0:TOP] = routes[0].astype(F32)
    lists = jnp.concatenate([jnp.transpose(wide[...])[:TOP], tasks[...].astype(F32)], axis=0)
    rest = jnp.concatenate([lists[:, D:], jnp.zeros((TOP + 1, 2 * D - rows), F32)], axis=1)
    lines = []
    for k in range(TOP + 1):
        lines = lines + [lists[k : k + 1, :D], rest[k : k + 1]]
    lines = lines + [jnp.zeros((INFO - 2 * (TOP + 1), D), F32)]
    own[rows : rows + INFO, :] = jnp.concatenate(lines, axis=0).astype(BF16)


def pack_call(patches, routes, tasks, attend, output, router, norm):
    rows = patches.shape[1]
    return once(
        pack_kernel, (), tuple(map(far, (patches, routes, tasks, attend, output, router, norm))),
        (((rows + INFO, D), BF16), ((attend.shape[0], WCOLS), BF16)),
        "pack", 12, (((rows, LANES), F32), ((LANES, LANES), F32)),
    )


def join_kernel(s0, s1, s2, s3, joined):
    part = s0.shape[0]
    for d, ref in enumerate((s0, s1, s2, s3)):
        joined[d * part : (d + 1) * part, :] = ref[...]


def join_call(shards):
    rows, cols = shards[0].shape
    return once(join_kernel, (), shards, (((4 * rows, cols), BF16),), "join", 12)[0]


def route_kernel(meta, i0, i1, i2, i3, row_out, pick_out, col_out, plan_out):
    base = meta[0]
    rows = i0.shape[1] + LANES
    later = lax.broadcasted_iota(jnp.int32, (rows, rows), 0)
    token = lax.broadcasted_iota(jnp.int32, (rows, rows), 1)
    before = (later < token).astype(F32).astype(BF16)
    one = (later == token).astype(F32).astype(BF16)
    local = row_out.shape[0]
    which = lax.broadcasted_iota(jnp.int32, (local, rows), 0)
    slot_names = (which + base).astype(F32)
    every = lax.broadcasted_iota(jnp.int32, (EXPERTS, rows), 0).astype(F32)
    experts = plan_out.shape[0] // 8
    starts = [jnp.int32(0)] * experts
    for d, ref in enumerate((i0, i1, i2, i3)):
        info = ref[...].astype(F32)

        def line(k):
            return jnp.concatenate([info[2 * k : 2 * k + 1], info[2 * k + 1 : 2 * k + 2, :LANES]], axis=1)

        mine = jnp.zeros((local, rows), jnp.bool_)
        chosen = jnp.zeros((EXPERTS, rows), jnp.bool_)
        for k in range(TOP):
            named = line(k)
            mine = mine | (slot_names == named)
            chosen = chosen | (every == named)
        mine = jnp.where(mine & (which < experts), 1.0, 0.0)
        chosen = jnp.where(chosen, 1.0, 0.0)
        rank = dot_nn(mine.astype(BF16), before)
        spot = jnp.where(mine > 0.5, rank, -1.0)
        at = slice(d * rows, (d + 1) * rows)
        row_out[:, at] = spot
        tasks = jnp.broadcast_to(line(TOP), (8, rows))
        pick_out[0:EXPERTS, at] = chosen
        pick_out[EXPERTS:, at] = tasks
        table = jnp.concatenate(
            [spot, jnp.zeros((16 - local, rows), F32), chosen, tasks, jnp.zeros((LANES - 40, rows), F32)],
            axis=0,
        )
        col_out[d * rows : (d + 1) * rows, :] = dot_nt(one, table.astype(BF16))
        for e in range(experts):
            held = jnp.sum(mine[e : e + 1, :]).astype(jnp.int32)
            plan_out[e * 8 + d] = starts[e]
            starts[e] = starts[e] + (held + 15) // 16 * 16
    for e in range(experts):
        plan_out[e * 8 + 4] = starts[e]
        plan_out[e * 8 + 5] = (starts[e] + CAP - 1) // CAP


def route_call(meta, pieces, experts):
    rows = pieces[0].shape[0] - INFO
    return pl.pallas_call(
        route_kernel,
        grid=(1,),
        in_specs=[smem()] + [pl.BlockSpec((INFO, D), lambda i: (rows // INFO, 0))] * 4,
        out_specs=(
            pl.BlockSpec((8, 4 * rows), lambda i: (0, 0)),
            pl.BlockSpec((EXPERTS + 8, 4 * rows), lambda i: (0, 0)),
            pl.BlockSpec((4 * rows, LANES), lambda i: (0, 0)),
            smem(),
        ),
        out_shape=(
            jax.ShapeDtypeStruct((8, 4 * rows), F32),
            jax.ShapeDtypeStruct((EXPERTS + 8, 4 * rows), F32),
            jax.ShapeDtypeStruct((4 * rows, LANES), F32),
            jax.ShapeDtypeStruct((experts * 8,), jnp.int32),
        ),
        compiler_params=room(24),
        cost_estimate=LIGHT,
        name="routing",
    )(meta, *pieces)


def front_kernel(
    meta, ends, image, p0, p1, p2, p3, near, away,
    qkv, full, att, lse_col, lse_row, middle, mixed,
    everything, scores, top, total, out_acc,
):
    rows = att.shape[0]
    part = near.shape[0] // 4
    for j in range(8):
        held = (near, away)[j // 4]
        full[pl.ds(pl.multiple_of(meta[16 + j], 16), part), :] = held[j % 4 * part : (j % 4 + 1) * part, :]
    for d, ref in enumerate((p0, p1, p2, p3)):
        everything[d * rows : (d + 1) * rows, :] = ref[:rows, :]
    norms = norm_rows_of(full)
    tile = 256

    def project(i, carry):
        at = pl.ds(pl.multiple_of(i * tile, tile), tile)
        unit, _ = unit_rows(everything[at, :].astype(F32))
        normed = (unit * norms[0:1] + norms[1:2]).astype(BF16)
        for third in range(3):
            made = dot_nn(normed, full[:, third * D : (third + 1) * D]).astype(BF16)
            if third == 0:
                made = made * jnp.asarray(HEAD_DIM ** (-0.5), BF16)
            for part in range(PAIRS):
                qkv[third * PAIRS + part, at, :] = made[:, part * LANES : (part + 1) * LANES]
        return carry

    lax.fori_loop(0, 4 * rows // tile, project, 0)
    own_row = images_of(meta, image, 0)
    own_col = jnp.transpose(jnp.broadcast_to(own_row, (LANES, rows)))[:, :1]
    lane = lax.broadcasted_iota(jnp.int32, (rows, LANES), 1)
    lse_col[...] = jnp.zeros_like(lse_col)

    def pair_of_heads(pair, carry):
        done = []
        for half in range(2):
            held = (lane < HEAD_DIM) if half == 0 else (lane >= HEAD_DIM)
            query = jnp.where(held, qkv[pair, 0:rows, :], jnp.zeros((), BF16))
            top[...] = jnp.full_like(top, MASKED)

            def score(d, c):
                @pl.when(wanted(meta, ends, d))
                def _():
                    key = qkv[PAIRS + pair, pl.ds(pl.multiple_of(d * rows, rows), rows), :]
                    same = own_col == images_of(meta, image, d)
                    raw = jnp.where(same, dot_nt(query, key), MASKED)
                    scores[d] = raw
                    top[...] = jnp.maximum(top[...], jnp.max(raw, axis=1, keepdims=True))

                return c

            lax.fori_loop(0, 4, score, 0)
            total[...] = jnp.zeros_like(total)
            out_acc[...] = jnp.zeros_like(out_acc)
            peak = top[:, :1]

            def weigh(d, c):
                @pl.when(wanted(meta, ends, d))
                def _():
                    value = qkv[2 * PAIRS + pair, pl.ds(pl.multiple_of(d * rows, rows), rows), :]
                    shares = jnp.exp(scores[d] - peak)
                    total[...] += jnp.sum(shares, axis=1, keepdims=True)
                    out_acc[...] += dot_nn(shares.astype(BF16), value)

                return c

            lax.fori_loop(0, 4, weigh, 0)
            done.append(out_acc[...] / total[:, :1])
            lse_col[...] = jnp.where(lane == 2 * pair + half, peak + jnp.log(total[:, :1]), lse_col[...])
        att[:, pl.ds(pl.multiple_of(pair * LANES, LANES), LANES)] = jnp.where(lane < HEAD_DIM, done[0], done[1])
        return carry

    lax.fori_loop(0, PAIRS, pair_of_heads, 0)
    lse_row[...] = jnp.transpose(lse_col[...])[:8]
    branch = dot_nn(att[...].astype(BF16), full[:, 3 * D : 4 * D])
    centre = everything[0:rows, :].astype(F32) + branch
    middle[...] = centre
    unit, _ = unit_rows(centre)
    mixed[...] = (unit * norms[2:3] + norms[3:4]).astype(BF16)


def front_call(meta, image, pieces, shards):
    rows = pieces[0].shape[0] - INFO
    return once(
        front_kernel, (meta, image), tuple(map(far, (image, *pieces, *shards))),
        (
            ((3 * PAIRS, 4 * rows, LANES), BF16), ((D, WCOLS), BF16), ((rows, D), F32), ((rows, LANES), F32),
            ((8, rows), F32), ((rows, D), F32), ((rows, D), BF16),
        ),
        "front", 40,
        (((4 * rows, D), BF16), ((4, rows, rows), F32), ((rows, 1), F32), ((rows, 1), F32), ((rows, LANES), F32)),
    )


def gate_rows(mix, router_rows, choice):
    both = dot_nt(router_rows, mix)
    open_ = choice[:EXPERTS] > 0.5
    logits = jnp.where(choice[EXPERTS : EXPERTS + 1] < 0.5, both[:EXPERTS], both[EXPERTS : 2 * EXPERTS])
    logits = jnp.where(open_, logits, MASKED)
    raised = jnp.where(open_, jnp.exp(logits - jnp.max(logits, axis=0, keepdims=True)), 0.0)
    return raised / jnp.sum(raised, axis=0, keepdims=True)


def expert_kernel(
    local, plan, meta, m0, m1, m2, m3, g0, g1, g2, g3, spot_row, choice, given, up, down,
    mine, other, results, gates_out,
    gates, hidden, upstream, gate_slots, sum_up, sum_down,
):
    core = meta[1]
    low_up, low_down = up.at[0], down.at[0]
    expert = meta[0] + local
    rows = m0.shape[0]
    mixes = (m0, m1, m2, m3)
    grads = (g0, g1, g2, g3)

    if local == 0:
        router_rows = jnp.transpose(given[:, 4 * D :])
        for d in range(4):
            at = slice(d * rows, (d + 1) * rows)
            gates[:, at] = gate_rows(mixes[d][...], router_rows, choice[:, at])
        gates_out[...] = gates[...]
    else:
        gates[...] = given[...]
        gates_out[...] = jnp.zeros_like(gates_out)
    slot_at = lax.broadcasted_iota(jnp.int32, (CAP, rows), 0).astype(F32)
    lane = lax.broadcasted_iota(jnp.int32, (CAP, LANES), 1)
    for d in range(4):
        at = slice(d * rows, (d + 1) * rows)
        hit = slot_at == spot_row[local : local + 1, at]
        pick = jnp.where(hit, 1.0, 0.0).astype(BF16)
        gate = jnp.sum(jnp.where(hit, gates[pl.ds(expert, 1), at], 0.0), axis=1, keepdims=True)
        start = pl.multiple_of(plan[local * 8 + d], 16)
        hidden[pl.ds(start, CAP), :] = dot_nn(pick, mixes[d][...]).astype(BF16)
        upstream[pl.ds(start, CAP), :] = (gate * dot_nn(pick, grads[d][...])).astype(BF16)
        gate_slots[pl.ds(start, CAP), :] = jnp.broadcast_to(gate, (CAP, LANES))
    ending = pl.multiple_of(plan[local * 8 + 4], 16)
    hidden[pl.ds(ending, CAP), :] = jnp.zeros((CAP, D), BF16)
    upstream[pl.ds(ending, CAP), :] = jnp.zeros((CAP, D), BF16)
    gate_slots[pl.ds(ending, CAP), :] = jnp.zeros((CAP, LANES), F32)
    sum_up[...] = jnp.zeros_like(sum_up)
    sum_down[...] = jnp.zeros_like(sum_down)
    wide = 512

    def tile(i, carry):
        at = pl.ds(pl.multiple_of(i * CAP, CAP), CAP)
        x = hidden[at, :]
        g = upstream[at, :]
        x_t = jnp.transpose(x)
        g_t = jnp.transpose(g)
        made = jnp.zeros((CAP, D), F32)
        back = jnp.zeros((CAP, D), F32)
        for j in range(FFN // wide):
            cols = slice(j * wide, (j + 1) * wide)
            pre = dot_nn(x, low_up[:, cols])
            pull = dot_nt(g, low_down[cols, :])
            share = 0.5 + 0.5 * lax.erf(pre * 0.7071067811865476)
            active = (pre * share).astype(BF16)
            slope = share + pre * (0.3989422804014327 * jnp.exp(-0.5 * pre * pre))
            pre_grad = (slope * pull).astype(BF16)
            made = made + dot_nn(active, low_down[cols, :])
            back = back + dot_nt(pre_grad, low_up[:, cols])
            sum_up[:, cols] += dot_nn(x_t, pre_grad)
            sum_down[:, cols] += dot_nn(g_t, active)
        results[at, 0:D] = (gate_slots[at, 0:1] * made).astype(BF16)
        results[at, D : 2 * D] = back.astype(BF16)
        term = jnp.sum(g.astype(F32) * made, axis=1, keepdims=True)
        high = term.astype(BF16).astype(F32)
        ends = jnp.where(lane == expert, high, 0.0) + jnp.where(lane == 32 + expert, term - high, 0.0)
        results[at, 2 * D :] = ends.astype(BF16)
        return carry

    count = plan[local * 8 + 5]
    lax.fori_loop(0, count, tile, 0)
    results[pl.ds(pl.multiple_of(count * CAP, CAP), CAP), :] = jnp.zeros((CAP, 2 * D + LANES), BF16)
    half = FFN // 2
    quarter = D // 2

    for ref, side in ((mine, core), (other, 1 - core)):
        for b in range(2):
            cols = pl.ds(pl.multiple_of(side * half + b * D, LANES), D)
            ref[b * D : (b + 1) * D, :] = sum_down[:, cols].astype(BF16)
        held = sum_up[pl.ds(pl.multiple_of(side * quarter, 16), quarter), :].astype(BF16)
        for b in range(4):
            ref[half + b * quarter : half + (b + 1) * quarter, :] = held[:, b * D : (b + 1) * D]


def expert_call(local, plan, meta, mixes, grads, spot_row, choice, given, up, down):
    rows = mixes[0].shape[0]
    slots = 4 * CAP + CAP
    cols = 2 * D + LANES
    return pl.pallas_call(
        functools.partial(expert_kernel, local),
        grid=(1,),
        in_specs=[smem()] * 2
        + [whole((rows, D))] * 8
        + [
            whole((8, 4 * rows)),
            whole((EXPERTS + 8, 4 * rows)),
            whole(given.shape),
            pl.BlockSpec((1, D, FFN), lambda _: (local, 0, 0), pipeline_mode=pl.Buffered(1)),
            pl.BlockSpec((1, FFN, D), lambda _: (local, 0, 0), pipeline_mode=pl.Buffered(1)),
        ],
        out_specs=(whole((4 * D, D)), whole((4 * D, D)), whole((slots, cols)), whole((EXPERTS, 4 * rows))),
        out_shape=(
            jax.ShapeDtypeStruct((4 * D, D), BF16),
            jax.ShapeDtypeStruct((4 * D, D), BF16),
            jax.ShapeDtypeStruct((slots, cols), BF16),
            jax.ShapeDtypeStruct((EXPERTS, 4 * rows), F32),
        ),
        scratch_shapes=[
            pltpu.VMEM((EXPERTS, 4 * rows), F32),
            pltpu.VMEM((slots, D), BF16),
            pltpu.VMEM((slots, D), BF16),
            pltpu.VMEM((slots, LANES), F32),
            pltpu.VMEM((D, FFN), F32),
            pltpu.VMEM((D, FFN), F32),
        ],
        compiler_params=room(36),
        cost_estimate=LIGHT,
        name="experts",
    )(plan, meta, *mixes, *grads, spot_row, choice, given, far(up), far(down))


def combine_kernel(
    plan, m0, m1, m2, m3, spot_col, gates, full, res0, res1, res2, res3,
    b0, b1, b2, b3, x0, x1, x2, x3, router_out,
    stack,
):
    rows = m0.shape[0]
    lane = lax.broadcasted_iota(jnp.int32, (rows, LANES), 1)
    slot_along = lax.broadcasted_iota(jnp.int32, (rows, CAP), 1).astype(F32)
    routers = jnp.concatenate([full[:, 4 * D :], full[:, 4 * D :]], axis=1)
    total = jnp.zeros((D, 2 * LANES), F32)
    for d, (mix, back_out, mix_out) in enumerate(((m0, b0, x0), (m1, b1, x1), (m2, b2, x2), (m3, b3, x3))):
        at = slice(d * rows, (d + 1) * rows)
        info = spot_col[at, :]
        puts = []
        for e in range(4):
            start = pl.multiple_of(plan[e * 8 + d], 16)
            stack[e * CAP : (e + 1) * CAP, :] = (res0, res1, res2, res3)[e][pl.ds(start, CAP), :]
            puts.append(jnp.where(slot_along == info[:, e : e + 1], 1.0, 0.0).astype(BF16))
        got = dot_nn(jnp.concatenate(puts, axis=1), stack[...])
        mix_out[...] = got[:, :D].astype(BF16)
        ends = got[:, 2 * D :]
        held = jnp.where(lane < EXPERTS, ends + pltpu.roll(ends, LANES - 32, 1), 0.0)
        gate = jnp.transpose(
            jnp.concatenate([gates[:, at], jnp.zeros((LANES - EXPERTS, rows), F32)], axis=0)
        )
        change = held - jnp.sum(held, axis=1, keepdims=True) * gate
        task = info[:, 32:33]
        early = jnp.where((lane < EXPERTS) & (task < 0.5), change, 0.0)
        late = jnp.where(
            (lane >= EXPERTS) & (lane < 2 * EXPERTS) & (task > 0.5), pltpu.roll(change, EXPERTS, 1), 0.0
        )
        both = early + late
        high = both.astype(BF16)
        low = (both - high.astype(F32)).astype(BF16)
        parts = jnp.concatenate([high, low], axis=1)
        pulled = dot_nt(parts, routers)
        total = total + dot_tn(mix[...], parts)
        back_out[...] = (got[:, D : 2 * D] + pulled).astype(BF16)
    router_out[...] = total[:, :LANES] + total[:, LANES:]


def combine_call(plan, mixes, spot_col, gates, full, results):
    rows = mixes[0].shape[0]
    return once(
        combine_kernel, (plan,), (*mixes, spot_col, gates, full, *results),
        (((rows, D), BF16),) * 8 + (((D, LANES), F32),),
        "combine", 40, (((4 * CAP, 2 * D + LANES), BF16),),
    )


def turn_kernel(b0, r1, r2, r3, middle, grad, full, att, lse_row, middle_grad, sent, dots_col, output_grad, norm_two):
    rows = middle.shape[0]
    norms = norm_rows_of(full)
    mixed_grad = b0[...].astype(F32) + r1[...].astype(F32) + r2[...].astype(F32) + r3[...].astype(F32)
    unit, scale = unit_rows(middle[...])
    norm_two[...] = jnp.zeros_like(norm_two)
    norm_two[0:1, :] = jnp.sum(mixed_grad * unit, axis=0, keepdims=True)
    norm_two[1:2, :] = jnp.sum(mixed_grad, axis=0, keepdims=True)
    pulled = mixed_grad * norms[2:3]
    through = pulled - jnp.mean(pulled, axis=1, keepdims=True)
    through = scale * (through - unit * jnp.mean(pulled * unit, axis=1, keepdims=True))
    whole = through + grad[...].astype(F32)
    middle_grad[...] = whole
    branch = whole.astype(BF16)
    output_grad[...] = dot_tn(att[...].astype(BF16), branch).astype(BF16)
    pulled = dot_nt(branch, full[:, 3 * D : 4 * D]).astype(BF16)
    sent[0:rows, :] = pulled
    product = pulled.astype(F32) * att[...]
    high = product.astype(BF16)
    low = (product - high.astype(F32)).astype(BF16)
    heads = (
        lax.broadcasted_iota(jnp.int32, (D, LANES), 0) // HEAD_DIM
        == lax.broadcasted_iota(jnp.int32, (D, LANES), 1)
    )
    heads = heads.astype(F32).astype(BF16)
    dots = dot_nn(high, heads) + dot_nn(low, heads)
    dots_col[...] = dots
    lines = jnp.concatenate([lse_row[...], jnp.transpose(dots)[:8]], axis=0)
    high = lines.astype(BF16).astype(F32)
    table = jnp.concatenate([high, lines - high], axis=0).astype(BF16)
    half = EXTRA // 2
    sent[rows : rows + half, :] = table[:, :D]
    sent[rows + half : rows + EXTRA, :] = jnp.zeros((half, D), BF16)
    sent[rows + half : rows + EXTRA, : rows - D] = table[:, D:]


def turn_call(back, received, middle, grad, full, att, lse_row):
    rows = middle.shape[0]
    return once(
        turn_kernel, (), (back, *received, middle, grad, full, att, lse_row),
        (((rows, D), F32), ((rows + EXTRA, D), BF16), ((rows, LANES), F32), ((D, D), BF16), ((8, D), F32)),
        "turn", 24,
    )


def attention_back_kernel(
    meta, ends, image, qkv, s0, s1, s2, s3, lse_col, dots_col, own, full, middle_grad, output_grad, norm_two, routers,
    input_grad, to0, to1, to2, to3,
    lines, grads, packed, acc_one, acc_two, shared,
):
    rows = input_grad.shape[0]
    half_extra = EXTRA // 2
    for d, ref in enumerate((s0, s1, s2, s3)):
        grads[d] = ref[0:rows, :]
        table = jnp.concatenate(
            [ref[rows : rows + half_extra, :], ref[rows + half_extra : rows + EXTRA, : rows - D]], axis=1
        ).astype(F32)
        lines[d] = table[:16] + table[16:]
    own_row = images_of(meta, image, 0)
    own_col = jnp.transpose(jnp.broadcast_to(own_row, (LANES, rows)))[:, :1]
    lane = lax.broadcasted_iota(jnp.int32, (rows, LANES), 1)
    none = jnp.zeros((), BF16)
    here = slice(0, rows)

    def pair_of_heads(pair, carry):
        lanes = pl.ds(pl.multiple_of(pair * LANES, LANES), LANES)
        made = []
        for half in range(2):
            head = 2 * pair + half
            held = (lane < HEAD_DIM) if half == 0 else (lane >= HEAD_DIM)
            query = jnp.where(held, qkv[pair, here, :], none)
            pull = jnp.where(held, grads[0, :, lanes], none)
            log_total = jnp.sum(jnp.where(lane == head, lse_col[...], 0.0), axis=1, keepdims=True)
            dots = jnp.sum(jnp.where(lane == head, dots_col[...], 0.0), axis=1, keepdims=True)
            acc_one[...] = jnp.zeros_like(acc_one)

            def over_keys(d, c):
                @pl.when(wanted(meta, ends, d))
                def _():
                    at = pl.ds(pl.multiple_of(d * rows, rows), rows)
                    key = qkv[PAIRS + pair, at, :]
                    same = own_col == images_of(meta, image, d)
                    shares = jnp.where(same, jnp.exp(dot_nt(query, key) - log_total), 0.0)
                    change = dot_nt(pull, qkv[2 * PAIRS + pair, at, :]) - dots
                    acc_one[...] += dot_nn((shares * change).astype(BF16), key)

                return c

            lax.fori_loop(0, 4, over_keys, 0)
            made.append(acc_one[...])
        packed[:, lanes] = jnp.where(lane < HEAD_DIM, made[0], made[1]) * (HEAD_DIM ** (-0.5))
        made = []
        for half in range(2):
            head = 2 * pair + half
            held = (lane < HEAD_DIM) if half == 0 else (lane >= HEAD_DIM)
            key = jnp.where(held, qkv[PAIRS + pair, here, :], none)
            value = jnp.where(held, qkv[2 * PAIRS + pair, here, :], none)
            acc_one[...] = jnp.zeros_like(acc_one)
            acc_two[...] = jnp.zeros_like(acc_two)

            def over_queries(d, c):
                @pl.when(wanted(meta, ends, d))
                def _():
                    at = pl.ds(pl.multiple_of(d * rows, rows), rows)
                    query = qkv[pair, at, :]
                    pull = grads[d, :, lanes]
                    same = own_col == images_of(meta, image, d)
                    log_total = lines[d, pl.ds(head, 1), :]
                    dots = lines[d, pl.ds(8 + head, 1), :]
                    shares = jnp.where(same, jnp.exp(dot_nt(key, query) - log_total), 0.0)
                    change = dot_nt(value, pull) - dots
                    acc_two[...] += dot_nn(shares.astype(BF16), pull)
                    acc_one[...] += dot_nn((shares * change).astype(BF16), query)

                return c

            lax.fori_loop(0, 4, over_queries, 0)
            made.append((acc_one[...], acc_two[...]))
        shift = pl.ds(pl.multiple_of(D + pair * LANES, LANES), LANES)
        packed[:, shift] = jnp.where(lane < HEAD_DIM, made[0][0], made[1][0])
        shift = pl.ds(pl.multiple_of(2 * D + pair * LANES, LANES), LANES)
        packed[:, shift] = jnp.where(lane < HEAD_DIM, made[0][1], made[1][1])
        return carry

    lax.fori_loop(0, PAIRS, pair_of_heads, 0)
    norms = norm_rows_of(full)
    unit, scale = unit_rows(own[0:rows, :].astype(F32))
    normed = (unit * norms[0:1] + norms[1:2]).astype(BF16)
    normed_grad = jnp.zeros((rows, D), F32)
    for third in range(3):
        part = packed[:, third * D : (third + 1) * D].astype(BF16)
        normed_grad = normed_grad + dot_nt(part, full[:, third * D : (third + 1) * D])
        weight_grad = dot_tn(normed, part).astype(BF16)
        for j in range(PAIRS):
            block = third * PAIRS + j
            shared[meta[4 + block // 4], :, block % 4 * LANES : (block % 4 + 1) * LANES] = weight_grad[
                :, j * LANES : (j + 1) * LANES
            ]
    pulled = normed_grad * norms[0:1]
    through = pulled - jnp.mean(pulled, axis=1, keepdims=True)
    through = scale * (through - unit * jnp.mean(pulled * unit, axis=1, keepdims=True))
    input_grad[...] = through + middle_grad[...]
    for j in range(PAIRS):
        block = 3 * PAIRS + j
        shared[meta[4 + block // 4], :, block % 4 * LANES : (block % 4 + 1) * LANES] = output_grad[
            :, j * LANES : (j + 1) * LANES
        ]
    lines_norm = jnp.concatenate(
        [
            jnp.zeros((NORM_AT, D), F32),
            jnp.sum(normed_grad * unit, axis=0, keepdims=True),
            jnp.sum(normed_grad, axis=0, keepdims=True),
            norm_two[0:2, :],
            jnp.zeros((LANES - NORM_AT - 4, D), F32),
        ],
        axis=0,
    )
    small = routers[...] + jnp.transpose(lines_norm)
    shared[meta[7], :, 0:LANES] = small.astype(BF16)
    shared[meta[7], :, LANES:] = jnp.zeros((D, 3 * LANES), BF16)
    part = D // 8
    for d, ref in enumerate((to0, to1, to2, to3)):
        for owner in range(8):
            at = pl.ds(pl.multiple_of(meta[28 + owner], 16), part)
            ref[at, :] = shared[d, owner * part : (owner + 1) * part, :]


def attention_back_call(meta, image, qkv, sent, lse_col, dots_col, own, full, middle_grad, output_grad, norm_two, routers):
    rows = middle_grad.shape[0]
    return once(
        attention_back_kernel, (meta, image),
        (image, qkv, *sent, lse_col, dots_col, own, full, middle_grad, output_grad, norm_two, routers),
        (((rows, D), F32),) + (((D, 4 * LANES), BF16),) * 4,
        "attention_back", 40,
        (
            ((4, 16, rows), F32), ((4, rows, D), BF16), ((rows, 3 * D), F32), ((rows, LANES), F32),
            ((rows, LANES), F32), ((4, D, 4 * LANES), BF16),
        ),
    )


def adamw(weight, moment, second, gradient, step_rate):
    moment = BETA_FIRST * moment + (1.0 - BETA_FIRST) * gradient
    second = BETA_SECOND * second + (1.0 - BETA_SECOND) * gradient * gradient
    spread = jnp.sqrt(second * (1.0 / (1.0 - BETA_SECOND**STEP))) + ADAM_EPS
    change = moment * (step_rate / (1.0 - BETA_FIRST**STEP)) / spread
    weight = weight * (1.0 - step_rate * DECAY) - change
    return (weight, moment, second)


def adam_kernel(meta, ready, passed, w1, m1, v1, w2, m2, v2, *rest):
    outs = rest[-6:]
    step = pl.program_id(0)
    half_steps = pl.num_programs(0) // 2
    mine = (step // half_steps) == meta[1]
    inner = step % half_steps
    up_rows, down_rows = w1.shape[1], w2.shape[1]
    half = FFN // 2
    quarter = D // 2

    def pick(rows_at, lanes_at):
        return jnp.where(mine, ready[rows_at, lanes_at], passed[rows_at, lanes_at]).astype(F32)

    per = D // down_rows
    down = pick(
        pl.ds(pl.multiple_of(inner // per * D, D), D), pl.ds(pl.multiple_of(inner % per * down_rows, LANES), down_rows)
    )
    up = jnp.concatenate(
        [
            pick(pl.ds(pl.multiple_of(half + b * quarter + inner * up_rows, 16), up_rows), slice(0, D))
            for b in range(4)
        ],
        axis=1,
    )
    for k, value in enumerate(adamw(w1[0], m1[0], v1[0], up, RATE_EXPAND)):
        outs[k][0] = value
    for k, value in enumerate(adamw(w2[0], m2[0], v2[0], jnp.transpose(down), RATE_REDUCE)):
        outs[3 + k][0] = value


def adam_call(expert, meta, ready, passed, states, previous):
    steps = 4
    up = pl.BlockSpec((1, D // steps, FFN), lambda i, *_: (expert, i, 0))
    down = pl.BlockSpec((1, FFN // steps, D), lambda i, *_: (expert, i, 0))
    specs = [whole(ready.shape)] * 2 + [up] * 3 + [down] * 3
    args = [ready, passed, *map(far, states)]
    aliases = {}
    if previous is not None:
        for k, value in enumerate(previous):
            aliases[1 + len(args)] = k
            args.append(value)
            specs.append(pl.BlockSpec(memory_space=pl.ANY))
    return pl.pallas_call(
        adam_kernel,
        grid_spec=pltpu.PrefetchScalarGridSpec(
            num_scalar_prefetch=1,
            grid=(steps,),
            in_specs=specs,
            out_specs=(up,) * 3 + (down,) * 3,
        ),
        out_shape=tuple(jax.ShapeDtypeStruct(s.shape, F32) for s in states),
        input_output_aliases=aliases,
        compiler_params=room(28),
        cost_estimate=LIGHT,
        name="adam",
    )(meta, *args)


def fold_kernel(a, b, c, d, kept, gone):
    rows = kept.shape[0]
    for ref, at in ((kept, slice(0, rows)), (gone, slice(rows, 2 * rows))):
        ref[...] = (
            a[at, :].astype(F32) + b[at, :].astype(F32) + c[at, :].astype(F32) + d[at, :].astype(F32)
        ).astype(BF16)


def fold_call(parts):
    rows, cols = parts[0].shape
    return once(fold_kernel, (), parts, (((rows // 2, cols), BF16),) * 2, "fold", 8)


def split_kernel(kept, came, *outs):
    for k, ref in enumerate(outs):
        at = slice(k * ref.shape[0], (k + 1) * ref.shape[0])
        ref[...] = (kept[at, :].astype(F32) + came[at, :].astype(F32)).astype(BF16)


def split_call(kept, came):
    rows, cols = kept.shape
    return once(split_kernel, (), (kept, came), (((rows // 4, cols), BF16),) * 4, "split", 8)


def settle_kernel(meta, *refs):
    pieces, states, outs, (buffer, square) = refs[:4], refs[4:16], refs[16:28], refs[28:]
    rows = pieces[0].shape[0]
    for d in range(4):
        buffer[meta[4 + d]] = pieces[d][...].astype(F32)
    square[...] = jnp.zeros_like(square)
    square[0:rows, :] = buffer[3, :, 0:LANES]
    turned = jnp.transpose(square[...])
    attend_sum = jnp.concatenate([buffer[0], buffer[1], buffer[2, :, 0:LANES]], axis=1)
    sums = (turned[NORM_AT : NORM_AT + 4, :rows], attend_sum, buffer[2, :, LANES:])
    for k, (total, rate) in enumerate(zip(sums, (RATE_NORM, RATE_ATTEND, RATE_OUTPUT))):
        held = [ref[...] for ref in states[3 * k : 3 * k + 3]]
        for ref, value in zip(outs[3 * k : 3 * k + 3], adamw(*held, total, rate)):
            ref[...] = value
    for t in range(TASKS):
        held = [ref[t] for ref in states[9:12]]
        total = turned[t * EXPERTS : (t + 1) * EXPERTS, :rows]
        for ref, value in zip(outs[9:12], adamw(*held, total, RATE_ROUTER)):
            ref[t] = value


def settle_call(meta, pieces, states):
    rows, cols = pieces[0].shape
    return once(
        settle_kernel, (meta,), (*pieces, *map(far, states)), tuple((s.shape, F32) for s in states),
        "settle", 12, (((4, rows, cols), F32), ((LANES, LANES), F32)),
    )


def swap_expert(value, d):
    return lax.ppermute(value, "expert", [(i, i ^ d) for i in range(4)])


def swap_tall(value, d):
    return lax.ppermute(value, "dp", [(2 * a + c, 2 * (a ^ d) + c) for a in range(4) for c in range(2)])


def swap_core(value):
    return lax.ppermute(value, "dp", [(i, i ^ 1) for i in range(8)])


def send_tall(value, hops):
    return lax.ppermute(value, "dp", [(2 * a + c, 2 * b + c) for a, b in hops for c in range(2)])


def tie(value, *others):
    flat, tree = jax.tree.flatten((value, others))
    return jax.tree.unflatten(tree, lax.optimization_barrier(flat))[0]


def fast_body(
    patches, out_grad, image_of, task_of, routes,
    norm_weight, norm_moment, norm_second,
    attend_weight, attend_moment, attend_second,
    output_weight, output_moment, output_second,
    router_weight, router_moment, router_second,
    expand_weight, expand_moment, expand_second,
    reduce_weight, reduce_moment, reduce_second,
):
    member = lax.axis_index("expert")
    place = lax.axis_index("dp")
    rows = patches.shape[1]
    count = expand_weight.shape[0]
    table = place_table(count, attend_weight.shape[0])
    meta = lax.dynamic_index_in_dim(jnp.asarray(table), place * 4 + member, 0, False)
    inner = (place >= 2) & (place < 6)
    image = image_of

    own, shard = pack_call(patches, routes, task_of, attend_weight, output_weight, router_weight, norm_weight)
    shards = [shard] + [swap_tall(shard, d) for d in (1, 2, 3)]
    pieces = [own] + [swap_expert(own, d) for d in (1, 2, 3)]
    near = join_call(shards)
    shards = [near, swap_core(near)]
    grad = out_grad[0]
    grads = [grad] + [swap_expert(tie(grad, *pieces[1:]), d) for d in (1, 2, 3)]

    qkv, full, att, lse_col, lse_row, middle, mixed = front_call(meta, image, pieces, shards)
    mixes = [mixed] + [swap_expert(mixed, d) for d in (1, 2, 3)]
    spot_row, choice, spot_col, plan = route_call(meta, pieces, count)

    up_low = tie(expand_weight, mixed).astype(BF16)
    down_low = tie(reduce_weight, mixed).astype(BF16)

    def first_hop(value):
        return send_tall(value, ((0, 1), (3, 2)))

    def second_hop(value):
        return send_tall(value, ((1, 2), (2, 1)))

    def third_hop(value):
        return send_tall(value, ((1, 0), (2, 3)))

    def settled(value, came):
        return jnp.where(inner, value, came)

    def expert(local, given):
        return expert_call(local, plan, meta, mixes, grads, spot_row, choice, given, up_low, down_low)

    mine0, other0, res0, gates = expert(0, full)
    half0 = mine0 + swap_core(other0)
    came_a0 = first_hop(half0)
    mine1, other1, res1, _ = expert(1, tie(gates, half0))
    got1 = swap_core(other1)
    mine2, other2, res2, _ = expert(2, tie(gates, mine1))
    got2 = swap_core(other2)
    pair0 = half0 + tie(came_a0, mine2)
    came_b0 = second_hop(pair0)
    half1 = mine1 + tie(got1, pair0)
    came_a1 = first_hop(half1)
    mine3, other3, res3, _ = expert(3, tie(gates, half1, pair0))
    got3 = swap_core(other3)
    half2 = mine2 + tie(got2, mine3)
    came_a2 = first_hop(half2)
    *outs, routers = combine_call(plan, mixes, spot_col, tie(gates, half2), full, (res0, res1, res2, res3))
    back, mix = outs[:4], outs[4:]
    returned = [swap_expert(back[d], d) for d in (1, 2, 3)]
    pair1 = half1 + tie(came_a1, routers)
    came_b1 = second_hop(pair1)
    whole0 = pair0 + tie(came_b0, routers)
    came_c0 = third_hop(whole0)
    half3 = mine3 + tie(got3, pair1, whole0)
    pair2 = half2 + tie(came_a2, half3, *returned)
    came_b2 = second_hop(pair2)
    came_a3 = first_hop(tie(half3, pair2))
    middle_grad, sent, dots_col, output_grad, norm_two = turn_call(
        tie(back[0], half3, pair2), returned, middle, grad, full, att, lse_row
    )
    sents = [sent] + [swap_expert(sent, d) for d in (1, 2, 3)]
    whole1 = pair1 + tie(came_b1, norm_two)
    ready0 = settled(whole0, tie(came_c0, norm_two))
    passed0 = swap_core(ready0)
    states = (expand_weight, expand_moment, expand_second, reduce_weight, reduce_moment, reduce_second)
    news = adam_call(0, meta, tie(ready0, pair2, whole1), passed0, states, None)
    came_c1 = third_hop(tie(whole1, news[0], *sents[1:]))
    pair3 = half3 + tie(came_a3, news[0], *sents[1:])
    came_b3 = second_hop(pair3)
    whole2 = pair2 + tie(came_b2, news[0])
    came_c2 = third_hop(whole2)
    input_grad, *shared = attention_back_call(
        meta, image, qkv, sents, tie(lse_col, pair3, whole2), dots_col, own, full, middle_grad,
        output_grad, norm_two, routers,
    )
    shared = [shared[0]] + [swap_expert(shared[d], d) for d in (1, 2, 3)]
    whole3 = pair3 + tie(came_b3, input_grad)
    came_c3 = third_hop(whole3)
    ready2 = settled(whole2, tie(came_c2, input_grad))
    ready1 = settled(whole1, tie(came_c1, input_grad))
    passed1 = tie(swap_core(ready1), whole3, ready2)
    news = adam_call(1, meta, ready1, passed1, states, news)
    kept, gone = fold_call([tie(shared[0], news[0])] + shared[1:])
    gone = swap_core(gone)
    ready3 = settled(whole3, tie(came_c3, kept))
    passed2 = tie(swap_core(tie(ready2, news[0])), ready3)
    piece, *away = split_call(kept, tie(gone, ready3))
    away = [swap_tall(away[d - 1], d) for d in (1, 2, 3)]
    news = adam_call(2, meta, tie(ready2, piece), passed2, states, news)
    piece = tie(piece, news[0]) + away[0] + away[1] + away[2]
    quarters = [piece] + [swap_expert(piece, d) for d in (1, 2, 3)]
    parts = [swap_expert(tie(mix[d], quarters[3]), d) for d in (1, 2, 3)]
    passed3 = swap_core(tie(ready3, kept))
    news = adam_call(3, meta, tie(ready3, piece), passed3, states, news)
    block_out = middle + tie(mix[0], news[0]).astype(F32)
    for part in parts:
        block_out = block_out + part.astype(F32)
    block_out = block_out.astype(BF16)[None]
    small = settle_call(
        meta, [tie(quarters[0], news[0])] + quarters[1:],
        (
            norm_weight, norm_moment, norm_second, attend_weight, attend_moment, attend_second,
            output_weight, output_moment, output_second, router_weight, router_moment, router_second,
        ),
    )
    return (block_out, input_grad[None], *small, *news)


def gelu_exact(values):
    return 0.5 * values * (1.0 + lax.erf(values * 0.7071067811865476))


def norm_rows(values, gain_row, offset):
    average = jnp.mean(values, axis=-1, keepdims=True)
    centred = values - average
    spread = jnp.mean(centred * centred, axis=-1, keepdims=True)
    return centred * lax.rsqrt(spread + NORM_EPS) * gain_row + offset


def body(
    patches,
    out_grad,
    image_of,
    task_of,
    routes,
    norm_weight,
    norm_moment,
    norm_second,
    attend_weight,
    attend_moment,
    attend_second,
    output_weight,
    output_moment,
    output_second,
    router_weight,
    router_moment,
    router_second,
    expand_weight,
    expand_moment,
    expand_second,
    reduce_weight,
    reduce_moment,
    reduce_second,
):
    precise = lax.Precision.HIGHEST
    member = lax.axis_index("expert")
    tokens = patches.shape[1]
    group_rows = image_of.shape[1]
    key_rows = min(512, group_rows)
    score_scale = HEAD_DIM ** (-0.5)
    norm_full, attend_full, output_full, router_full = (
        lax.all_gather(norm_weight.astype(jnp.bfloat16), "dp", axis=1, tiled=True),
        lax.all_gather(attend_weight.astype(jnp.bfloat16), "dp", axis=0, tiled=True),
        lax.all_gather(output_weight.astype(jnp.bfloat16), "dp", axis=0, tiled=True),
        lax.all_gather(router_weight.astype(jnp.bfloat16), "dp", axis=2, tiled=True),
    )
    norm_values = norm_full.astype(jnp.float32)
    router_values = router_full.astype(jnp.float32)
    expand_low = expand_weight.astype(jnp.bfloat16)
    reduce_low = reduce_weight.astype(jnp.bfloat16)
    inputs = patches[0].astype(jnp.float32)
    image_row = image_of[0]
    my_image = lax.dynamic_slice_in_dim(image_row, member * tokens, tokens)
    task_row = task_of[0]
    route_rows = routes[0]
    first_image = my_image[0]
    last_image = my_image[tokens - 1]
    first_key = jnp.sum((image_row < first_image).astype(jnp.int32))
    last_key = jnp.sum((image_row <= last_image).astype(jnp.int32)) - 1
    first_block = first_key // key_rows
    end_block = last_key // key_rows + 1
    normed_one, first_back = jax.vjp(norm_rows, inputs, norm_values[0], norm_values[1])
    normed_low = normed_one.astype(jnp.bfloat16)
    packed = jnp.dot(normed_low, attend_full, preferred_element_type=jnp.float32).astype(
        jnp.bfloat16
    )
    queries = packed[:, :D].reshape(tokens, HEADS, HEAD_DIM)
    key_value = packed[:, D:]
    key_value_all = lax.all_gather(key_value, "expert", axis=0, tiled=True)
    keys_all = key_value_all[:, :D].reshape(group_rows, HEADS, HEAD_DIM)
    values_all = key_value_all[:, D:].reshape(group_rows, HEADS, HEAD_DIM)

    def scores_of(query_part, key_part, same_image):
        raw = (
            jnp.einsum("thd,khd->htk", query_part, key_part, preferred_element_type=jnp.float32)
            * score_scale
        )
        return jnp.where(same_image[None], raw, MASKED)

    def block_at(block_index):
        first_row = block_index * key_rows
        key_part = lax.dynamic_slice_in_dim(keys_all, first_row, key_rows, 0)
        value_part = lax.dynamic_slice_in_dim(values_all, first_row, key_rows, 0)
        same_image = (
            my_image[:, None]
            == lax.dynamic_slice_in_dim(image_row, first_row, key_rows, 0)[None, :]
        )
        return (key_part, value_part, same_image)

    def max_step(block_index, state_in):
        highest, totals = state_in
        key_part, value_part, same_image = block_at(block_index)
        scores = scores_of(queries, key_part, same_image)
        raised = jnp.maximum(highest, jnp.max(scores, axis=-1))
        shares = jnp.where(same_image[None], jnp.exp(scores - raised[..., None]), 0.0)
        return (raised, totals * jnp.exp(highest - raised) + jnp.sum(shares, axis=-1))

    start_max = jnp.full((HEADS, tokens), MASKED, jnp.float32)
    highest, totals = lax.fori_loop(
        first_block, end_block, max_step, (start_max, jnp.zeros((HEADS, tokens), jnp.float32))
    )
    log_total = highest + jnp.log(totals)

    def value_step(block_index, accum):
        key_part, value_part, same_image = block_at(block_index)
        scores = scores_of(queries, key_part, same_image)
        soft_part = jnp.where(same_image[None], jnp.exp(scores - log_total[..., None]), 0.0).astype(
            jnp.bfloat16
        )
        return accum + jnp.einsum(
            "htk,khd->thd", soft_part, value_part, preferred_element_type=jnp.float32
        )

    attended = lax.fori_loop(
        first_block, end_block, value_step, jnp.zeros((tokens, HEADS, HEAD_DIM), jnp.float32)
    )
    attended_low = attended.reshape(tokens, D).astype(jnp.bfloat16)
    branch = jnp.dot(attended_low, output_full, preferred_element_type=jnp.float32)
    middle = inputs + branch
    normed_two, second_back = jax.vjp(norm_rows, middle, norm_values[2], norm_values[3])
    mixed_low = normed_two.astype(jnp.bfloat16)
    task_hot = (task_row[:, None] == jnp.arange(TASKS, dtype=jnp.int32)[None, :]).astype(
        jnp.float32
    )
    route_hot = (
        route_rows[:, :, None] == jnp.arange(EXPERTS, dtype=jnp.int32)[None, None, :]
    ).astype(jnp.float32)

    def gating(hidden, router):
        logits = jnp.einsum("td,ced->tce", hidden, router, precision=precise)
        task_logits = jnp.einsum("tc,tce->te", task_hot, logits, precision=precise)
        chosen = jnp.einsum("te,tke->tk", task_logits, route_hot, precision=precise)
        peak = jnp.max(chosen, axis=-1, keepdims=True)
        raised = jnp.exp(chosen - peak)
        return raised / jnp.sum(raised, axis=-1, keepdims=True)

    gate_values, gate_back = jax.vjp(gating, mixed_low.astype(jnp.float32), router_values)
    pair_expert = route_rows.reshape(-1)
    pair_hot = (pair_expert[:, None] == jnp.arange(EXPERTS, dtype=jnp.int32)[None, :]).astype(
        jnp.int32
    )
    slot_index = jnp.sum((jnp.cumsum(pair_hot, axis=0) - pair_hot) * pair_hot, axis=1)
    flat_slot = pair_expert * CAP + slot_index

    def scatter_pairs(pair_values):
        return (
            jnp.zeros((EXPERTS * CAP, D), pair_values.dtype)
            .at[flat_slot]
            .set(pair_values)
            .reshape(EXPERTS, CAP, D)
        )

    def gather_pairs(buffer):
        return (
            buffer.reshape(EXPERTS * CAP, D)[flat_slot].astype(jnp.float32).reshape(tokens, TOP, D)
        )

    received = lax.all_to_all(
        scatter_pairs(jnp.repeat(mixed_low, TOP, axis=0)),
        "expert",
        split_axis=0,
        concat_axis=1,
        tiled=True,
    )
    hidden_pre = jnp.einsum(
        "ecd,edh->ech", received, expand_low, preferred_element_type=jnp.float32
    )
    active, gelu_back = jax.vjp(gelu_exact, hidden_pre)
    active_low = active.astype(jnp.bfloat16)
    expert_out = jnp.einsum(
        "ech,ehd->ecd", active_low, reduce_low, preferred_element_type=jnp.float32
    ).astype(jnp.bfloat16)
    returned = lax.all_to_all(expert_out, "expert", split_axis=1, concat_axis=0, tiled=True)
    pair_out = gather_pairs(returned)
    expert_mix = jnp.einsum("tk,tkd->td", gate_values, pair_out, precision=precise)
    block_out = (middle + expert_mix).astype(jnp.bfloat16)[None]
    upstream = out_grad[0].astype(jnp.float32)
    gate_grad = jnp.sum(upstream[:, None, :] * pair_out, axis=-1)
    pair_grad = (
        (gate_values[:, :, None] * upstream[:, None, :])
        .astype(jnp.bfloat16)
        .reshape(tokens * TOP, D)
    )
    grad_in = lax.all_to_all(
        scatter_pairs(pair_grad), "expert", split_axis=0, concat_axis=1, tiled=True
    )
    reduce_grad = jnp.einsum(
        "ech,ecd->ehd", active_low, grad_in, preferred_element_type=jnp.float32
    )
    active_grad = jnp.einsum(
        "ecd,ehd->ech", grad_in, reduce_low, preferred_element_type=jnp.float32
    )
    pre_grad = gelu_back(active_grad)[0].astype(jnp.bfloat16)
    expand_grad = jnp.einsum("ecd,ech->edh", received, pre_grad, preferred_element_type=jnp.float32)
    back_rows = jnp.einsum(
        "ech,edh->ecd", pre_grad, expand_low, preferred_element_type=jnp.float32
    ).astype(jnp.bfloat16)
    expand_sum, reduce_sum = (
        lax.psum(expand_grad.astype(jnp.bfloat16), "dp").astype(jnp.float32),
        lax.psum(reduce_grad.astype(jnp.bfloat16), "dp").astype(jnp.float32),
    )
    came_back = lax.all_to_all(back_rows, "expert", split_axis=1, concat_axis=0, tiled=True)
    routed_grad = jnp.sum(gather_pairs(came_back), axis=1)
    hidden_gate_grad, router_grad = gate_back(gate_grad)
    middle_part, gain_two, offset_two = second_back(routed_grad + hidden_gate_grad)
    middle_grad = middle_part + upstream
    branch_grad = middle_grad.astype(jnp.bfloat16)
    output_grad = jnp.einsum(
        "td,te->de", attended_low, branch_grad, preferred_element_type=jnp.float32
    )
    attended_grad = (
        jnp.einsum("te,de->td", branch_grad, output_full, preferred_element_type=jnp.float32)
        .astype(jnp.bfloat16)
        .reshape(tokens, HEADS, HEAD_DIM)
    )
    row_dots = jnp.einsum(
        "thd,thd->ht", attended_grad.astype(jnp.float32), attended, precision=precise
    )

    def score_grad(query_part, key_part, value_part, grad_part, same_image, log_part, dots_part):
        scores = scores_of(query_part, key_part, same_image)
        soft_part = jnp.where(same_image[None], jnp.exp(scores - log_part[..., None]), 0.0)
        soft_grad = jnp.einsum(
            "thd,khd->htk", grad_part, value_part, preferred_element_type=jnp.float32
        )
        return (soft_part, (soft_part * (soft_grad - dots_part[..., None])).astype(jnp.bfloat16))

    def pair_step(block_index, state_in):
        query_acc, terms_acc = state_in
        key_part, value_part, same_image = block_at(block_index)
        soft_part, dscore = score_grad(
            queries, key_part, value_part, attended_grad, same_image, log_total, row_dots
        )
        query_acc = query_acc + jnp.einsum(
            "htk,khd->thd", dscore, key_part, preferred_element_type=jnp.float32
        )
        key_term = (
            jnp.einsum("htk,thd->khd", dscore, queries, preferred_element_type=jnp.float32)
            * score_scale
        )
        value_term = jnp.einsum(
            "htk,thd->khd",
            soft_part.astype(jnp.bfloat16),
            attended_grad,
            preferred_element_type=jnp.float32,
        )
        terms = jnp.concatenate(
            [key_term.reshape(key_rows, D), value_term.reshape(key_rows, D)], axis=1
        )
        terms_acc = lax.dynamic_update_slice_in_dim(terms_acc, terms, block_index * key_rows, 0)
        return (query_acc, terms_acc)

    query_acc, key_value_terms = lax.fori_loop(
        first_block,
        end_block,
        pair_step,
        (
            jnp.zeros((tokens, HEADS, HEAD_DIM), jnp.float32),
            jnp.zeros((group_rows, 2 * D), jnp.float32),
        ),
    )
    key_value_grad = lax.psum_scatter(
        key_value_terms.astype(jnp.bfloat16), "expert", scatter_dimension=0, tiled=True
    ).astype(jnp.float32)
    query_grad = (query_acc * score_scale).reshape(tokens, D)
    packed_grad = jnp.concatenate([query_grad, key_value_grad], axis=1).astype(jnp.bfloat16)
    attend_grad = jnp.einsum(
        "td,te->de", normed_low, packed_grad, preferred_element_type=jnp.float32
    )
    normed_grad = jnp.einsum(
        "te,de->td", packed_grad, attend_full, preferred_element_type=jnp.float32
    )
    input_part, gain_one, offset_one = first_back(normed_grad)
    input_grad = (middle_grad + input_part)[None]
    norm_grad = jnp.stack([gain_one, offset_one, gain_two, offset_two])
    shared = (norm_grad, attend_grad, output_grad, router_grad)
    summed = (
        lax.psum(shared[0].astype(jnp.bfloat16), "expert").astype(jnp.float32),
        lax.psum(shared[1].astype(jnp.bfloat16), "expert").astype(jnp.float32),
        lax.psum(shared[2].astype(jnp.bfloat16), "expert").astype(jnp.float32),
        lax.psum(shared[3].astype(jnp.bfloat16), "expert").astype(jnp.float32),
    )
    norm_sum, attend_sum, output_sum, router_sum = (
        lax.psum_scatter(
            summed[0].astype(jnp.bfloat16), "dp", scatter_dimension=1, tiled=True
        ).astype(jnp.float32),
        lax.psum_scatter(
            summed[1].astype(jnp.bfloat16), "dp", scatter_dimension=0, tiled=True
        ).astype(jnp.float32),
        lax.psum_scatter(
            summed[2].astype(jnp.bfloat16), "dp", scatter_dimension=0, tiled=True
        ).astype(jnp.float32),
        lax.psum_scatter(
            summed[3].astype(jnp.bfloat16), "dp", scatter_dimension=2, tiled=True
        ).astype(jnp.float32),
    )
    norm_new = adamw(norm_weight, norm_moment, norm_second, norm_sum, RATE_NORM)
    attend_new = adamw(attend_weight, attend_moment, attend_second, attend_sum, RATE_ATTEND)
    output_new = adamw(output_weight, output_moment, output_second, output_sum, RATE_OUTPUT)
    router_new = adamw(router_weight, router_moment, router_second, router_sum, RATE_ROUTER)
    expand_new = adamw(expand_weight, expand_moment, expand_second, expand_sum, RATE_EXPAND)
    reduce_new = adamw(reduce_weight, reduce_moment, reduce_second, reduce_sum, RATE_REDUCE)
    return (
        block_out,
        input_grad,
        norm_new[0],
        norm_new[1],
        norm_new[2],
        attend_new[0],
        attend_new[1],
        attend_new[2],
        output_new[0],
        output_new[1],
        output_new[2],
        router_new[0],
        router_new[1],
        router_new[2],
        expand_new[0],
        expand_new[1],
        expand_new[2],
        reduce_new[0],
        reduce_new[1],
        reduce_new[2],
    )


def solution(mesh):
    placed = (
        P("dp", "expert", None),
        P("dp", "expert", None),
        P("dp", None),
        P("dp", "expert"),
        P("dp", "expert", None),
        P(None, "dp"),
        P(None, "dp"),
        P(None, "dp"),
        P("dp", None),
        P("dp", None),
        P("dp", None),
        P("dp", None),
        P("dp", None),
        P("dp", None),
        P(None, None, "dp"),
        P(None, None, "dp"),
        P(None, None, "dp"),
        P("expert", None, None),
        P("expert", None, None),
        P("expert", None, None),
        P("expert", None, None),
        P("expert", None, None),
        P("expert", None, None),
    )
    fits = mesh.shape["dp"] == 8 and mesh.shape["expert"] == 4
    return jax.shard_map(
        fast_body if fits else body,
        mesh=mesh,
        in_specs=placed,
        out_specs=(
            P("dp", "expert", None),
            P("dp", "expert", None),
            P(None, "dp"),
            P(None, "dp"),
            P(None, "dp"),
            P("dp", None),
            P("dp", None),
            P("dp", None),
            P("dp", None),
            P("dp", None),
            P("dp", None),
            P(None, None, "dp"),
            P(None, None, "dp"),
            P(None, None, "dp"),
            P("expert", None, None),
            P("expert", None, None),
            P("expert", None, None),
            P("expert", None, None),
            P("expert", None, None),
            P("expert", None, None),
        ),
        check_vma=False,
    )
```

```python
import functools

import jax
import jax.numpy as jnp
import numpy as np
from jax import lax
from jax.experimental import pallas as pl
from jax.experimental.pallas import tpu as pltpu
from jax.sharding import PartitionSpec as P

D = 384
HEADS = 6
HEAD_DIM = 64
FFN = 1536
EXPERTS = 16
TASKS = 2
TOP = 4
STEP = 10
CAP = 256
PAIRS = HEADS // 2
LANES = 128
WCOLS = 4 * D + LANES
INFO = 16
NORM_AT = 2 * EXPERTS
EXTRA = 64

NORM_EPS = 1e-06
ADAM_EPS = 1e-08
BETA_FIRST = 0.9
BETA_SECOND = 0.999
DECAY = 0.05
RATE_NORM = 0.5
RATE_ATTEND = 0.2
RATE_OUTPUT = 0.7
RATE_ROUTER = 0.06
RATE_EXPAND = 0.13
RATE_REDUCE = 0.25
MASKED = -1e30
F32 = jnp.float32
BF16 = jnp.bfloat16
LIGHT = pl.CostEstimate(flops=1, transcendentals=0, bytes_accessed=1)


def dot_nn(a, b):
    return lax.dot_general(a, b, (((1,), (0,)), ((), ())), preferred_element_type=F32)


def dot_nt(a, b):
    return lax.dot_general(a, b, (((1,), (1,)), ((), ())), preferred_element_type=F32)


def dot_tn(a, b):
    return lax.dot_general(a, b, (((0,), (0,)), ((), ())), preferred_element_type=F32)


def unit_rows(values):
    average = jnp.mean(values, axis=-1, keepdims=True)
    centred = values - average
    spread = jnp.mean(centred * centred, axis=-1, keepdims=True)
    scale = lax.rsqrt(spread + NORM_EPS)
    return centred * scale, scale


def eye(n):
    rows = lax.broadcasted_iota(jnp.int32, (n, n), 0)
    cols = lax.broadcasted_iota(jnp.int32, (n, n), 1)
    return (rows == cols).astype(F32).astype(BF16)


def norm_rows_of(full_ref):
    return dot_nt(eye(LANES), full_ref[:, 4 * D :])[NORM_AT : NORM_AT + 8]


def vmem():
    return pl.BlockSpec(memory_space=pltpu.VMEM)


def smem():
    return pl.BlockSpec(memory_space=pltpu.SMEM)


def room(mebibytes):
    return pltpu.CompilerParams(vmem_limit_bytes=mebibytes * 2**20)


def whole(shape):
    return pl.BlockSpec(shape, lambda *_: (0,) * len(shape), pipeline_mode=pl.Buffered(1))


def far(value):
    return pltpu.with_memory_space_constraint(value, pltpu.HBM)


def once(kernel, scalars, arrays, outs, name, mebibytes, scratch=()):
    return pl.pallas_call(
        kernel,
        grid=(1,),
        in_specs=[smem()] * len(scalars) + [whole(a.shape) for a in arrays],
        out_specs=tuple(whole(o[0]) for o in outs),
        out_shape=tuple(jax.ShapeDtypeStruct(*o) for o in outs),
        scratch_shapes=[pltpu.VMEM(*held) for held in scratch],
        compiler_params=room(mebibytes),
        cost_estimate=LIGHT,
        name=name,
    )(*scalars, *arrays)


def place_table(count, shard_rows):
    table = np.zeros((32, 48), np.int32)
    for place in range(8):
        for member in range(4):
            tall, core = place // 2, place % 2
            row = table[place * 4 + member]
            row[0:3] = member * count, core, tall in (1, 2)
            for d in range(4):
                row[4 + d] = member ^ d
                row[16 + d] = shard_rows * (2 * (tall ^ d) + core)
                row[20 + d] = shard_rows * (2 * (tall ^ d) + 1 - core)
            for owner in range(8):
                row[28 + owner] = shard_rows * ((owner % 2 ^ core) * 4 + (owner // 2 ^ tall))
    return table


def wanted(meta, ends, d):
    rows = ends.shape[1] // 4
    here, there = meta[4] * rows, meta[4 + d] * rows
    return (ends[0, there] <= ends[0, here + rows - 1]) & (ends[0, there + rows - 1] >= ends[0, here])


def images_of(meta, image, d):
    rows = image.shape[1] // 4
    return image[0:1, pl.ds(pl.multiple_of(meta[4 + d] * rows, LANES), rows)].astype(F32)


def pack_kernel(
    patches, routes, tasks, attend, output, router, norm, own, shard, wide, square,
):
    rows = patches.shape[1]
    shard_rows = attend.shape[0]
    shard[:, 0 : 3 * D] = attend[...].astype(BF16)
    shard[:, 3 * D : 4 * D] = output[...].astype(BF16)
    square[...] = jnp.zeros_like(square)
    for t in range(TASKS):
        square[t * EXPERTS : (t + 1) * EXPERTS, 0:shard_rows] = router[t]
    square[NORM_AT : NORM_AT + 4, 0:shard_rows] = norm[...]
    shard[:, 4 * D :] = jnp.transpose(square[...])[:shard_rows].astype(BF16)
    own[0:rows, :] = patches[0]
    wide[...] = jnp.zeros_like(wide)
    wide[:, 0:TOP] = routes[0].astype(F32)
    lists = jnp.concatenate([jnp.transpose(wide[...])[:TOP], tasks[...].astype(F32)], axis=0)
    rest = jnp.concatenate([lists[:, D:], jnp.zeros((TOP + 1, 2 * D - rows), F32)], axis=1)
    lines = []
    for k in range(TOP + 1):
        lines = lines + [lists[k : k + 1, :D], rest[k : k + 1]]
    lines = lines + [jnp.zeros((INFO - 2 * (TOP + 1), D), F32)]
    own[rows : rows + INFO, :] = jnp.concatenate(lines, axis=0).astype(BF16)


def pack_call(patches, routes, tasks, attend, output, router, norm):
    rows = patches.shape[1]
    return once(
        pack_kernel, (), tuple(map(far, (patches, routes, tasks, attend, output, router, norm))),
        (((rows + INFO, D), BF16), ((attend.shape[0], WCOLS), BF16)),
        "pack", 12, (((rows, LANES), F32), ((LANES, LANES), F32)),
    )


def join_kernel(s0, s1, s2, s3, joined):
    part = s0.shape[0]
    for d, ref in enumerate((s0, s1, s2, s3)):
        joined[d * part : (d + 1) * part, :] = ref[...]


def join_call(shards):
    rows, cols = shards[0].shape
    return once(join_kernel, (), shards, (((4 * rows, cols), BF16),), "join", 12)[0]


def route_kernel(meta, i0, i1, i2, i3, row_out, pick_out, col_out, plan_out):
    base = meta[0]
    rows = i0.shape[1] + LANES
    later = lax.broadcasted_iota(jnp.int32, (rows, rows), 0)
    token = lax.broadcasted_iota(jnp.int32, (rows, rows), 1)
    before = (later < token).astype(F32).astype(BF16)
    one = (later == token).astype(F32).astype(BF16)
    local = row_out.shape[0]
    which = lax.broadcasted_iota(jnp.int32, (local, rows), 0)
    slot_names = (which + base).astype(F32)
    every = lax.broadcasted_iota(jnp.int32, (EXPERTS, rows), 0).astype(F32)
    experts = plan_out.shape[0] // 8
    starts = [jnp.int32(0)] * experts
    for d, ref in enumerate((i0, i1, i2, i3)):
        info = ref[...].astype(F32)

        def line(k):
            return jnp.concatenate([info[2 * k : 2 * k + 1], info[2 * k + 1 : 2 * k + 2, :LANES]], axis=1)

        mine = jnp.zeros((local, rows), jnp.bool_)
        chosen = jnp.zeros((EXPERTS, rows), jnp.bool_)
        for k in range(TOP):
            named = line(k)
            mine = mine | (slot_names == named)
            chosen = chosen | (every == named)
        mine = jnp.where(mine & (which < experts), 1.0, 0.0)
        chosen = jnp.where(chosen, 1.0, 0.0)
        rank = dot_nn(mine.astype(BF16), before)
        spot = jnp.where(mine > 0.5, rank, -1.0)
        at = slice(d * rows, (d + 1) * rows)
        row_out[:, at] = spot
        tasks = jnp.broadcast_to(line(TOP), (8, rows))
        pick_out[0:EXPERTS, at] = chosen
        pick_out[EXPERTS:, at] = tasks
        table = jnp.concatenate(
            [spot, jnp.zeros((16 - local, rows), F32), chosen, tasks, jnp.zeros((LANES - 40, rows), F32)],
            axis=0,
        )
        col_out[d * rows : (d + 1) * rows, :] = dot_nt(one, table.astype(BF16))
        for e in range(experts):
            held = jnp.sum(mine[e : e + 1, :]).astype(jnp.int32)
            plan_out[e * 8 + d] = starts[e]
            starts[e] = starts[e] + (held + 15) // 16 * 16
    for e in range(experts):
        plan_out[e * 8 + 4] = starts[e]
        plan_out[e * 8 + 5] = (starts[e] + CAP - 1) // CAP


def route_call(meta, pieces, experts):
    rows = pieces[0].shape[0] - INFO
    return pl.pallas_call(
        route_kernel,
        grid=(1,),
        in_specs=[smem()] + [pl.BlockSpec((INFO, D), lambda i: (rows // INFO, 0))] * 4,
        out_specs=(
            pl.BlockSpec((8, 4 * rows), lambda i: (0, 0)),
            pl.BlockSpec((EXPERTS + 8, 4 * rows), lambda i: (0, 0)),
            pl.BlockSpec((4 * rows, LANES), lambda i: (0, 0)),
            smem(),
        ),
        out_shape=(
            jax.ShapeDtypeStruct((8, 4 * rows), F32),
            jax.ShapeDtypeStruct((EXPERTS + 8, 4 * rows), F32),
            jax.ShapeDtypeStruct((4 * rows, LANES), F32),
            jax.ShapeDtypeStruct((experts * 8,), jnp.int32),
        ),
        compiler_params=room(24),
        cost_estimate=LIGHT,
        name="routing",
    )(meta, *pieces)


def front_kernel(
    meta, ends, image, p0, p1, p2, p3, near, away,
    qkv, full, att, lse_col, lse_row, middle, mixed,
    everything, scores, top, total, out_acc,
):
    rows = att.shape[0]
    part = near.shape[0] // 4
    for j in range(8):
        held = (near, away)[j // 4]
        full[pl.ds(pl.multiple_of(meta[16 + j], 16), part), :] = held[j % 4 * part : (j % 4 + 1) * part, :]
    for d, ref in enumerate((p0, p1, p2, p3)):
        everything[d * rows : (d + 1) * rows, :] = ref[:rows, :]
    norms = norm_rows_of(full)
    tile = 256

    def project(i, carry):
        at = pl.ds(pl.multiple_of(i * tile, tile), tile)
        unit, _ = unit_rows(everything[at, :].astype(F32))
        normed = (unit * norms[0:1] + norms[1:2]).astype(BF16)
        for third in range(3):
            made = dot_nn(normed, full[:, third * D : (third + 1) * D]).astype(BF16)
            if third == 0:
                made = made * jnp.asarray(HEAD_DIM ** (-0.5), BF16)
            for part in range(PAIRS):
                qkv[third * PAIRS + part, at, :] = made[:, part * LANES : (part + 1) * LANES]
        return carry

    lax.fori_loop(0, 4 * rows // tile, project, 0)
    own_row = images_of(meta, image, 0)
    own_col = jnp.transpose(jnp.broadcast_to(own_row, (LANES, rows)))[:, :1]
    lane = lax.broadcasted_iota(jnp.int32, (rows, LANES), 1)
    lse_col[...] = jnp.zeros_like(lse_col)

    def pair_of_heads(pair, carry):
        sides = (lane < HEAD_DIM, lane >= HEAD_DIM)
        queries = [jnp.where(held, qkv[pair, 0:rows, :], jnp.zeros((), BF16)) for held in sides]
        top[...] = jnp.full_like(top, MASKED)

        def score(d, c):
            @pl.when(wanted(meta, ends, d))
            def _():
                key = qkv[PAIRS + pair, pl.ds(pl.multiple_of(d * rows, rows), rows), :]
                same = own_col == images_of(meta, image, d)
                for half in range(2):
                    raw = jnp.where(same, dot_nt(queries[half], key), MASKED)
                    scores[half, d] = raw
                    top[half] = jnp.maximum(top[half], jnp.max(raw, axis=1, keepdims=True))

            return c

        lax.fori_loop(0, 4, score, 0)
        total[...] = jnp.zeros_like(total)
        out_acc[...] = jnp.zeros_like(out_acc)
        peaks = (top[0], top[1])

        def weigh(d, c):
            @pl.when(wanted(meta, ends, d))
            def _():
                value = qkv[2 * PAIRS + pair, pl.ds(pl.multiple_of(d * rows, rows), rows), :]
                for half in range(2):
                    shares = jnp.exp(scores[half, d] - peaks[half])
                    total[half] += jnp.sum(shares, axis=1, keepdims=True)
                    out_acc[half] += dot_nn(shares.astype(BF16), value)

            return c

        lax.fori_loop(0, 4, weigh, 0)
        done = []
        for half in range(2):
            done.append(out_acc[half] / total[half])
            lse_col[...] = jnp.where(lane == 2 * pair + half, peaks[half] + jnp.log(total[half]), lse_col[...])
        att[:, pl.ds(pl.multiple_of(pair * LANES, LANES), LANES)] = jnp.where(lane < HEAD_DIM, done[0], done[1])
        return carry

    lax.fori_loop(0, PAIRS, pair_of_heads, 0)
    lse_row[...] = jnp.transpose(lse_col[...])[:8]
    branch = dot_nn(att[...].astype(BF16), full[:, 3 * D : 4 * D])
    centre = everything[0:rows, :].astype(F32) + branch
    middle[...] = centre
    unit, _ = unit_rows(centre)
    mixed[...] = (unit * norms[2:3] + norms[3:4]).astype(BF16)


def front_call(meta, image, pieces, shards):
    rows = pieces[0].shape[0] - INFO
    return once(
        front_kernel, (meta, image), tuple(map(far, (image, *pieces, *shards))),
        (
            ((3 * PAIRS, 4 * rows, LANES), BF16), ((D, WCOLS), BF16), ((rows, D), F32), ((rows, LANES), F32),
            ((8, rows), F32), ((rows, D), F32), ((rows, D), BF16),
        ),
        "front", 40,
        (
            ((4 * rows, D), BF16), ((2, 4, rows, rows), F32), ((2, rows, 1), F32), ((2, rows, 1), F32),
            ((2, rows, LANES), F32),
        ),
    )


def gate_rows(mix, router_rows, choice):
    both = dot_nt(router_rows, mix)
    open_ = choice[:EXPERTS] > 0.5
    logits = jnp.where(choice[EXPERTS : EXPERTS + 1] < 0.5, both[:EXPERTS], both[EXPERTS : 2 * EXPERTS])
    logits = jnp.where(open_, logits, MASKED)
    raised = jnp.where(open_, jnp.exp(logits - jnp.max(logits, axis=0, keepdims=True)), 0.0)
    return raised / jnp.sum(raised, axis=0, keepdims=True)


def expert_kernel(
    local, plan, meta, m0, m1, m2, m3, g0, g1, g2, g3, spot_row, choice, given, up, down,
    mine, other, results, gates_out,
    gates, hidden, upstream, gate_slots, sum_up, sum_down,
):
    core = meta[1]
    low_up, low_down = up.at[0], down.at[0]
    expert = meta[0] + local
    rows = m0.shape[0]
    mixes = (m0, m1, m2, m3)
    grads = (g0, g1, g2, g3)

    if local == 0:
        router_rows = jnp.transpose(given[:, 4 * D :])
        for d in range(4):
            at = slice(d * rows, (d + 1) * rows)
            gates[:, at] = gate_rows(mixes[d][...], router_rows, choice[:, at])
        gates_out[...] = gates[...]
    else:
        gates[...] = given[...]
        gates_out[...] = jnp.zeros_like(gates_out)
    slot_at = lax.broadcasted_iota(jnp.int32, (CAP, rows), 0).astype(F32)
    lane = lax.broadcasted_iota(jnp.int32, (CAP, LANES), 1)
    for d in range(4):
        at = slice(d * rows, (d + 1) * rows)
        hit = slot_at == spot_row[local : local + 1, at]
        pick = jnp.where(hit, 1.0, 0.0).astype(BF16)
        gate = jnp.sum(jnp.where(hit, gates[pl.ds(expert, 1), at], 0.0), axis=1, keepdims=True)
        start = pl.multiple_of(plan[local * 8 + d], 16)
        hidden[pl.ds(start, CAP), :] = dot_nn(pick, mixes[d][...]).astype(BF16)
        upstream[pl.ds(start, CAP), :] = (gate * dot_nn(pick, grads[d][...])).astype(BF16)
        gate_slots[pl.ds(start, CAP), :] = jnp.broadcast_to(gate, (CAP, LANES))
    ending = pl.multiple_of(plan[local * 8 + 4], 16)
    hidden[pl.ds(ending, CAP), :] = jnp.zeros((CAP, D), BF16)
    upstream[pl.ds(ending, CAP), :] = jnp.zeros((CAP, D), BF16)
    gate_slots[pl.ds(ending, CAP), :] = jnp.zeros((CAP, LANES), F32)
    sum_up[...] = jnp.zeros_like(sum_up)
    sum_down[...] = jnp.zeros_like(sum_down)
    wide = 512

    def tile(i, carry):
        at = pl.ds(pl.multiple_of(i * CAP, CAP), CAP)
        x = hidden[at, :]
        g = upstream[at, :]
        x_t = jnp.transpose(x)
        g_t = jnp.transpose(g)
        made = jnp.zeros((CAP, D), F32)
        back = jnp.zeros((CAP, D), F32)
        for j in range(FFN // wide):
            cols = slice(j * wide, (j + 1) * wide)
            pre = dot_nn(x, low_up[:, cols])
            pull = dot_nt(g, low_down[cols, :])
            share = 0.5 + 0.5 * lax.erf(pre * 0.7071067811865476)
            active = (pre * share).astype(BF16)
            slope = share + pre * (0.3989422804014327 * jnp.exp(-0.5 * pre * pre))
            pre_grad = (slope * pull).astype(BF16)
            made = made + dot_nn(active, low_down[cols, :])
            back = back + dot_nt(pre_grad, low_up[:, cols])
            sum_up[:, cols] += dot_nn(x_t, pre_grad)
            sum_down[:, cols] += dot_nn(g_t, active)
        results[at, 0:D] = (gate_slots[at, 0:1] * made).astype(BF16)
        results[at, D : 2 * D] = back.astype(BF16)
        term = jnp.sum(g.astype(F32) * made, axis=1, keepdims=True)
        high = term.astype(BF16).astype(F32)
        ends = jnp.where(lane == expert, high, 0.0) + jnp.where(lane == 32 + expert, term - high, 0.0)
        results[at, 2 * D :] = ends.astype(BF16)
        return carry

    count = plan[local * 8 + 5]
    lax.fori_loop(0, count, tile, 0)
    results[pl.ds(pl.multiple_of(count * CAP, CAP), CAP), :] = jnp.zeros((CAP, 2 * D + LANES), BF16)
    half = FFN // 2
    quarter = D // 2

    for ref, side in ((mine, core), (other, 1 - core)):
        for b in range(2):
            cols = pl.ds(pl.multiple_of(side * half + b * D, LANES), D)
            ref[b * D : (b + 1) * D, :] = sum_down[:, cols].astype(BF16)
        held = sum_up[pl.ds(pl.multiple_of(side * quarter, 16), quarter), :].astype(BF16)
        for b in range(4):
            ref[half + b * quarter : half + (b + 1) * quarter, :] = held[:, b * D : (b + 1) * D]


def expert_call(local, plan, meta, mixes, grads, spot_row, choice, given, up, down):
    rows = mixes[0].shape[0]
    slots = 4 * CAP + CAP
    cols = 2 * D + LANES
    return pl.pallas_call(
        functools.partial(expert_kernel, local),
        grid=(1,),
        in_specs=[smem()] * 2
        + [whole((rows, D))] * 8
        + [
            whole((8, 4 * rows)),
            whole((EXPERTS + 8, 4 * rows)),
            whole(given.shape),
            pl.BlockSpec((1, D, FFN), lambda _: (local, 0, 0), pipeline_mode=pl.Buffered(1)),
            pl.BlockSpec((1, FFN, D), lambda _: (local, 0, 0), pipeline_mode=pl.Buffered(1)),
        ],
        out_specs=(whole((4 * D, D)), whole((4 * D, D)), whole((slots, cols)), whole((EXPERTS, 4 * rows))),
        out_shape=(
            jax.ShapeDtypeStruct((4 * D, D), BF16),
            jax.ShapeDtypeStruct((4 * D, D), BF16),
            jax.ShapeDtypeStruct((slots, cols), BF16),
            jax.ShapeDtypeStruct((EXPERTS, 4 * rows), F32),
        ),
        scratch_shapes=[
            pltpu.VMEM((EXPERTS, 4 * rows), F32),
            pltpu.VMEM((slots, D), BF16),
            pltpu.VMEM((slots, D), BF16),
            pltpu.VMEM((slots, LANES), F32),
            pltpu.VMEM((D, FFN), F32),
            pltpu.VMEM((D, FFN), F32),
        ],
        compiler_params=room(36),
        cost_estimate=LIGHT,
        name="experts",
    )(plan, meta, *mixes, *grads, spot_row, choice, given, far(up), far(down))


def combine_kernel(
    plan, m0, m1, m2, m3, spot_col, gates, full, res0, res1, res2, res3,
    b0, b1, b2, b3, x0, x1, x2, x3, router_out,
    stack,
):
    rows = m0.shape[0]
    lane = lax.broadcasted_iota(jnp.int32, (rows, LANES), 1)
    slot_along = lax.broadcasted_iota(jnp.int32, (rows, CAP), 1).astype(F32)
    routers = jnp.concatenate([full[:, 4 * D :], full[:, 4 * D :]], axis=1)
    total = jnp.zeros((D, 2 * LANES), F32)
    for d, (mix, back_out, mix_out) in enumerate(((m0, b0, x0), (m1, b1, x1), (m2, b2, x2), (m3, b3, x3))):
        at = slice(d * rows, (d + 1) * rows)
        info = spot_col[at, :]
        puts = []
        for e in range(4):
            start = pl.multiple_of(plan[e * 8 + d], 16)
            stack[e * CAP : (e + 1) * CAP, :] = (res0, res1, res2, res3)[e][pl.ds(start, CAP), :]
            puts.append(jnp.where(slot_along == info[:, e : e + 1], 1.0, 0.0).astype(BF16))
        got = dot_nn(jnp.concatenate(puts, axis=1), stack[...])
        mix_out[...] = got[:, :D].astype(BF16)
        ends = got[:, 2 * D :]
        held = jnp.where(lane < EXPERTS, ends + pltpu.roll(ends, LANES - 32, 1), 0.0)
        gate = jnp.transpose(
            jnp.concatenate([gates[:, at], jnp.zeros((LANES - EXPERTS, rows), F32)], axis=0)
        )
        change = held - jnp.sum(held, axis=1, keepdims=True) * gate
        task = info[:, 32:33]
        early = jnp.where((lane < EXPERTS) & (task < 0.5), change, 0.0)
        late = jnp.where(
            (lane >= EXPERTS) & (lane < 2 * EXPERTS) & (task > 0.5), pltpu.roll(change, EXPERTS, 1), 0.0
        )
        both = early + late
        high = both.astype(BF16)
        low = (both - high.astype(F32)).astype(BF16)
        parts = jnp.concatenate([high, low], axis=1)
        pulled = dot_nt(parts, routers)
        total = total + dot_tn(mix[...], parts)
        back_out[...] = (got[:, D : 2 * D] + pulled).astype(BF16)
    router_out[...] = total[:, :LANES] + total[:, LANES:]


def combine_call(plan, mixes, spot_col, gates, full, results):
    rows = mixes[0].shape[0]
    return once(
        combine_kernel, (plan,), (*mixes, spot_col, gates, full, *results),
        (((rows, D), BF16),) * 8 + (((D, LANES), F32),),
        "combine", 40, (((4 * CAP, 2 * D + LANES), BF16),),
    )


def turn_kernel(b0, r1, r2, r3, middle, grad, full, att, lse_row, middle_grad, sent, dots_col, output_grad, norm_two):
    rows = middle.shape[0]
    norms = norm_rows_of(full)
    mixed_grad = b0[...].astype(F32) + r1[...].astype(F32) + r2[...].astype(F32) + r3[...].astype(F32)
    unit, scale = unit_rows(middle[...])
    norm_two[...] = jnp.zeros_like(norm_two)
    norm_two[0:1, :] = jnp.sum(mixed_grad * unit, axis=0, keepdims=True)
    norm_two[1:2, :] = jnp.sum(mixed_grad, axis=0, keepdims=True)
    pulled = mixed_grad * norms[2:3]
    through = pulled - jnp.mean(pulled, axis=1, keepdims=True)
    through = scale * (through - unit * jnp.mean(pulled * unit, axis=1, keepdims=True))
    whole = through + grad[...].astype(F32)
    middle_grad[...] = whole
    branch = whole.astype(BF16)
    output_grad[...] = dot_tn(att[...].astype(BF16), branch).astype(BF16)
    pulled = dot_nt(branch, full[:, 3 * D : 4 * D]).astype(BF16)
    sent[0:rows, :] = pulled
    product = pulled.astype(F32) * att[...]
    high = product.astype(BF16)
    low = (product - high.astype(F32)).astype(BF16)
    heads = (
        lax.broadcasted_iota(jnp.int32, (D, LANES), 0) // HEAD_DIM
        == lax.broadcasted_iota(jnp.int32, (D, LANES), 1)
    )
    heads = heads.astype(F32).astype(BF16)
    dots = dot_nn(high, heads) + dot_nn(low, heads)
    dots_col[...] = dots
    lines = jnp.concatenate([lse_row[...], jnp.transpose(dots)[:8]], axis=0)
    high = lines.astype(BF16).astype(F32)
    table = jnp.concatenate([high, lines - high], axis=0).astype(BF16)
    half = EXTRA // 2
    sent[rows : rows + half, :] = table[:, :D]
    sent[rows + half : rows + EXTRA, :] = jnp.zeros((half, D), BF16)
    sent[rows + half : rows + EXTRA, : rows - D] = table[:, D:]


def turn_call(back, received, middle, grad, full, att, lse_row):
    rows = middle.shape[0]
    return once(
        turn_kernel, (), (back, *received, middle, grad, full, att, lse_row),
        (((rows, D), F32), ((rows + EXTRA, D), BF16), ((rows, LANES), F32), ((D, D), BF16), ((8, D), F32)),
        "turn", 24,
    )


def attention_back_kernel(
    meta, ends, image, qkv, s0, s1, s2, s3, lse_col, dots_col, own, full, middle_grad, output_grad, norm_two, routers,
    input_grad, to0, to1, to2, to3,
    lines, grads, packed, acc_one, acc_two, shared,
):
    rows = input_grad.shape[0]
    half_extra = EXTRA // 2
    for d, ref in enumerate((s0, s1, s2, s3)):
        grads[d] = ref[0:rows, :]
        table = jnp.concatenate(
            [ref[rows : rows + half_extra, :], ref[rows + half_extra : rows + EXTRA, : rows - D]], axis=1
        ).astype(F32)
        lines[d] = table[:16] + table[16:]
    own_row = images_of(meta, image, 0)
    own_col = jnp.transpose(jnp.broadcast_to(own_row, (LANES, rows)))[:, :1]
    lane = lax.broadcasted_iota(jnp.int32, (rows, LANES), 1)
    none = jnp.zeros((), BF16)
    here = slice(0, rows)

    def pair_of_heads(pair, carry):
        lanes = pl.ds(pl.multiple_of(pair * LANES, LANES), LANES)
        sides = (lane < HEAD_DIM, lane >= HEAD_DIM)
        queries = [jnp.where(held, qkv[pair, here, :], none) for held in sides]
        pulls = [jnp.where(held, grads[0, :, lanes], none) for held in sides]
        log_totals, all_dots = [
            [
                jnp.sum(jnp.where(lane == 2 * pair + half, table[...], 0.0), axis=1, keepdims=True)
                for half in range(2)
            ]
            for table in (lse_col, dots_col)
        ]
        acc_one[...] = jnp.zeros_like(acc_one)

        def over_keys(d, c):
            @pl.when(wanted(meta, ends, d))
            def _():
                at = pl.ds(pl.multiple_of(d * rows, rows), rows)
                key = qkv[PAIRS + pair, at, :]
                same = own_col == images_of(meta, image, d)
                for half in range(2):
                    shares = jnp.where(same, jnp.exp(dot_nt(queries[half], key) - log_totals[half]), 0.0)
                    change = dot_nt(pulls[half], qkv[2 * PAIRS + pair, at, :]) - all_dots[half]
                    acc_one[half] += dot_nn((shares * change).astype(BF16), key)

            return c

        lax.fori_loop(0, 4, over_keys, 0)
        packed[:, lanes] = jnp.where(lane < HEAD_DIM, acc_one[0], acc_one[1]) * (HEAD_DIM ** (-0.5))
        keys = [jnp.where(held, qkv[PAIRS + pair, here, :], none) for held in sides]
        values = [jnp.where(held, qkv[2 * PAIRS + pair, here, :], none) for held in sides]
        acc_one[...] = jnp.zeros_like(acc_one)
        acc_two[...] = jnp.zeros_like(acc_two)

        def over_queries(d, c):
            @pl.when(wanted(meta, ends, d))
            def _():
                at = pl.ds(pl.multiple_of(d * rows, rows), rows)
                query = qkv[pair, at, :]
                pull = grads[d, :, lanes]
                same = own_col == images_of(meta, image, d)
                for half in range(2):
                    log_total = lines[d, pl.ds(2 * pair + half, 1), :]
                    dots = lines[d, pl.ds(8 + 2 * pair + half, 1), :]
                    shares = jnp.where(same, jnp.exp(dot_nt(keys[half], query) - log_total), 0.0)
                    change = dot_nt(values[half], pull) - dots
                    acc_two[half] += dot_nn(shares.astype(BF16), pull)
                    acc_one[half] += dot_nn((shares * change).astype(BF16), query)

            return c

        lax.fori_loop(0, 4, over_queries, 0)
        made = [(acc_one[half], acc_two[half]) for half in range(2)]
        shift = pl.ds(pl.multiple_of(D + pair * LANES, LANES), LANES)
        packed[:, shift] = jnp.where(lane < HEAD_DIM, made[0][0], made[1][0])
        shift = pl.ds(pl.multiple_of(2 * D + pair * LANES, LANES), LANES)
        packed[:, shift] = jnp.where(lane < HEAD_DIM, made[0][1], made[1][1])
        return carry

    lax.fori_loop(0, PAIRS, pair_of_heads, 0)
    norms = norm_rows_of(full)
    unit, scale = unit_rows(own[0:rows, :].astype(F32))
    normed = (unit * norms[0:1] + norms[1:2]).astype(BF16)
    normed_grad = jnp.zeros((rows, D), F32)
    for third in range(3):
        part = packed[:, third * D : (third + 1) * D].astype(BF16)
        normed_grad = normed_grad + dot_nt(part, full[:, third * D : (third + 1) * D])
        weight_grad = dot_tn(normed, part).astype(BF16)
        for j in range(PAIRS):
            block = third * PAIRS + j
            shared[meta[4 + block // 4], :, block % 4 * LANES : (block % 4 + 1) * LANES] = weight_grad[
                :, j * LANES : (j + 1) * LANES
            ]
    pulled = normed_grad * norms[0:1]
    through = pulled - jnp.mean(pulled, axis=1, keepdims=True)
    through = scale * (through - unit * jnp.mean(pulled * unit, axis=1, keepdims=True))
    input_grad[...] = through + middle_grad[...]
    for j in range(PAIRS):
        block = 3 * PAIRS + j
        shared[meta[4 + block // 4], :, block % 4 * LANES : (block % 4 + 1) * LANES] = output_grad[
            :, j * LANES : (j + 1) * LANES
        ]
    lines_norm = jnp.concatenate(
        [
            jnp.zeros((NORM_AT, D), F32),
            jnp.sum(normed_grad * unit, axis=0, keepdims=True),
            jnp.sum(normed_grad, axis=0, keepdims=True),
            norm_two[0:2, :],
            jnp.zeros((LANES - NORM_AT - 4, D), F32),
        ],
        axis=0,
    )
    small = routers[...] + jnp.transpose(lines_norm)
    shared[meta[7], :, 0:LANES] = small.astype(BF16)
    shared[meta[7], :, LANES:] = jnp.zeros((D, 3 * LANES), BF16)
    part = D // 8
    for d, ref in enumerate((to0, to1, to2, to3)):
        for owner in range(8):
            at = pl.ds(pl.multiple_of(meta[28 + owner], 16), part)
            ref[at, :] = shared[d, owner * part : (owner + 1) * part, :]


def attention_back_call(meta, image, qkv, sent, lse_col, dots_col, own, full, middle_grad, output_grad, norm_two, routers):
    rows = middle_grad.shape[0]
    return once(
        attention_back_kernel, (meta, image),
        (image, qkv, *sent, lse_col, dots_col, own, full, middle_grad, output_grad, norm_two, routers),
        (((rows, D), F32),) + (((D, 4 * LANES), BF16),) * 4,
        "attention_back", 40,
        (
            ((4, 16, rows), F32), ((4, rows, D), BF16), ((rows, 3 * D), F32), ((2, rows, LANES), F32),
            ((2, rows, LANES), F32), ((4, D, 4 * LANES), BF16),
        ),
    )


def adamw(weight, moment, second, gradient, step_rate):
    moment = BETA_FIRST * moment + (1.0 - BETA_FIRST) * gradient
    second = BETA_SECOND * second + (1.0 - BETA_SECOND) * gradient * gradient
    spread = jnp.sqrt(second * (1.0 / (1.0 - BETA_SECOND**STEP))) + ADAM_EPS
    change = moment * (step_rate / (1.0 - BETA_FIRST**STEP)) / spread
    weight = weight * (1.0 - step_rate * DECAY) - change
    return (weight, moment, second)


def adam_kernel(meta, ready, passed, w1, m1, v1, w2, m2, v2, *rest):
    outs = rest[-6:]
    step = pl.program_id(0)
    half_steps = pl.num_programs(0) // 2
    mine = (step // half_steps) == meta[1]
    inner = step % half_steps
    up_rows, down_rows = w1.shape[1], w2.shape[1]
    half = FFN // 2
    quarter = D // 2

    def pick(rows_at, lanes_at):
        return jnp.where(mine, ready[rows_at, lanes_at], passed[rows_at, lanes_at]).astype(F32)

    per = D // down_rows
    down = pick(
        pl.ds(pl.multiple_of(inner // per * D, D), D), pl.ds(pl.multiple_of(inner % per * down_rows, LANES), down_rows)
    )
    up = jnp.concatenate(
        [
            pick(pl.ds(pl.multiple_of(half + b * quarter + inner * up_rows, 16), up_rows), slice(0, D))
            for b in range(4)
        ],
        axis=1,
    )
    for k, value in enumerate(adamw(w1[0], m1[0], v1[0], up, RATE_EXPAND)):
        outs[k][0] = value
    for k, value in enumerate(adamw(w2[0], m2[0], v2[0], jnp.transpose(down), RATE_REDUCE)):
        outs[3 + k][0] = value


def adam_call(expert, meta, ready, passed, states, previous):
    steps = 4
    up = pl.BlockSpec((1, D // steps, FFN), lambda i, *_: (expert, i, 0))
    down = pl.BlockSpec((1, FFN // steps, D), lambda i, *_: (expert, i, 0))
    specs = [whole(ready.shape)] * 2 + [up] * 3 + [down] * 3
    args = [ready, passed, *map(far, states)]
    aliases = {}
    if previous is not None:
        for k, value in enumerate(previous):
            aliases[1 + len(args)] = k
            args.append(value)
            specs.append(pl.BlockSpec(memory_space=pl.ANY))
    return pl.pallas_call(
        adam_kernel,
        grid_spec=pltpu.PrefetchScalarGridSpec(
            num_scalar_prefetch=1,
            grid=(steps,),
            in_specs=specs,
            out_specs=(up,) * 3 + (down,) * 3,
        ),
        out_shape=tuple(jax.ShapeDtypeStruct(s.shape, F32) for s in states),
        input_output_aliases=aliases,
        compiler_params=room(28),
        cost_estimate=LIGHT,
        name="adam",
    )(meta, *args)


def fold_kernel(a, b, c, d, kept, gone):
    rows = kept.shape[0]
    for ref, at in ((kept, slice(0, rows)), (gone, slice(rows, 2 * rows))):
        ref[...] = (
            a[at, :].astype(F32) + b[at, :].astype(F32) + c[at, :].astype(F32) + d[at, :].astype(F32)
        ).astype(BF16)


def fold_call(parts):
    rows, cols = parts[0].shape
    return once(fold_kernel, (), parts, (((rows // 2, cols), BF16),) * 2, "fold", 8)


def split_kernel(kept, came, *outs):
    for k, ref in enumerate(outs):
        at = slice(k * ref.shape[0], (k + 1) * ref.shape[0])
        ref[...] = (kept[at, :].astype(F32) + came[at, :].astype(F32)).astype(BF16)


def split_call(kept, came):
    rows, cols = kept.shape
    return once(split_kernel, (), (kept, came), (((rows // 4, cols), BF16),) * 4, "split", 8)


def settle_kernel(meta, *refs):
    pieces, states, outs, (buffer, square) = refs[:4], refs[4:16], refs[16:28], refs[28:]
    rows = pieces[0].shape[0]
    for d in range(4):
        buffer[meta[4 + d]] = pieces[d][...].astype(F32)
    square[...] = jnp.zeros_like(square)
    square[0:rows, :] = buffer[3, :, 0:LANES]
    turned = jnp.transpose(square[...])
    attend_sum = jnp.concatenate([buffer[0], buffer[1], buffer[2, :, 0:LANES]], axis=1)
    sums = (turned[NORM_AT : NORM_AT + 4, :rows], attend_sum, buffer[2, :, LANES:])
    for k, (total, rate) in enumerate(zip(sums, (RATE_NORM, RATE_ATTEND, RATE_OUTPUT))):
        held = [ref[...] for ref in states[3 * k : 3 * k + 3]]
        for ref, value in zip(outs[3 * k : 3 * k + 3], adamw(*held, total, rate)):
            ref[...] = value
    for t in range(TASKS):
        held = [ref[t] for ref in states[9:12]]
        total = turned[t * EXPERTS : (t + 1) * EXPERTS, :rows]
        for ref, value in zip(outs[9:12], adamw(*held, total, RATE_ROUTER)):
            ref[t] = value


def settle_call(meta, pieces, states):
    rows, cols = pieces[0].shape
    return once(
        settle_kernel, (meta,), (*pieces, *map(far, states)), tuple((s.shape, F32) for s in states),
        "settle", 12, (((4, rows, cols), F32), ((LANES, LANES), F32)),
    )


def swap_expert(value, d):
    return lax.ppermute(value, "expert", [(i, i ^ d) for i in range(4)])


def swap_tall(value, d):
    return lax.ppermute(value, "dp", [(2 * a + c, 2 * (a ^ d) + c) for a in range(4) for c in range(2)])


def swap_core(value):
    return lax.ppermute(value, "dp", [(i, i ^ 1) for i in range(8)])


def send_tall(value, hops):
    return lax.ppermute(value, "dp", [(2 * a + c, 2 * b + c) for a, b in hops for c in range(2)])


def tie(value, *others):
    flat, tree = jax.tree.flatten((value, others))
    return jax.tree.unflatten(tree, lax.optimization_barrier(flat))[0]


def fast_body(
    patches, out_grad, image_of, task_of, routes,
    norm_weight, norm_moment, norm_second,
    attend_weight, attend_moment, attend_second,
    output_weight, output_moment, output_second,
    router_weight, router_moment, router_second,
    expand_weight, expand_moment, expand_second,
    reduce_weight, reduce_moment, reduce_second,
):
    member = lax.axis_index("expert")
    place = lax.axis_index("dp")
    rows = patches.shape[1]
    count = expand_weight.shape[0]
    table = place_table(count, attend_weight.shape[0])
    meta = lax.dynamic_index_in_dim(jnp.asarray(table), place * 4 + member, 0, False)
    inner = (place >= 2) & (place < 6)
    image = image_of

    own, shard = pack_call(patches, routes, task_of, attend_weight, output_weight, router_weight, norm_weight)
    shards = [shard] + [swap_tall(shard, d) for d in (1, 2, 3)]
    pieces = [own] + [swap_expert(own, d) for d in (1, 2, 3)]
    near = join_call(shards)
    shards = [near, swap_core(near)]
    grad = out_grad[0]
    grads = [grad] + [swap_expert(tie(grad, *pieces[1:]), d) for d in (1, 2, 3)]

    qkv, full, att, lse_col, lse_row, middle, mixed = front_call(meta, image, pieces, shards)
    mixes = [mixed] + [swap_expert(mixed, d) for d in (1, 2, 3)]
    spot_row, choice, spot_col, plan = route_call(meta, pieces, count)

    up_low = tie(expand_weight, mixed).astype(BF16)
    down_low = tie(reduce_weight, mixed).astype(BF16)

    def first_hop(value):
        return send_tall(value, ((0, 1), (3, 2)))

    def second_hop(value):
        return send_tall(value, ((1, 2), (2, 1)))

    def third_hop(value):
        return send_tall(value, ((1, 0), (2, 3)))

    def settled(value, came):
        return jnp.where(inner, value, came)

    def expert(local, given):
        return expert_call(local, plan, meta, mixes, grads, spot_row, choice, given, up_low, down_low)

    mine0, other0, res0, gates = expert(0, full)
    half0 = mine0 + swap_core(other0)
    came_a0 = first_hop(half0)
    mine1, other1, res1, _ = expert(1, tie(gates, half0))
    got1 = swap_core(other1)
    mine2, other2, res2, _ = expert(2, tie(gates, mine1))
    got2 = swap_core(other2)
    pair0 = half0 + tie(came_a0, mine2)
    came_b0 = second_hop(pair0)
    half1 = mine1 + tie(got1, pair0)
    came_a1 = first_hop(half1)
    mine3, other3, res3, _ = expert(3, tie(gates, half1, pair0))
    got3 = swap_core(other3)
    half2 = mine2 + tie(got2, mine3)
    came_a2 = first_hop(half2)
    *outs, routers = combine_call(plan, mixes, spot_col, tie(gates, half2), full, (res0, res1, res2, res3))
    back, mix = outs[:4], outs[4:]
    returned = [swap_expert(back[d], d) for d in (1, 2, 3)]
    pair1 = half1 + tie(came_a1, routers)
    came_b1 = second_hop(pair1)
    whole0 = pair0 + tie(came_b0, routers)
    came_c0 = third_hop(whole0)
    half3 = mine3 + tie(got3, pair1, whole0)
    pair2 = half2 + tie(came_a2, half3, *returned)
    came_b2 = second_hop(pair2)
    came_a3 = first_hop(tie(half3, pair2))
    middle_grad, sent, dots_col, output_grad, norm_two = turn_call(
        tie(back[0], half3, pair2), returned, middle, grad, full, att, lse_row
    )
    sents = [sent] + [swap_expert(sent, d) for d in (1, 2, 3)]
    whole1 = pair1 + tie(came_b1, norm_two)
    ready0 = settled(whole0, tie(came_c0, norm_two))
    passed0 = swap_core(ready0)
    states = (expand_weight, expand_moment, expand_second, reduce_weight, reduce_moment, reduce_second)
    news = adam_call(0, meta, tie(ready0, pair2, whole1), passed0, states, None)
    came_c1 = third_hop(tie(whole1, news[0], *sents[1:]))
    pair3 = half3 + tie(came_a3, news[0], *sents[1:])
    came_b3 = second_hop(pair3)
    whole2 = pair2 + tie(came_b2, news[0])
    came_c2 = third_hop(whole2)
    input_grad, *shared = attention_back_call(
        meta, image, qkv, sents, tie(lse_col, pair3, whole2), dots_col, own, full, middle_grad,
        output_grad, norm_two, routers,
    )
    shared = [shared[0]] + [swap_expert(shared[d], d) for d in (1, 2, 3)]
    whole3 = pair3 + tie(came_b3, input_grad)
    came_c3 = third_hop(whole3)
    ready2 = settled(whole2, tie(came_c2, input_grad))
    ready1 = settled(whole1, tie(came_c1, input_grad))
    passed1 = tie(swap_core(ready1), whole3, ready2)
    news = adam_call(1, meta, ready1, passed1, states, news)
    kept, gone = fold_call([tie(shared[0], news[0])] + shared[1:])
    gone = swap_core(gone)
    ready3 = settled(whole3, tie(came_c3, kept))
    passed2 = tie(swap_core(tie(ready2, news[0])), ready3)
    piece, *away = split_call(kept, tie(gone, ready3))
    away = [swap_tall(away[d - 1], d) for d in (1, 2, 3)]
    news = adam_call(2, meta, tie(ready2, piece), passed2, states, news)
    piece = tie(piece, news[0]) + away[0] + away[1] + away[2]
    quarters = [piece] + [swap_expert(piece, d) for d in (1, 2, 3)]
    parts = [swap_expert(tie(mix[d], quarters[3]), d) for d in (1, 2, 3)]
    passed3 = swap_core(tie(ready3, kept))
    news = adam_call(3, meta, tie(ready3, piece), passed3, states, news)
    block_out = middle + tie(mix[0], news[0]).astype(F32)
    for part in parts:
        block_out = block_out + part.astype(F32)
    block_out = block_out.astype(BF16)[None]
    small = settle_call(
        meta, [tie(quarters[0], news[0])] + quarters[1:],
        (
            norm_weight, norm_moment, norm_second, attend_weight, attend_moment, attend_second,
            output_weight, output_moment, output_second, router_weight, router_moment, router_second,
        ),
    )
    return (block_out, input_grad[None], *small, *news)


def gelu_exact(values):
    return 0.5 * values * (1.0 + lax.erf(values * 0.7071067811865476))


def norm_rows(values, gain_row, offset):
    average = jnp.mean(values, axis=-1, keepdims=True)
    centred = values - average
    spread = jnp.mean(centred * centred, axis=-1, keepdims=True)
    return centred * lax.rsqrt(spread + NORM_EPS) * gain_row + offset


def body(
    patches,
    out_grad,
    image_of,
    task_of,
    routes,
    norm_weight,
    norm_moment,
    norm_second,
    attend_weight,
    attend_moment,
    attend_second,
    output_weight,
    output_moment,
    output_second,
    router_weight,
    router_moment,
    router_second,
    expand_weight,
    expand_moment,
    expand_second,
    reduce_weight,
    reduce_moment,
    reduce_second,
):
    precise = lax.Precision.HIGHEST
    member = lax.axis_index("expert")
    tokens = patches.shape[1]
    group_rows = image_of.shape[1]
    key_rows = min(512, group_rows)
    score_scale = HEAD_DIM ** (-0.5)
    norm_full, attend_full, output_full, router_full = (
        lax.all_gather(norm_weight.astype(jnp.bfloat16), "dp", axis=1, tiled=True),
        lax.all_gather(attend_weight.astype(jnp.bfloat16), "dp", axis=0, tiled=True),
        lax.all_gather(output_weight.astype(jnp.bfloat16), "dp", axis=0, tiled=True),
        lax.all_gather(router_weight.astype(jnp.bfloat16), "dp", axis=2, tiled=True),
    )
    norm_values = norm_full.astype(jnp.float32)
    router_values = router_full.astype(jnp.float32)
    expand_low = expand_weight.astype(jnp.bfloat16)
    reduce_low = reduce_weight.astype(jnp.bfloat16)
    inputs = patches[0].astype(jnp.float32)
    image_row = image_of[0]
    my_image = lax.dynamic_slice_in_dim(image_row, member * tokens, tokens)
    task_row = task_of[0]
    route_rows = routes[0]
    first_image = my_image[0]
    last_image = my_image[tokens - 1]
    first_key = jnp.sum((image_row < first_image).astype(jnp.int32))
    last_key = jnp.sum((image_row <= last_image).astype(jnp.int32)) - 1
    first_block = first_key // key_rows
    end_block = last_key // key_rows + 1
    normed_one, first_back = jax.vjp(norm_rows, inputs, norm_values[0], norm_values[1])
    normed_low = normed_one.astype(jnp.bfloat16)
    packed = jnp.dot(normed_low, attend_full, preferred_element_type=jnp.float32).astype(
        jnp.bfloat16
    )
    queries = packed[:, :D].reshape(tokens, HEADS, HEAD_DIM)
    key_value = packed[:, D:]
    key_value_all = lax.all_gather(key_value, "expert", axis=0, tiled=True)
    keys_all = key_value_all[:, :D].reshape(group_rows, HEADS, HEAD_DIM)
    values_all = key_value_all[:, D:].reshape(group_rows, HEADS, HEAD_DIM)

    def scores_of(query_part, key_part, same_image):
        raw = (
            jnp.einsum("thd,khd->htk", query_part, key_part, preferred_element_type=jnp.float32)
            * score_scale
        )
        return jnp.where(same_image[None], raw, MASKED)

    def block_at(block_index):
        first_row = block_index * key_rows
        key_part = lax.dynamic_slice_in_dim(keys_all, first_row, key_rows, 0)
        value_part = lax.dynamic_slice_in_dim(values_all, first_row, key_rows, 0)
        same_image = (
            my_image[:, None]
            == lax.dynamic_slice_in_dim(image_row, first_row, key_rows, 0)[None, :]
        )
        return (key_part, value_part, same_image)

    def max_step(block_index, state_in):
        highest, totals = state_in
        key_part, value_part, same_image = block_at(block_index)
        scores = scores_of(queries, key_part, same_image)
        raised = jnp.maximum(highest, jnp.max(scores, axis=-1))
        shares = jnp.where(same_image[None], jnp.exp(scores - raised[..., None]), 0.0)
        return (raised, totals * jnp.exp(highest - raised) + jnp.sum(shares, axis=-1))

    start_max = jnp.full((HEADS, tokens), MASKED, jnp.float32)
    highest, totals = lax.fori_loop(
        first_block, end_block, max_step, (start_max, jnp.zeros((HEADS, tokens), jnp.float32))
    )
    log_total = highest + jnp.log(totals)

    def value_step(block_index, accum):
        key_part, value_part, same_image = block_at(block_index)
        scores = scores_of(queries, key_part, same_image)
        soft_part = jnp.where(same_image[None], jnp.exp(scores - log_total[..., None]), 0.0).astype(
            jnp.bfloat16
        )
        return accum + jnp.einsum(
            "htk,khd->thd", soft_part, value_part, preferred_element_type=jnp.float32
        )

    attended = lax.fori_loop(
        first_block, end_block, value_step, jnp.zeros((tokens, HEADS, HEAD_DIM), jnp.float32)
    )
    attended_low = attended.reshape(tokens, D).astype(jnp.bfloat16)
    branch = jnp.dot(attended_low, output_full, preferred_element_type=jnp.float32)
    middle = inputs + branch
    normed_two, second_back = jax.vjp(norm_rows, middle, norm_values[2], norm_values[3])
    mixed_low = normed_two.astype(jnp.bfloat16)
    task_hot = (task_row[:, None] == jnp.arange(TASKS, dtype=jnp.int32)[None, :]).astype(
        jnp.float32
    )
    route_hot = (
        route_rows[:, :, None] == jnp.arange(EXPERTS, dtype=jnp.int32)[None, None, :]
    ).astype(jnp.float32)

    def gating(hidden, router):
        logits = jnp.einsum("td,ced->tce", hidden, router, precision=precise)
        task_logits = jnp.einsum("tc,tce->te", task_hot, logits, precision=precise)
        chosen = jnp.einsum("te,tke->tk", task_logits, route_hot, precision=precise)
        peak = jnp.max(chosen, axis=-1, keepdims=True)
        raised = jnp.exp(chosen - peak)
        return raised / jnp.sum(raised, axis=-1, keepdims=True)

    gate_values, gate_back = jax.vjp(gating, mixed_low.astype(jnp.float32), router_values)
    pair_expert = route_rows.reshape(-1)
    pair_hot = (pair_expert[:, None] == jnp.arange(EXPERTS, dtype=jnp.int32)[None, :]).astype(
        jnp.int32
    )
    slot_index = jnp.sum((jnp.cumsum(pair_hot, axis=0) - pair_hot) * pair_hot, axis=1)
    flat_slot = pair_expert * CAP + slot_index

    def scatter_pairs(pair_values):
        return (
            jnp.zeros((EXPERTS * CAP, D), pair_values.dtype)
            .at[flat_slot]
            .set(pair_values)
            .reshape(EXPERTS, CAP, D)
        )

    def gather_pairs(buffer):
        return (
            buffer.reshape(EXPERTS * CAP, D)[flat_slot].astype(jnp.float32).reshape(tokens, TOP, D)
        )

    received = lax.all_to_all(
        scatter_pairs(jnp.repeat(mixed_low, TOP, axis=0)),
        "expert",
        split_axis=0,
        concat_axis=1,
        tiled=True,
    )
    hidden_pre = jnp.einsum(
        "ecd,edh->ech", received, expand_low, preferred_element_type=jnp.float32
    )
    active, gelu_back = jax.vjp(gelu_exact, hidden_pre)
    active_low = active.astype(jnp.bfloat16)
    expert_out = jnp.einsum(
        "ech,ehd->ecd", active_low, reduce_low, preferred_element_type=jnp.float32
    ).astype(jnp.bfloat16)
    returned = lax.all_to_all(expert_out, "expert", split_axis=1, concat_axis=0, tiled=True)
    pair_out = gather_pairs(returned)
    expert_mix = jnp.einsum("tk,tkd->td", gate_values, pair_out, precision=precise)
    block_out = (middle + expert_mix).astype(jnp.bfloat16)[None]
    upstream = out_grad[0].astype(jnp.float32)
    gate_grad = jnp.sum(upstream[:, None, :] * pair_out, axis=-1)
    pair_grad = (
        (gate_values[:, :, None] * upstream[:, None, :])
        .astype(jnp.bfloat16)
        .reshape(tokens * TOP, D)
    )
    grad_in = lax.all_to_all(
        scatter_pairs(pair_grad), "expert", split_axis=0, concat_axis=1, tiled=True
    )
    reduce_grad = jnp.einsum(
        "ech,ecd->ehd", active_low, grad_in, preferred_element_type=jnp.float32
    )
    active_grad = jnp.einsum(
        "ecd,ehd->ech", grad_in, reduce_low, preferred_element_type=jnp.float32
    )
    pre_grad = gelu_back(active_grad)[0].astype(jnp.bfloat16)
    expand_grad = jnp.einsum("ecd,ech->edh", received, pre_grad, preferred_element_type=jnp.float32)
    back_rows = jnp.einsum(
        "ech,edh->ecd", pre_grad, expand_low, preferred_element_type=jnp.float32
    ).astype(jnp.bfloat16)
    expand_sum, reduce_sum = (
        lax.psum(expand_grad.astype(jnp.bfloat16), "dp").astype(jnp.float32),
        lax.psum(reduce_grad.astype(jnp.bfloat16), "dp").astype(jnp.float32),
    )
    came_back = lax.all_to_all(back_rows, "expert", split_axis=1, concat_axis=0, tiled=True)
    routed_grad = jnp.sum(gather_pairs(came_back), axis=1)
    hidden_gate_grad, router_grad = gate_back(gate_grad)
    middle_part, gain_two, offset_two = second_back(routed_grad + hidden_gate_grad)
    middle_grad = middle_part + upstream
    branch_grad = middle_grad.astype(jnp.bfloat16)
    output_grad = jnp.einsum(
        "td,te->de", attended_low, branch_grad, preferred_element_type=jnp.float32
    )
    attended_grad = (
        jnp.einsum("te,de->td", branch_grad, output_full, preferred_element_type=jnp.float32)
        .astype(jnp.bfloat16)
        .reshape(tokens, HEADS, HEAD_DIM)
    )
    row_dots = jnp.einsum(
        "thd,thd->ht", attended_grad.astype(jnp.float32), attended, precision=precise
    )

    def score_grad(query_part, key_part, value_part, grad_part, same_image, log_part, dots_part):
        scores = scores_of(query_part, key_part, same_image)
        soft_part = jnp.where(same_image[None], jnp.exp(scores - log_part[..., None]), 0.0)
        soft_grad = jnp.einsum(
            "thd,khd->htk", grad_part, value_part, preferred_element_type=jnp.float32
        )
        return (soft_part, (soft_part * (soft_grad - dots_part[..., None])).astype(jnp.bfloat16))

    def pair_step(block_index, state_in):
        query_acc, terms_acc = state_in
        key_part, value_part, same_image = block_at(block_index)
        soft_part, dscore = score_grad(
            queries, key_part, value_part, attended_grad, same_image, log_total, row_dots
        )
        query_acc = query_acc + jnp.einsum(
            "htk,khd->thd", dscore, key_part, preferred_element_type=jnp.float32
        )
        key_term = (
            jnp.einsum("htk,thd->khd", dscore, queries, preferred_element_type=jnp.float32)
            * score_scale
        )
        value_term = jnp.einsum(
            "htk,thd->khd",
            soft_part.astype(jnp.bfloat16),
            attended_grad,
            preferred_element_type=jnp.float32,
        )
        terms = jnp.concatenate(
            [key_term.reshape(key_rows, D), value_term.reshape(key_rows, D)], axis=1
        )
        terms_acc = lax.dynamic_update_slice_in_dim(terms_acc, terms, block_index * key_rows, 0)
        return (query_acc, terms_acc)

    query_acc, key_value_terms = lax.fori_loop(
        first_block,
        end_block,
        pair_step,
        (
            jnp.zeros((tokens, HEADS, HEAD_DIM), jnp.float32),
            jnp.zeros((group_rows, 2 * D), jnp.float32),
        ),
    )
    key_value_grad = lax.psum_scatter(
        key_value_terms.astype(jnp.bfloat16), "expert", scatter_dimension=0, tiled=True
    ).astype(jnp.float32)
    query_grad = (query_acc * score_scale).reshape(tokens, D)
    packed_grad = jnp.concatenate([query_grad, key_value_grad], axis=1).astype(jnp.bfloat16)
    attend_grad = jnp.einsum(
        "td,te->de", normed_low, packed_grad, preferred_element_type=jnp.float32
    )
    normed_grad = jnp.einsum(
        "te,de->td", packed_grad, attend_full, preferred_element_type=jnp.float32
    )
    input_part, gain_one, offset_one = first_back(normed_grad)
    input_grad = (middle_grad + input_part)[None]
    norm_grad = jnp.stack([gain_one, offset_one, gain_two, offset_two])
    shared = (norm_grad, attend_grad, output_grad, router_grad)
    summed = (
        lax.psum(shared[0].astype(jnp.bfloat16), "expert").astype(jnp.float32),
        lax.psum(shared[1].astype(jnp.bfloat16), "expert").astype(jnp.float32),
        lax.psum(shared[2].astype(jnp.bfloat16), "expert").astype(jnp.float32),
        lax.psum(shared[3].astype(jnp.bfloat16), "expert").astype(jnp.float32),
    )
    norm_sum, attend_sum, output_sum, router_sum = (
        lax.psum_scatter(
            summed[0].astype(jnp.bfloat16), "dp", scatter_dimension=1, tiled=True
        ).astype(jnp.float32),
        lax.psum_scatter(
            summed[1].astype(jnp.bfloat16), "dp", scatter_dimension=0, tiled=True
        ).astype(jnp.float32),
        lax.psum_scatter(
            summed[2].astype(jnp.bfloat16), "dp", scatter_dimension=0, tiled=True
        ).astype(jnp.float32),
        lax.psum_scatter(
            summed[3].astype(jnp.bfloat16), "dp", scatter_dimension=2, tiled=True
        ).astype(jnp.float32),
    )
    norm_new = adamw(norm_weight, norm_moment, norm_second, norm_sum, RATE_NORM)
    attend_new = adamw(attend_weight, attend_moment, attend_second, attend_sum, RATE_ATTEND)
    output_new = adamw(output_weight, output_moment, output_second, output_sum, RATE_OUTPUT)
    router_new = adamw(router_weight, router_moment, router_second, router_sum, RATE_ROUTER)
    expand_new = adamw(expand_weight, expand_moment, expand_second, expand_sum, RATE_EXPAND)
    reduce_new = adamw(reduce_weight, reduce_moment, reduce_second, reduce_sum, RATE_REDUCE)
    return (
        block_out,
        input_grad,
        norm_new[0],
        norm_new[1],
        norm_new[2],
        attend_new[0],
        attend_new[1],
        attend_new[2],
        output_new[0],
        output_new[1],
        output_new[2],
        router_new[0],
        router_new[1],
        router_new[2],
        expand_new[0],
        expand_new[1],
        expand_new[2],
        reduce_new[0],
        reduce_new[1],
        reduce_new[2],
    )


def solution(mesh):
    placed = (
        P("dp", "expert", None),
        P("dp", "expert", None),
        P("dp", None),
        P("dp", "expert"),
        P("dp", "expert", None),
        P(None, "dp"),
        P(None, "dp"),
        P(None, "dp"),
        P("dp", None),
        P("dp", None),
        P("dp", None),
        P("dp", None),
        P("dp", None),
        P("dp", None),
        P(None, None, "dp"),
        P(None, None, "dp"),
        P(None, None, "dp"),
        P("expert", None, None),
        P("expert", None, None),
        P("expert", None, None),
        P("expert", None, None),
        P("expert", None, None),
        P("expert", None, None),
    )
    fits = mesh.shape["dp"] == 8 and mesh.shape["expert"] == 4
    return jax.shard_map(
        fast_body if fits else body,
        mesh=mesh,
        in_specs=placed,
        out_specs=(
            P("dp", "expert", None),
            P("dp", "expert", None),
            P(None, "dp"),
            P(None, "dp"),
            P(None, "dp"),
            P("dp", None),
            P("dp", None),
            P("dp", None),
            P("dp", None),
            P("dp", None),
            P("dp", None),
            P(None, None, "dp"),
            P(None, None, "dp"),
            P(None, None, "dp"),
            P("expert", None, None),
            P("expert", None, None),
            P("expert", None, None),
            P("expert", None, None),
            P("expert", None, None),
            P("expert", None, None),
        ),
        check_vma=False,
    )
```

```python
import functools

import jax
import jax.numpy as jnp
import numpy as np
from jax import lax
from jax.experimental import pallas as pl
from jax.experimental.pallas import tpu as pltpu
from jax.sharding import PartitionSpec as P

D = 384
HEADS = 6
HEAD_DIM = 64
FFN = 1536
EXPERTS = 16
TASKS = 2
TOP = 4
STEP = 10
CAP = 256
PAIRS = HEADS // 2
LANES = 128
WCOLS = 4 * D + LANES
INFO = 16
NORM_AT = 2 * EXPERTS
EXTRA = 64

NORM_EPS = 1e-06
ADAM_EPS = 1e-08
BETA_FIRST = 0.9
BETA_SECOND = 0.999
DECAY = 0.05
RATE_NORM = 0.5
RATE_ATTEND = 0.2
RATE_OUTPUT = 0.7
RATE_ROUTER = 0.06
RATE_EXPAND = 0.13
RATE_REDUCE = 0.25
MASKED = -1e30
F32 = jnp.float32
BF16 = jnp.bfloat16
LIGHT = pl.CostEstimate(flops=1, transcendentals=0, bytes_accessed=1)


def dot_nn(a, b):
    return lax.dot_general(a, b, (((1,), (0,)), ((), ())), preferred_element_type=F32)


def dot_nt(a, b):
    return lax.dot_general(a, b, (((1,), (1,)), ((), ())), preferred_element_type=F32)


def dot_tn(a, b):
    return lax.dot_general(a, b, (((0,), (0,)), ((), ())), preferred_element_type=F32)


def unit_rows(values):
    average = jnp.mean(values, axis=-1, keepdims=True)
    centred = values - average
    spread = jnp.mean(centred * centred, axis=-1, keepdims=True)
    scale = lax.rsqrt(spread + NORM_EPS)
    return centred * scale, scale


def eye(n):
    rows = lax.broadcasted_iota(jnp.int32, (n, n), 0)
    cols = lax.broadcasted_iota(jnp.int32, (n, n), 1)
    return (rows == cols).astype(F32).astype(BF16)


def norm_rows_of(full_ref):
    return dot_nt(eye(LANES), full_ref[:, 4 * D :])[NORM_AT : NORM_AT + 8]


def vmem():
    return pl.BlockSpec(memory_space=pltpu.VMEM)


def smem():
    return pl.BlockSpec(memory_space=pltpu.SMEM)


def room(mebibytes):
    return pltpu.CompilerParams(vmem_limit_bytes=mebibytes * 2**20)


def whole(shape):
    return pl.BlockSpec(shape, lambda *_: (0,) * len(shape), pipeline_mode=pl.Buffered(1))


def far(value):
    return pltpu.with_memory_space_constraint(value, pltpu.HBM)


def once(kernel, scalars, arrays, outs, name, mebibytes, scratch=()):
    return pl.pallas_call(
        kernel,
        grid=(1,),
        in_specs=[smem()] * len(scalars) + [whole(a.shape) for a in arrays],
        out_specs=tuple(whole(o[0]) for o in outs),
        out_shape=tuple(jax.ShapeDtypeStruct(*o) for o in outs),
        scratch_shapes=[pltpu.VMEM(*held) for held in scratch],
        compiler_params=room(mebibytes),
        cost_estimate=LIGHT,
        name=name,
    )(*scalars, *arrays)


def place_table(count, shard_rows):
    table = np.zeros((32, 48), np.int32)
    for place in range(8):
        for member in range(4):
            tall, core = place // 2, place % 2
            row = table[place * 4 + member]
            row[0:3] = member * count, core, tall in (1, 2)
            for d in range(4):
                row[4 + d] = member ^ d
                row[16 + d] = shard_rows * (2 * (tall ^ d) + core)
                row[20 + d] = shard_rows * (2 * (tall ^ d) + 1 - core)
            for owner in range(8):
                row[28 + owner] = shard_rows * ((owner % 2 ^ core) * 4 + (owner // 2 ^ tall))
    return table


def wanted(meta, ends, d):
    rows = ends.shape[1] // 4
    here, there = meta[4] * rows, meta[4 + d] * rows
    return (ends[0, there] <= ends[0, here + rows - 1]) & (ends[0, there + rows - 1] >= ends[0, here])


def images_of(meta, image, d):
    rows = image.shape[1] // 4
    return image[0:1, pl.ds(pl.multiple_of(meta[4 + d] * rows, LANES), rows)].astype(F32)


def pack_kernel(
    patches, routes, tasks, attend, output, router, norm, own, shard, square,
):
    rows = patches.shape[1]
    shard_rows = attend.shape[0]
    shard[:, 0 : 3 * D] = attend[...].astype(BF16)
    shard[:, 3 * D : 4 * D] = output[...].astype(BF16)
    square[...] = jnp.zeros_like(square)
    for t in range(TASKS):
        square[t * EXPERTS : (t + 1) * EXPERTS, 0:shard_rows] = router[t]
    square[NORM_AT : NORM_AT + 4, 0:shard_rows] = norm[...]
    shard[:, 4 * D :] = jnp.transpose(square[...])[:shard_rows].astype(BF16)
    own[0:rows, :] = patches[0]
    lists = jnp.concatenate([routes[...].astype(F32), tasks[...].astype(F32)], axis=0)
    rest = jnp.concatenate([lists[:, D:], jnp.zeros((TOP + 1, 2 * D - rows), F32)], axis=1)
    lines = []
    for k in range(TOP + 1):
        lines = lines + [lists[k : k + 1, :D], rest[k : k + 1]]
    lines = lines + [jnp.zeros((INFO - 2 * (TOP + 1), D), F32)]
    own[rows : rows + INFO, :] = jnp.concatenate(lines, axis=0).astype(BF16)


def pack_call(patches, routes, tasks, attend, output, router, norm):
    rows = patches.shape[1]
    return once(
        pack_kernel, (), tuple(map(far, (patches, routes, tasks, attend, output, router, norm))),
        (((rows + INFO, D), BF16), ((attend.shape[0], WCOLS), BF16)),
        "pack", 12, (((LANES, LANES), F32),),
    )


def join_kernel(s0, s1, s2, s3, joined):
    part = s0.shape[0]
    for d, ref in enumerate((s0, s1, s2, s3)):
        joined[d * part : (d + 1) * part, :] = ref[...]


def join_call(shards):
    rows, cols = shards[0].shape
    return once(join_kernel, (), shards, (((4 * rows, cols), BF16),), "join", 12)[0]


def route_kernel(meta, i0, i1, i2, i3, row_out, pick_out, col_out, plan_out):
    base = meta[0]
    rows = i0.shape[1] + LANES
    later = lax.broadcasted_iota(jnp.int32, (rows, rows), 0)
    token = lax.broadcasted_iota(jnp.int32, (rows, rows), 1)
    before = (later < token).astype(F32).astype(BF16)
    one = (later == token).astype(F32).astype(BF16)
    local = row_out.shape[0]
    which = lax.broadcasted_iota(jnp.int32, (local, rows), 0)
    slot_names = (which + base).astype(F32)
    every = lax.broadcasted_iota(jnp.int32, (EXPERTS, rows), 0).astype(F32)
    experts = plan_out.shape[0] // 8
    starts = [jnp.int32(0)] * experts
    for d, ref in enumerate((i0, i1, i2, i3)):
        info = ref[...].astype(F32)

        def line(k):
            return jnp.concatenate([info[2 * k : 2 * k + 1], info[2 * k + 1 : 2 * k + 2, :LANES]], axis=1)

        mine = jnp.zeros((local, rows), jnp.bool_)
        chosen = jnp.zeros((EXPERTS, rows), jnp.bool_)
        for k in range(TOP):
            named = line(k)
            mine = mine | (slot_names == named)
            chosen = chosen | (every == named)
        mine = jnp.where(mine & (which < experts), 1.0, 0.0)
        chosen = jnp.where(chosen, 1.0, 0.0)
        rank = dot_nn(mine.astype(BF16), before)
        spot = jnp.where(mine > 0.5, rank, -1.0)
        at = slice(d * rows, (d + 1) * rows)
        row_out[:, at] = spot
        tasks = jnp.broadcast_to(line(TOP), (8, rows))
        pick_out[0:EXPERTS, at] = chosen
        pick_out[EXPERTS:, at] = tasks
        table = jnp.concatenate(
            [spot, jnp.zeros((16 - local, rows), F32), chosen, tasks, jnp.zeros((LANES - 40, rows), F32)],
            axis=0,
        )
        col_out[d * rows : (d + 1) * rows, :] = dot_nt(one, table.astype(BF16))
        for e in range(experts):
            held = jnp.sum(mine[e : e + 1, :]).astype(jnp.int32)
            plan_out[e * 8 + d] = starts[e]
            starts[e] = starts[e] + (held + 15) // 16 * 16
    for e in range(experts):
        plan_out[e * 8 + 4] = starts[e]
        plan_out[e * 8 + 5] = (starts[e] + CAP - 1) // CAP


def route_call(meta, pieces, experts):
    rows = pieces[0].shape[0] - INFO
    return pl.pallas_call(
        route_kernel,
        grid=(1,),
        in_specs=[smem()] + [pl.BlockSpec((INFO, D), lambda i: (rows // INFO, 0))] * 4,
        out_specs=(
            pl.BlockSpec((8, 4 * rows), lambda i: (0, 0)),
            pl.BlockSpec((EXPERTS + 8, 4 * rows), lambda i: (0, 0)),
            pl.BlockSpec((4 * rows, LANES), lambda i: (0, 0)),
            smem(),
        ),
        out_shape=(
            jax.ShapeDtypeStruct((8, 4 * rows), F32),
            jax.ShapeDtypeStruct((EXPERTS + 8, 4 * rows), F32),
            jax.ShapeDtypeStruct((4 * rows, LANES), F32),
            jax.ShapeDtypeStruct((experts * 8,), jnp.int32),
        ),
        compiler_params=room(24),
        cost_estimate=LIGHT,
        name="routing",
    )(meta, *pieces)


def front_kernel(
    meta, ends, image, p0, p1, p2, p3, near, away,
    qkv, full, att, lse_col, lse_row, middle, mixed,
    everything, scores, top, total, out_acc,
):
    rows = att.shape[0]
    part = near.shape[0] // 4
    for j in range(8):
        held = (near, away)[j // 4]
        full[pl.ds(pl.multiple_of(meta[16 + j], 16), part), :] = held[j % 4 * part : (j % 4 + 1) * part, :]
    for d, ref in enumerate((p0, p1, p2, p3)):
        everything[d * rows : (d + 1) * rows, :] = ref[:rows, :]
    norms = norm_rows_of(full)
    tile = 256

    def project(i, carry):
        at = pl.ds(pl.multiple_of(i * tile, tile), tile)
        unit, _ = unit_rows(everything[at, :].astype(F32))
        normed = (unit * norms[0:1] + norms[1:2]).astype(BF16)
        for third in range(3):
            made = dot_nn(normed, full[:, third * D : (third + 1) * D]).astype(BF16)
            if third == 0:
                made = made * jnp.asarray(HEAD_DIM ** (-0.5), BF16)
            for part in range(PAIRS):
                qkv[third * PAIRS + part, at, :] = made[:, part * LANES : (part + 1) * LANES]
        return carry

    lax.fori_loop(0, 4 * rows // tile, project, 0)
    own_row = images_of(meta, image, 0)
    own_col = jnp.transpose(jnp.broadcast_to(own_row, (LANES, rows)))[:, :1]
    lane = lax.broadcasted_iota(jnp.int32, (rows, LANES), 1)
    lse_col[...] = jnp.zeros_like(lse_col)

    def pair_of_heads(pair, carry):
        sides = (lane < HEAD_DIM, lane >= HEAD_DIM)
        queries = [jnp.where(held, qkv[pair, 0:rows, :], jnp.zeros((), BF16)) for held in sides]
        top[...] = jnp.full_like(top, MASKED)

        def score(d, c):
            @pl.when(wanted(meta, ends, d))
            def _():
                key = qkv[PAIRS + pair, pl.ds(pl.multiple_of(d * rows, rows), rows), :]
                same = own_col == images_of(meta, image, d)
                for half in range(2):
                    raw = jnp.where(same, dot_nt(queries[half], key), MASKED)
                    scores[half, d] = raw
                    top[half] = jnp.maximum(top[half], jnp.max(raw, axis=1, keepdims=True))

            return c

        lax.fori_loop(0, 4, score, 0)
        total[...] = jnp.zeros_like(total)
        out_acc[...] = jnp.zeros_like(out_acc)
        peaks = (top[0], top[1])

        def weigh(d, c):
            @pl.when(wanted(meta, ends, d))
            def _():
                value = qkv[2 * PAIRS + pair, pl.ds(pl.multiple_of(d * rows, rows), rows), :]
                for half in range(2):
                    shares = jnp.exp(scores[half, d] - peaks[half])
                    total[half] += jnp.sum(shares, axis=1, keepdims=True)
                    out_acc[half] += dot_nn(shares.astype(BF16), value)

            return c

        lax.fori_loop(0, 4, weigh, 0)
        done = []
        for half in range(2):
            done.append(out_acc[half] / total[half])
            lse_col[...] = jnp.where(lane == 2 * pair + half, peaks[half] + jnp.log(total[half]), lse_col[...])
        att[:, pl.ds(pl.multiple_of(pair * LANES, LANES), LANES)] = jnp.where(lane < HEAD_DIM, done[0], done[1])
        return carry

    lax.fori_loop(0, PAIRS, pair_of_heads, 0)
    lse_row[...] = jnp.transpose(lse_col[...])[:8]
    branch = dot_nn(att[...].astype(BF16), full[:, 3 * D : 4 * D])
    centre = everything[0:rows, :].astype(F32) + branch
    middle[...] = centre
    unit, _ = unit_rows(centre)
    mixed[...] = (unit * norms[2:3] + norms[3:4]).astype(BF16)


def front_call(meta, image, pieces, shards):
    rows = pieces[0].shape[0] - INFO
    return once(
        front_kernel, (meta, image), tuple(map(far, (image, *pieces, *shards))),
        (
            ((3 * PAIRS, 4 * rows, LANES), BF16), ((D, WCOLS), BF16), ((rows, D), F32), ((rows, LANES), F32),
            ((8, rows), F32), ((rows, D), F32), ((rows, D), BF16),
        ),
        "front", 40,
        (
            ((4 * rows, D), BF16), ((2, 4, rows, rows), F32), ((2, rows, 1), F32), ((2, rows, 1), F32),
            ((2, rows, LANES), F32),
        ),
    )


def gate_rows(mix, router_rows, choice):
    both = dot_nt(router_rows, mix)
    open_ = choice[:EXPERTS] > 0.5
    logits = jnp.where(choice[EXPERTS : EXPERTS + 1] < 0.5, both[:EXPERTS], both[EXPERTS : 2 * EXPERTS])
    logits = jnp.where(open_, logits, MASKED)
    raised = jnp.where(open_, jnp.exp(logits - jnp.max(logits, axis=0, keepdims=True)), 0.0)
    return raised / jnp.sum(raised, axis=0, keepdims=True)


def expert_kernel(
    local, plan, meta, m0, m1, m2, m3, g0, g1, g2, g3, spot_row, choice, given, up, down,
    mine, other, results, gates_out,
    gates, hidden, upstream, gate_slots, sum_up, sum_down,
):
    core = meta[1]
    low_up, low_down = up.at[0], down.at[0]
    expert = meta[0] + local
    rows = m0.shape[0]
    mixes = (m0, m1, m2, m3)
    grads = (g0, g1, g2, g3)

    if local == 0:
        router_rows = jnp.transpose(given[:, 4 * D :])
        for d in range(4):
            at = slice(d * rows, (d + 1) * rows)
            gates[:, at] = gate_rows(mixes[d][...], router_rows, choice[:, at])
        gates_out[...] = gates[...]
    else:
        gates[...] = given[...]
        gates_out[...] = jnp.zeros_like(gates_out)
    slot_at = lax.broadcasted_iota(jnp.int32, (CAP, rows), 0).astype(F32)
    lane = lax.broadcasted_iota(jnp.int32, (CAP, LANES), 1)
    for d in range(4):
        at = slice(d * rows, (d + 1) * rows)
        hit = slot_at == spot_row[local : local + 1, at]
        pick = jnp.where(hit, 1.0, 0.0).astype(BF16)
        gate = jnp.sum(jnp.where(hit, gates[pl.ds(expert, 1), at], 0.0), axis=1, keepdims=True)
        start = pl.multiple_of(plan[local * 8 + d], 16)
        hidden[pl.ds(start, CAP), :] = dot_nn(pick, mixes[d][...]).astype(BF16)
        upstream[pl.ds(start, CAP), :] = (gate * dot_nn(pick, grads[d][...])).astype(BF16)
        gate_slots[pl.ds(start, CAP), :] = jnp.broadcast_to(gate, (CAP, LANES))
    ending = pl.multiple_of(plan[local * 8 + 4], 16)
    hidden[pl.ds(ending, CAP), :] = jnp.zeros((CAP, D), BF16)
    upstream[pl.ds(ending, CAP), :] = jnp.zeros((CAP, D), BF16)
    gate_slots[pl.ds(ending, CAP), :] = jnp.zeros((CAP, LANES), F32)
    sum_up[...] = jnp.zeros_like(sum_up)
    sum_down[...] = jnp.zeros_like(sum_down)
    wide = 512

    def tile(i, carry):
        at = pl.ds(pl.multiple_of(i * CAP, CAP), CAP)
        x = hidden[at, :]
        g = upstream[at, :]
        x_t = jnp.transpose(x)
        g_t = jnp.transpose(g)
        made = jnp.zeros((CAP, D), F32)
        back = jnp.zeros((CAP, D), F32)
        for j in range(FFN // wide):
            cols = slice(j * wide, (j + 1) * wide)
            pre = dot_nn(x, low_up[:, cols])
            pull = dot_nt(g, low_down[cols, :])
            share = 0.5 + 0.5 * lax.erf(pre * 0.7071067811865476)
            active = (pre * share).astype(BF16)
            slope = share + pre * (0.3989422804014327 * jnp.exp(-0.5 * pre * pre))
            pre_grad = (slope * pull).astype(BF16)
            made = made + dot_nn(active, low_down[cols, :])
            back = back + dot_nt(pre_grad, low_up[:, cols])
            sum_up[:, cols] += dot_nn(x_t, pre_grad)
            sum_down[:, cols] += dot_nn(g_t, active)
        results[at, 0:D] = (gate_slots[at, 0:1] * made).astype(BF16)
        results[at, D : 2 * D] = back.astype(BF16)
        term = jnp.sum(g.astype(F32) * made, axis=1, keepdims=True)
        high = term.astype(BF16).astype(F32)
        ends = jnp.where(lane == expert, high, 0.0) + jnp.where(lane == 32 + expert, term - high, 0.0)
        results[at, 2 * D :] = ends.astype(BF16)
        return carry

    count = plan[local * 8 + 5]
    lax.fori_loop(0, count, tile, 0)
    results[pl.ds(pl.multiple_of(count * CAP, CAP), CAP), :] = jnp.zeros((CAP, 2 * D + LANES), BF16)
    half = FFN // 2
    quarter = D // 2

    for ref, side in ((mine, core), (other, 1 - core)):
        for b in range(2):
            cols = pl.ds(pl.multiple_of(side * half + b * D, LANES), D)
            ref[b * D : (b + 1) * D, :] = sum_down[:, cols].astype(BF16)
        held = sum_up[pl.ds(pl.multiple_of(side * quarter, 16), quarter), :].astype(BF16)
        for b in range(4):
            ref[half + b * quarter : half + (b + 1) * quarter, :] = held[:, b * D : (b + 1) * D]


def expert_call(local, plan, meta, mixes, grads, spot_row, choice, given, up, down):
    rows = mixes[0].shape[0]
    slots = 4 * CAP + CAP
    cols = 2 * D + LANES
    return pl.pallas_call(
        functools.partial(expert_kernel, local),
        grid=(1,),
        in_specs=[smem()] * 2
        + [whole((rows, D))] * 8
        + [
            whole((8, 4 * rows)),
            whole((EXPERTS + 8, 4 * rows)),
            whole(given.shape),
            pl.BlockSpec((1, D, FFN), lambda _: (local, 0, 0), pipeline_mode=pl.Buffered(1)),
            pl.BlockSpec((1, FFN, D), lambda _: (local, 0, 0), pipeline_mode=pl.Buffered(1)),
        ],
        out_specs=(whole((4 * D, D)), whole((4 * D, D)), whole((slots, cols)), whole((EXPERTS, 4 * rows))),
        out_shape=(
            jax.ShapeDtypeStruct((4 * D, D), BF16),
            jax.ShapeDtypeStruct((4 * D, D), BF16),
            jax.ShapeDtypeStruct((slots, cols), BF16),
            jax.ShapeDtypeStruct((EXPERTS, 4 * rows), F32),
        ),
        scratch_shapes=[
            pltpu.VMEM((EXPERTS, 4 * rows), F32),
            pltpu.VMEM((slots, D), BF16),
            pltpu.VMEM((slots, D), BF16),
            pltpu.VMEM((slots, LANES), F32),
            pltpu.VMEM((D, FFN), F32),
            pltpu.VMEM((D, FFN), F32),
        ],
        compiler_params=room(36),
        cost_estimate=LIGHT,
        name="experts",
    )(plan, meta, *mixes, *grads, spot_row, choice, given, far(up), far(down))


def combine_kernel(
    plan, m0, m1, m2, m3, spot_col, gates, full, res0, res1, res2, res3,
    b0, b1, b2, b3, x0, x1, x2, x3, router_out,
    stack,
):
    rows = m0.shape[0]
    lane = lax.broadcasted_iota(jnp.int32, (rows, LANES), 1)
    slot_along = lax.broadcasted_iota(jnp.int32, (rows, CAP), 1).astype(F32)
    routers = jnp.concatenate([full[:, 4 * D :], full[:, 4 * D :]], axis=1)
    total = jnp.zeros((D, 2 * LANES), F32)
    for d, (mix, back_out, mix_out) in enumerate(((m0, b0, x0), (m1, b1, x1), (m2, b2, x2), (m3, b3, x3))):
        at = slice(d * rows, (d + 1) * rows)
        info = spot_col[at, :]
        puts = []
        for e in range(4):
            start = pl.multiple_of(plan[e * 8 + d], 16)
            stack[e * CAP : (e + 1) * CAP, :] = (res0, res1, res2, res3)[e][pl.ds(start, CAP), :]
            puts.append(jnp.where(slot_along == info[:, e : e + 1], 1.0, 0.0).astype(BF16))
        got = dot_nn(jnp.concatenate(puts, axis=1), stack[...])
        mix_out[...] = got[:, :D].astype(BF16)
        ends = got[:, 2 * D :]
        held = jnp.where(lane < EXPERTS, ends + pltpu.roll(ends, LANES - 32, 1), 0.0)
        gate = jnp.transpose(
            jnp.concatenate([gates[:, at], jnp.zeros((LANES - EXPERTS, rows), F32)], axis=0)
        )
        change = held - jnp.sum(held, axis=1, keepdims=True) * gate
        task = info[:, 32:33]
        early = jnp.where((lane < EXPERTS) & (task < 0.5), change, 0.0)
        late = jnp.where(
            (lane >= EXPERTS) & (lane < 2 * EXPERTS) & (task > 0.5), pltpu.roll(change, EXPERTS, 1), 0.0
        )
        both = early + late
        high = both.astype(BF16)
        low = (both - high.astype(F32)).astype(BF16)
        parts = jnp.concatenate([high, low], axis=1)
        pulled = dot_nt(parts, routers)
        total = total + dot_tn(mix[...], parts)
        back_out[...] = (got[:, D : 2 * D] + pulled).astype(BF16)
    router_out[...] = total[:, :LANES] + total[:, LANES:]


def combine_call(plan, mixes, spot_col, gates, full, results):
    rows = mixes[0].shape[0]
    return once(
        combine_kernel, (plan,), (*mixes, spot_col, gates, full, *results),
        (((rows, D), BF16),) * 8 + (((D, LANES), F32),),
        "combine", 40, (((4 * CAP, 2 * D + LANES), BF16),),
    )


def turn_kernel(b0, r1, r2, r3, middle, grad, full, att, lse_row, middle_grad, sent, dots_col, output_grad, norm_two):
    rows = middle.shape[0]
    norms = norm_rows_of(full)
    mixed_grad = b0[...].astype(F32) + r1[...].astype(F32) + r2[...].astype(F32) + r3[...].astype(F32)
    unit, scale = unit_rows(middle[...])
    norm_two[...] = jnp.zeros_like(norm_two)
    norm_two[0:1, :] = jnp.sum(mixed_grad * unit, axis=0, keepdims=True)
    norm_two[1:2, :] = jnp.sum(mixed_grad, axis=0, keepdims=True)
    pulled = mixed_grad * norms[2:3]
    through = pulled - jnp.mean(pulled, axis=1, keepdims=True)
    through = scale * (through - unit * jnp.mean(pulled * unit, axis=1, keepdims=True))
    whole = through + grad[...].astype(F32)
    middle_grad[...] = whole
    branch = whole.astype(BF16)
    output_grad[...] = dot_tn(att[...].astype(BF16), branch).astype(BF16)
    pulled = dot_nt(branch, full[:, 3 * D : 4 * D]).astype(BF16)
    sent[0:rows, :] = pulled
    product = pulled.astype(F32) * att[...]
    high = product.astype(BF16)
    low = (product - high.astype(F32)).astype(BF16)
    heads = (
        lax.broadcasted_iota(jnp.int32, (D, LANES), 0) // HEAD_DIM
        == lax.broadcasted_iota(jnp.int32, (D, LANES), 1)
    )
    heads = heads.astype(F32).astype(BF16)
    dots = dot_nn(high, heads) + dot_nn(low, heads)
    dots_col[...] = dots
    lines = jnp.concatenate([lse_row[...], jnp.transpose(dots)[:8]], axis=0)
    high = lines.astype(BF16).astype(F32)
    table = jnp.concatenate([high, lines - high], axis=0).astype(BF16)
    half = EXTRA // 2
    sent[rows : rows + half, :] = table[:, :D]
    sent[rows + half : rows + EXTRA, :] = jnp.zeros((half, D), BF16)
    sent[rows + half : rows + EXTRA, : rows - D] = table[:, D:]


def turn_call(back, received, middle, grad, full, att, lse_row):
    rows = middle.shape[0]
    return once(
        turn_kernel, (), (back, *received, middle, grad, full, att, lse_row),
        (((rows, D), F32), ((rows + EXTRA, D), BF16), ((rows, LANES), F32), ((D, D), BF16), ((8, D), F32)),
        "turn", 24,
    )


def attention_back_kernel(
    meta, ends, image, qkv, s0, s1, s2, s3, lse_col, dots_col, own, full, middle_grad, output_grad, norm_two, routers,
    input_grad, to0, to1, to2, to3,
    lines, grads, packed, acc_one, acc_two, shared,
):
    rows = input_grad.shape[0]
    half_extra = EXTRA // 2
    for d, ref in enumerate((s0, s1, s2, s3)):
        grads[d] = ref[0:rows, :]
        table = jnp.concatenate(
            [ref[rows : rows + half_extra, :], ref[rows + half_extra : rows + EXTRA, : rows - D]], axis=1
        ).astype(F32)
        lines[d] = table[:16] + table[16:]
    own_row = images_of(meta, image, 0)
    own_col = jnp.transpose(jnp.broadcast_to(own_row, (LANES, rows)))[:, :1]
    lane = lax.broadcasted_iota(jnp.int32, (rows, LANES), 1)
    none = jnp.zeros((), BF16)
    here = slice(0, rows)

    def pair_of_heads(pair, carry):
        lanes = pl.ds(pl.multiple_of(pair * LANES, LANES), LANES)
        sides = (lane < HEAD_DIM, lane >= HEAD_DIM)
        queries = [jnp.where(held, qkv[pair, here, :], none) for held in sides]
        pulls = [jnp.where(held, grads[0, :, lanes], none) for held in sides]
        log_totals, all_dots = [
            [
                jnp.sum(jnp.where(lane == 2 * pair + half, table[...], 0.0), axis=1, keepdims=True)
                for half in range(2)
            ]
            for table in (lse_col, dots_col)
        ]
        acc_one[...] = jnp.zeros_like(acc_one)

        def over_keys(d, c):
            @pl.when(wanted(meta, ends, d))
            def _():
                at = pl.ds(pl.multiple_of(d * rows, rows), rows)
                key = qkv[PAIRS + pair, at, :]
                same = own_col == images_of(meta, image, d)
                for half in range(2):
                    shares = jnp.where(same, jnp.exp(dot_nt(queries[half], key) - log_totals[half]), 0.0)
                    change = dot_nt(pulls[half], qkv[2 * PAIRS + pair, at, :]) - all_dots[half]
                    acc_one[half] += dot_nn((shares * change).astype(BF16), key)

            return c

        lax.fori_loop(0, 4, over_keys, 0)
        packed[:, lanes] = jnp.where(lane < HEAD_DIM, acc_one[0], acc_one[1]) * (HEAD_DIM ** (-0.5))
        keys = [jnp.where(held, qkv[PAIRS + pair, here, :], none) for held in sides]
        values = [jnp.where(held, qkv[2 * PAIRS + pair, here, :], none) for held in sides]
        acc_one[...] = jnp.zeros_like(acc_one)
        acc_two[...] = jnp.zeros_like(acc_two)

        def over_queries(d, c):
            @pl.when(wanted(meta, ends, d))
            def _():
                at = pl.ds(pl.multiple_of(d * rows, rows), rows)
                query = qkv[pair, at, :]
                pull = grads[d, :, lanes]
                same = own_col == images_of(meta, image, d)
                for half in range(2):
                    log_total = lines[d, pl.ds(2 * pair + half, 1), :]
                    dots = lines[d, pl.ds(8 + 2 * pair + half, 1), :]
                    shares = jnp.where(same, jnp.exp(dot_nt(keys[half], query) - log_total), 0.0)
                    change = dot_nt(values[half], pull) - dots
                    acc_two[half] += dot_nn(shares.astype(BF16), pull)
                    acc_one[half] += dot_nn((shares * change).astype(BF16), query)

            return c

        lax.fori_loop(0, 4, over_queries, 0)
        made = [(acc_one[half], acc_two[half]) for half in range(2)]
        shift = pl.ds(pl.multiple_of(D + pair * LANES, LANES), LANES)
        packed[:, shift] = jnp.where(lane < HEAD_DIM, made[0][0], made[1][0])
        shift = pl.ds(pl.multiple_of(2 * D + pair * LANES, LANES), LANES)
        packed[:, shift] = jnp.where(lane < HEAD_DIM, made[0][1], made[1][1])
        return carry

    lax.fori_loop(0, PAIRS, pair_of_heads, 0)
    norms = norm_rows_of(full)
    unit, scale = unit_rows(own[0:rows, :].astype(F32))
    normed = (unit * norms[0:1] + norms[1:2]).astype(BF16)
    normed_grad = jnp.zeros((rows, D), F32)
    for third in range(3):
        part = packed[:, third * D : (third + 1) * D].astype(BF16)
        normed_grad = normed_grad + dot_nt(part, full[:, third * D : (third + 1) * D])
        weight_grad = dot_tn(normed, part).astype(BF16)
        for j in range(PAIRS):
            block = third * PAIRS + j
            shared[meta[4 + block // 4], :, block % 4 * LANES : (block % 4 + 1) * LANES] = weight_grad[
                :, j * LANES : (j + 1) * LANES
            ]
    pulled = normed_grad * norms[0:1]
    through = pulled - jnp.mean(pulled, axis=1, keepdims=True)
    through = scale * (through - unit * jnp.mean(pulled * unit, axis=1, keepdims=True))
    input_grad[...] = through + middle_grad[...]
    for j in range(PAIRS):
        block = 3 * PAIRS + j
        shared[meta[4 + block // 4], :, block % 4 * LANES : (block % 4 + 1) * LANES] = output_grad[
            :, j * LANES : (j + 1) * LANES
        ]
    lines_norm = jnp.concatenate(
        [
            jnp.zeros((NORM_AT, D), F32),
            jnp.sum(normed_grad * unit, axis=0, keepdims=True),
            jnp.sum(normed_grad, axis=0, keepdims=True),
            norm_two[0:2, :],
            jnp.zeros((LANES - NORM_AT - 4, D), F32),
        ],
        axis=0,
    )
    small = routers[...] + jnp.transpose(lines_norm)
    shared[meta[7], :, 0:LANES] = small.astype(BF16)
    shared[meta[7], :, LANES:] = jnp.zeros((D, 3 * LANES), BF16)
    part = D // 8
    for d, ref in enumerate((to0, to1, to2, to3)):
        for owner in range(8):
            at = pl.ds(pl.multiple_of(meta[28 + owner], 16), part)
            ref[at, :] = shared[d, owner * part : (owner + 1) * part, :]


def attention_back_call(meta, image, qkv, sent, lse_col, dots_col, own, full, middle_grad, output_grad, norm_two, routers):
    rows = middle_grad.shape[0]
    return once(
        attention_back_kernel, (meta, image),
        (image, qkv, *sent, lse_col, dots_col, own, full, middle_grad, output_grad, norm_two, routers),
        (((rows, D), F32),) + (((D, 4 * LANES), BF16),) * 4,
        "attention_back", 40,
        (
            ((4, 16, rows), F32), ((4, rows, D), BF16), ((rows, 3 * D), F32), ((2, rows, LANES), F32),
            ((2, rows, LANES), F32), ((4, D, 4 * LANES), BF16),
        ),
    )


def adamw(weight, moment, second, gradient, step_rate):
    moment = BETA_FIRST * moment + (1.0 - BETA_FIRST) * gradient
    second = BETA_SECOND * second + (1.0 - BETA_SECOND) * gradient * gradient
    spread = jnp.sqrt(second * (1.0 / (1.0 - BETA_SECOND**STEP))) + ADAM_EPS
    change = moment * (step_rate / (1.0 - BETA_FIRST**STEP)) / spread
    weight = weight * (1.0 - step_rate * DECAY) - change
    return (weight, moment, second)


def adam_kernel(meta, ready, passed, w1, m1, v1, w2, m2, v2, *rest):
    outs = rest[-6:]
    step = pl.program_id(0)
    half_steps = pl.num_programs(0) // 2
    mine = (step // half_steps) == meta[1]
    inner = step % half_steps
    up_rows, down_rows = w1.shape[1], w2.shape[1]
    half = FFN // 2
    quarter = D // 2

    def pick(rows_at, lanes_at):
        return jnp.where(mine, ready[rows_at, lanes_at], passed[rows_at, lanes_at]).astype(F32)

    per = D // down_rows
    down = pick(
        pl.ds(pl.multiple_of(inner // per * D, D), D), pl.ds(pl.multiple_of(inner % per * down_rows, LANES), down_rows)
    )
    up = jnp.concatenate(
        [
            pick(pl.ds(pl.multiple_of(half + b * quarter + inner * up_rows, 16), up_rows), slice(0, D))
            for b in range(4)
        ],
        axis=1,
    )
    for k, value in enumerate(adamw(w1[0], m1[0], v1[0], up, RATE_EXPAND)):
        outs[k][0] = value
    for k, value in enumerate(adamw(w2[0], m2[0], v2[0], jnp.transpose(down), RATE_REDUCE)):
        outs[3 + k][0] = value


def adam_call(expert, meta, ready, passed, states, previous):
    steps = 4
    up = pl.BlockSpec((1, D // steps, FFN), lambda i, *_: (expert, i, 0))
    down = pl.BlockSpec((1, FFN // steps, D), lambda i, *_: (expert, i, 0))
    specs = [whole(ready.shape)] * 2 + [up] * 3 + [down] * 3
    args = [ready, passed, *map(far, states)]
    aliases = {}
    if previous is not None:
        for k, value in enumerate(previous):
            aliases[1 + len(args)] = k
            args.append(value)
            specs.append(pl.BlockSpec(memory_space=pl.ANY))
    return pl.pallas_call(
        adam_kernel,
        grid_spec=pltpu.PrefetchScalarGridSpec(
            num_scalar_prefetch=1,
            grid=(steps,),
            in_specs=specs,
            out_specs=(up,) * 3 + (down,) * 3,
        ),
        out_shape=tuple(jax.ShapeDtypeStruct(s.shape, F32) for s in states),
        input_output_aliases=aliases,
        compiler_params=room(28),
        cost_estimate=LIGHT,
        name="adam",
    )(meta, *args)


def fold_kernel(a, b, c, d, kept, gone):
    rows = kept.shape[0]
    for ref, at in ((kept, slice(0, rows)), (gone, slice(rows, 2 * rows))):
        ref[...] = (
            a[at, :].astype(F32) + b[at, :].astype(F32) + c[at, :].astype(F32) + d[at, :].astype(F32)
        ).astype(BF16)


def fold_call(parts):
    rows, cols = parts[0].shape
    return once(fold_kernel, (), parts, (((rows // 2, cols), BF16),) * 2, "fold", 8)


def split_kernel(kept, came, *outs):
    for k, ref in enumerate(outs):
        at = slice(k * ref.shape[0], (k + 1) * ref.shape[0])
        ref[...] = (kept[at, :].astype(F32) + came[at, :].astype(F32)).astype(BF16)


def split_call(kept, came):
    rows, cols = kept.shape
    return once(split_kernel, (), (kept, came), (((rows // 4, cols), BF16),) * 4, "split", 8)


def settle_kernel(meta, *refs):
    pieces, states, outs, (buffer, square) = refs[:4], refs[4:16], refs[16:28], refs[28:]
    rows = pieces[0].shape[0]
    for d in range(4):
        buffer[meta[4 + d]] = pieces[d][...].astype(F32)
    square[...] = jnp.zeros_like(square)
    square[0:rows, :] = buffer[3, :, 0:LANES]
    turned = jnp.transpose(square[...])
    attend_sum = jnp.concatenate([buffer[0], buffer[1], buffer[2, :, 0:LANES]], axis=1)
    sums = (turned[NORM_AT : NORM_AT + 4, :rows], attend_sum, buffer[2, :, LANES:])
    for k, (total, rate) in enumerate(zip(sums, (RATE_NORM, RATE_ATTEND, RATE_OUTPUT))):
        held = [ref[...] for ref in states[3 * k : 3 * k + 3]]
        for ref, value in zip(outs[3 * k : 3 * k + 3], adamw(*held, total, rate)):
            ref[...] = value
    for t in range(TASKS):
        held = [ref[t] for ref in states[9:12]]
        total = turned[t * EXPERTS : (t + 1) * EXPERTS, :rows]
        for ref, value in zip(outs[9:12], adamw(*held, total, RATE_ROUTER)):
            ref[t] = value


def settle_call(meta, pieces, states):
    rows, cols = pieces[0].shape
    return once(
        settle_kernel, (meta,), (*pieces, *map(far, states)), tuple((s.shape, F32) for s in states),
        "settle", 12, (((4, rows, cols), F32), ((LANES, LANES), F32)),
    )


def swap_expert(value, d):
    return lax.ppermute(value, "expert", [(i, i ^ d) for i in range(4)])


def swap_tall(value, d):
    return lax.ppermute(value, "dp", [(2 * a + c, 2 * (a ^ d) + c) for a in range(4) for c in range(2)])


def swap_core(value):
    return lax.ppermute(value, "dp", [(i, i ^ 1) for i in range(8)])


def send_tall(value, hops):
    return lax.ppermute(value, "dp", [(2 * a + c, 2 * b + c) for a, b in hops for c in range(2)])


def tie(value, *others):
    flat, tree = jax.tree.flatten((value, others))
    return jax.tree.unflatten(tree, lax.optimization_barrier(flat))[0]


def fast_body(
    patches, out_grad, image_of, task_of, routes,
    norm_weight, norm_moment, norm_second,
    attend_weight, attend_moment, attend_second,
    output_weight, output_moment, output_second,
    router_weight, router_moment, router_second,
    expand_weight, expand_moment, expand_second,
    reduce_weight, reduce_moment, reduce_second,
):
    member = lax.axis_index("expert")
    place = lax.axis_index("dp")
    rows = patches.shape[1]
    count = expand_weight.shape[0]
    table = place_table(count, attend_weight.shape[0])
    meta = lax.dynamic_index_in_dim(jnp.asarray(table), place * 4 + member, 0, False)
    inner = (place >= 2) & (place < 6)
    image = image_of

    own, shard = pack_call(patches, routes[0].T, task_of, attend_weight, output_weight, router_weight, norm_weight)
    shards = [shard] + [swap_tall(shard, d) for d in (1, 2, 3)]
    pieces = [own] + [swap_expert(own, d) for d in (1, 2, 3)]
    near = join_call(shards)
    shards = [near, swap_core(near)]
    grad = out_grad[0]
    grads = [grad] + [swap_expert(tie(grad, *pieces[1:]), d) for d in (1, 2, 3)]

    qkv, full, att, lse_col, lse_row, middle, mixed = front_call(meta, image, pieces, shards)
    mixes = [mixed] + [swap_expert(mixed, d) for d in (1, 2, 3)]
    spot_row, choice, spot_col, plan = route_call(meta, pieces, count)

    up_low = tie(expand_weight, mixed).astype(BF16)
    down_low = tie(reduce_weight, mixed).astype(BF16)

    def first_hop(value):
        return send_tall(value, ((0, 1), (3, 2)))

    def second_hop(value):
        return send_tall(value, ((1, 2), (2, 1)))

    def third_hop(value):
        return send_tall(value, ((1, 0), (2, 3)))

    def settled(value, came):
        return jnp.where(inner, value, came)

    def expert(local, given):
        return expert_call(local, plan, meta, mixes, grads, spot_row, choice, given, up_low, down_low)

    mine0, other0, res0, gates = expert(0, full)
    half0 = mine0 + swap_core(other0)
    came_a0 = first_hop(half0)
    mine1, other1, res1, _ = expert(1, tie(gates, half0))
    got1 = swap_core(other1)
    mine2, other2, res2, _ = expert(2, tie(gates, mine1))
    got2 = swap_core(other2)
    pair0 = half0 + tie(came_a0, mine2)
    came_b0 = second_hop(pair0)
    half1 = mine1 + tie(got1, pair0)
    came_a1 = first_hop(half1)
    mine3, other3, res3, _ = expert(3, tie(gates, half1, pair0))
    got3 = swap_core(other3)
    half2 = mine2 + tie(got2, mine3)
    came_a2 = first_hop(half2)
    *outs, routers = combine_call(plan, mixes, spot_col, tie(gates, half2), full, (res0, res1, res2, res3))
    back, mix = outs[:4], outs[4:]
    returned = [swap_expert(back[d], d) for d in (1, 2, 3)]
    pair1 = half1 + tie(came_a1, routers)
    came_b1 = second_hop(pair1)
    whole0 = pair0 + tie(came_b0, routers)
    came_c0 = third_hop(whole0)
    half3 = mine3 + tie(got3, pair1, whole0)
    pair2 = half2 + tie(came_a2, half3, *returned)
    came_b2 = second_hop(pair2)
    came_a3 = first_hop(tie(half3, pair2))
    middle_grad, sent, dots_col, output_grad, norm_two = turn_call(
        tie(back[0], half3, pair2), returned, middle, grad, full, att, lse_row
    )
    sents = [sent] + [swap_expert(sent, d) for d in (1, 2)]
    whole1 = pair1 + tie(came_b1, norm_two)
    came_c1 = third_hop(whole1)
    ready0 = settled(whole0, tie(came_c0, norm_two))
    passed0 = swap_core(ready0)
    states = (expand_weight, expand_moment, expand_second, reduce_weight, reduce_moment, reduce_second)
    news = adam_call(0, meta, tie(ready0, pair2, whole1), passed0, states, None)
    sents.append(swap_expert(tie(sent, news[0]), 3))
    ready1 = settled(whole1, tie(came_c1, news[0], *sents[1:3]))
    passed1 = swap_core(ready1)
    pair3 = half3 + tie(came_a3, news[0], *sents[1:])
    came_b3 = second_hop(pair3)
    whole2 = pair2 + tie(came_b2, news[0])
    came_c2 = third_hop(whole2)
    input_grad, *shared = attention_back_call(
        meta, image, qkv, sents, tie(lse_col, pair3, whole2, ready1), dots_col, own, full, middle_grad,
        output_grad, norm_two, routers,
    )
    shared = [shared[0]] + [swap_expert(shared[d], d) for d in (1, 2, 3)]
    whole3 = pair3 + tie(came_b3, input_grad)
    came_c3 = third_hop(whole3)
    ready2 = settled(whole2, tie(came_c2, input_grad))
    passed1 = tie(passed1, whole3, ready2)
    news = adam_call(1, meta, ready1, passed1, states, news)
    kept, gone = fold_call([tie(shared[0], news[0])] + shared[1:])
    gone = swap_core(gone)
    ready3 = settled(whole3, tie(came_c3, kept))
    passed2 = tie(swap_core(tie(ready2, news[0])), ready3)
    piece, *away = split_call(kept, tie(gone, ready3))
    away = [swap_tall(away[d - 1], d) for d in (1, 2, 3)]
    news = adam_call(2, meta, tie(ready2, piece), passed2, states, news)
    piece = tie(piece, news[0]) + away[0] + away[1] + away[2]
    quarters = [piece] + [swap_expert(piece, d) for d in (1, 2, 3)]
    parts = [swap_expert(tie(mix[d], quarters[3]), d) for d in (1, 2, 3)]
    passed3 = swap_core(tie(ready3, kept))
    news = adam_call(3, meta, tie(ready3, piece), passed3, states, news)
    block_out = middle + tie(mix[0], news[0]).astype(F32)
    for part in parts:
        block_out = block_out + part.astype(F32)
    block_out = block_out.astype(BF16)[None]
    small = settle_call(
        meta, [tie(quarters[0], news[0])] + quarters[1:],
        (
            norm_weight, norm_moment, norm_second, attend_weight, attend_moment, attend_second,
            output_weight, output_moment, output_second, router_weight, router_moment, router_second,
        ),
    )
    return (block_out, input_grad[None], *small, *news)


def gelu_exact(values):
    return 0.5 * values * (1.0 + lax.erf(values * 0.7071067811865476))


def norm_rows(values, gain_row, offset):
    average = jnp.mean(values, axis=-1, keepdims=True)
    centred = values - average
    spread = jnp.mean(centred * centred, axis=-1, keepdims=True)
    return centred * lax.rsqrt(spread + NORM_EPS) * gain_row + offset


def body(
    patches,
    out_grad,
    image_of,
    task_of,
    routes,
    norm_weight,
    norm_moment,
    norm_second,
    attend_weight,
    attend_moment,
    attend_second,
    output_weight,
    output_moment,
    output_second,
    router_weight,
    router_moment,
    router_second,
    expand_weight,
    expand_moment,
    expand_second,
    reduce_weight,
    reduce_moment,
    reduce_second,
):
    precise = lax.Precision.HIGHEST
    member = lax.axis_index("expert")
    tokens = patches.shape[1]
    group_rows = image_of.shape[1]
    key_rows = min(512, group_rows)
    score_scale = HEAD_DIM ** (-0.5)
    norm_full, attend_full, output_full, router_full = (
        lax.all_gather(norm_weight.astype(jnp.bfloat16), "dp", axis=1, tiled=True),
        lax.all_gather(attend_weight.astype(jnp.bfloat16), "dp", axis=0, tiled=True),
        lax.all_gather(output_weight.astype(jnp.bfloat16), "dp", axis=0, tiled=True),
        lax.all_gather(router_weight.astype(jnp.bfloat16), "dp", axis=2, tiled=True),
    )
    norm_values = norm_full.astype(jnp.float32)
    router_values = router_full.astype(jnp.float32)
    expand_low = expand_weight.astype(jnp.bfloat16)
    reduce_low = reduce_weight.astype(jnp.bfloat16)
    inputs = patches[0].astype(jnp.float32)
    image_row = image_of[0]
    my_image = lax.dynamic_slice_in_dim(image_row, member * tokens, tokens)
    task_row = task_of[0]
    route_rows = routes[0]
    first_image = my_image[0]
    last_image = my_image[tokens - 1]
    first_key = jnp.sum((image_row < first_image).astype(jnp.int32))
    last_key = jnp.sum((image_row <= last_image).astype(jnp.int32)) - 1
    first_block = first_key // key_rows
    end_block = last_key // key_rows + 1
    normed_one, first_back = jax.vjp(norm_rows, inputs, norm_values[0], norm_values[1])
    normed_low = normed_one.astype(jnp.bfloat16)
    packed = jnp.dot(normed_low, attend_full, preferred_element_type=jnp.float32).astype(
        jnp.bfloat16
    )
    queries = packed[:, :D].reshape(tokens, HEADS, HEAD_DIM)
    key_value = packed[:, D:]
    key_value_all = lax.all_gather(key_value, "expert", axis=0, tiled=True)
    keys_all = key_value_all[:, :D].reshape(group_rows, HEADS, HEAD_DIM)
    values_all = key_value_all[:, D:].reshape(group_rows, HEADS, HEAD_DIM)

    def scores_of(query_part, key_part, same_image):
        raw = (
            jnp.einsum("thd,khd->htk", query_part, key_part, preferred_element_type=jnp.float32)
            * score_scale
        )
        return jnp.where(same_image[None], raw, MASKED)

    def block_at(block_index):
        first_row = block_index * key_rows
        key_part = lax.dynamic_slice_in_dim(keys_all, first_row, key_rows, 0)
        value_part = lax.dynamic_slice_in_dim(values_all, first_row, key_rows, 0)
        same_image = (
            my_image[:, None]
            == lax.dynamic_slice_in_dim(image_row, first_row, key_rows, 0)[None, :]
        )
        return (key_part, value_part, same_image)

    def max_step(block_index, state_in):
        highest, totals = state_in
        key_part, value_part, same_image = block_at(block_index)
        scores = scores_of(queries, key_part, same_image)
        raised = jnp.maximum(highest, jnp.max(scores, axis=-1))
        shares = jnp.where(same_image[None], jnp.exp(scores - raised[..., None]), 0.0)
        return (raised, totals * jnp.exp(highest - raised) + jnp.sum(shares, axis=-1))

    start_max = jnp.full((HEADS, tokens), MASKED, jnp.float32)
    highest, totals = lax.fori_loop(
        first_block, end_block, max_step, (start_max, jnp.zeros((HEADS, tokens), jnp.float32))
    )
    log_total = highest + jnp.log(totals)

    def value_step(block_index, accum):
        key_part, value_part, same_image = block_at(block_index)
        scores = scores_of(queries, key_part, same_image)
        soft_part = jnp.where(same_image[None], jnp.exp(scores - log_total[..., None]), 0.0).astype(
            jnp.bfloat16
        )
        return accum + jnp.einsum(
            "htk,khd->thd", soft_part, value_part, preferred_element_type=jnp.float32
        )

    attended = lax.fori_loop(
        first_block, end_block, value_step, jnp.zeros((tokens, HEADS, HEAD_DIM), jnp.float32)
    )
    attended_low = attended.reshape(tokens, D).astype(jnp.bfloat16)
    branch = jnp.dot(attended_low, output_full, preferred_element_type=jnp.float32)
    middle = inputs + branch
    normed_two, second_back = jax.vjp(norm_rows, middle, norm_values[2], norm_values[3])
    mixed_low = normed_two.astype(jnp.bfloat16)
    task_hot = (task_row[:, None] == jnp.arange(TASKS, dtype=jnp.int32)[None, :]).astype(
        jnp.float32
    )
    route_hot = (
        route_rows[:, :, None] == jnp.arange(EXPERTS, dtype=jnp.int32)[None, None, :]
    ).astype(jnp.float32)

    def gating(hidden, router):
        logits = jnp.einsum("td,ced->tce", hidden, router, precision=precise)
        task_logits = jnp.einsum("tc,tce->te", task_hot, logits, precision=precise)
        chosen = jnp.einsum("te,tke->tk", task_logits, route_hot, precision=precise)
        peak = jnp.max(chosen, axis=-1, keepdims=True)
        raised = jnp.exp(chosen - peak)
        return raised / jnp.sum(raised, axis=-1, keepdims=True)

    gate_values, gate_back = jax.vjp(gating, mixed_low.astype(jnp.float32), router_values)
    pair_expert = route_rows.reshape(-1)
    pair_hot = (pair_expert[:, None] == jnp.arange(EXPERTS, dtype=jnp.int32)[None, :]).astype(
        jnp.int32
    )
    slot_index = jnp.sum((jnp.cumsum(pair_hot, axis=0) - pair_hot) * pair_hot, axis=1)
    flat_slot = pair_expert * CAP + slot_index

    def scatter_pairs(pair_values):
        return (
            jnp.zeros((EXPERTS * CAP, D), pair_values.dtype)
            .at[flat_slot]
            .set(pair_values)
            .reshape(EXPERTS, CAP, D)
        )

    def gather_pairs(buffer):
        return (
            buffer.reshape(EXPERTS * CAP, D)[flat_slot].astype(jnp.float32).reshape(tokens, TOP, D)
        )

    received = lax.all_to_all(
        scatter_pairs(jnp.repeat(mixed_low, TOP, axis=0)),
        "expert",
        split_axis=0,
        concat_axis=1,
        tiled=True,
    )
    hidden_pre = jnp.einsum(
        "ecd,edh->ech", received, expand_low, preferred_element_type=jnp.float32
    )
    active, gelu_back = jax.vjp(gelu_exact, hidden_pre)
    active_low = active.astype(jnp.bfloat16)
    expert_out = jnp.einsum(
        "ech,ehd->ecd", active_low, reduce_low, preferred_element_type=jnp.float32
    ).astype(jnp.bfloat16)
    returned = lax.all_to_all(expert_out, "expert", split_axis=1, concat_axis=0, tiled=True)
    pair_out = gather_pairs(returned)
    expert_mix = jnp.einsum("tk,tkd->td", gate_values, pair_out, precision=precise)
    block_out = (middle + expert_mix).astype(jnp.bfloat16)[None]
    upstream = out_grad[0].astype(jnp.float32)
    gate_grad = jnp.sum(upstream[:, None, :] * pair_out, axis=-1)
    pair_grad = (
        (gate_values[:, :, None] * upstream[:, None, :])
        .astype(jnp.bfloat16)
        .reshape(tokens * TOP, D)
    )
    grad_in = lax.all_to_all(
        scatter_pairs(pair_grad), "expert", split_axis=0, concat_axis=1, tiled=True
    )
    reduce_grad = jnp.einsum(
        "ech,ecd->ehd", active_low, grad_in, preferred_element_type=jnp.float32
    )
    active_grad = jnp.einsum(
        "ecd,ehd->ech", grad_in, reduce_low, preferred_element_type=jnp.float32
    )
    pre_grad = gelu_back(active_grad)[0].astype(jnp.bfloat16)
    expand_grad = jnp.einsum("ecd,ech->edh", received, pre_grad, preferred_element_type=jnp.float32)
    back_rows = jnp.einsum(
        "ech,edh->ecd", pre_grad, expand_low, preferred_element_type=jnp.float32
    ).astype(jnp.bfloat16)
    expand_sum, reduce_sum = (
        lax.psum(expand_grad.astype(jnp.bfloat16), "dp").astype(jnp.float32),
        lax.psum(reduce_grad.astype(jnp.bfloat16), "dp").astype(jnp.float32),
    )
    came_back = lax.all_to_all(back_rows, "expert", split_axis=1, concat_axis=0, tiled=True)
    routed_grad = jnp.sum(gather_pairs(came_back), axis=1)
    hidden_gate_grad, router_grad = gate_back(gate_grad)
    middle_part, gain_two, offset_two = second_back(routed_grad + hidden_gate_grad)
    middle_grad = middle_part + upstream
    branch_grad = middle_grad.astype(jnp.bfloat16)
    output_grad = jnp.einsum(
        "td,te->de", attended_low, branch_grad, preferred_element_type=jnp.float32
    )
    attended_grad = (
        jnp.einsum("te,de->td", branch_grad, output_full, preferred_element_type=jnp.float32)
        .astype(jnp.bfloat16)
        .reshape(tokens, HEADS, HEAD_DIM)
    )
    row_dots = jnp.einsum(
        "thd,thd->ht", attended_grad.astype(jnp.float32), attended, precision=precise
    )

    def score_grad(query_part, key_part, value_part, grad_part, same_image, log_part, dots_part):
        scores = scores_of(query_part, key_part, same_image)
        soft_part = jnp.where(same_image[None], jnp.exp(scores - log_part[..., None]), 0.0)
        soft_grad = jnp.einsum(
            "thd,khd->htk", grad_part, value_part, preferred_element_type=jnp.float32
        )
        return (soft_part, (soft_part * (soft_grad - dots_part[..., None])).astype(jnp.bfloat16))

    def pair_step(block_index, state_in):
        query_acc, terms_acc = state_in
        key_part, value_part, same_image = block_at(block_index)
        soft_part, dscore = score_grad(
            queries, key_part, value_part, attended_grad, same_image, log_total, row_dots
        )
        query_acc = query_acc + jnp.einsum(
            "htk,khd->thd", dscore, key_part, preferred_element_type=jnp.float32
        )
        key_term = (
            jnp.einsum("htk,thd->khd", dscore, queries, preferred_element_type=jnp.float32)
            * score_scale
        )
        value_term = jnp.einsum(
            "htk,thd->khd",
            soft_part.astype(jnp.bfloat16),
            attended_grad,
            preferred_element_type=jnp.float32,
        )
        terms = jnp.concatenate(
            [key_term.reshape(key_rows, D), value_term.reshape(key_rows, D)], axis=1
        )
        terms_acc = lax.dynamic_update_slice_in_dim(terms_acc, terms, block_index * key_rows, 0)
        return (query_acc, terms_acc)

    query_acc, key_value_terms = lax.fori_loop(
        first_block,
        end_block,
        pair_step,
        (
            jnp.zeros((tokens, HEADS, HEAD_DIM), jnp.float32),
            jnp.zeros((group_rows, 2 * D), jnp.float32),
        ),
    )
    key_value_grad = lax.psum_scatter(
        key_value_terms.astype(jnp.bfloat16), "expert", scatter_dimension=0, tiled=True
    ).astype(jnp.float32)
    query_grad = (query_acc * score_scale).reshape(tokens, D)
    packed_grad = jnp.concatenate([query_grad, key_value_grad], axis=1).astype(jnp.bfloat16)
    attend_grad = jnp.einsum(
        "td,te->de", normed_low, packed_grad, preferred_element_type=jnp.float32
    )
    normed_grad = jnp.einsum(
        "te,de->td", packed_grad, attend_full, preferred_element_type=jnp.float32
    )
    input_part, gain_one, offset_one = first_back(normed_grad)
    input_grad = (middle_grad + input_part)[None]
    norm_grad = jnp.stack([gain_one, offset_one, gain_two, offset_two])
    shared = (norm_grad, attend_grad, output_grad, router_grad)
    summed = (
        lax.psum(shared[0].astype(jnp.bfloat16), "expert").astype(jnp.float32),
        lax.psum(shared[1].astype(jnp.bfloat16), "expert").astype(jnp.float32),
        lax.psum(shared[2].astype(jnp.bfloat16), "expert").astype(jnp.float32),
        lax.psum(shared[3].astype(jnp.bfloat16), "expert").astype(jnp.float32),
    )
    norm_sum, attend_sum, output_sum, router_sum = (
        lax.psum_scatter(
            summed[0].astype(jnp.bfloat16), "dp", scatter_dimension=1, tiled=True
        ).astype(jnp.float32),
        lax.psum_scatter(
            summed[1].astype(jnp.bfloat16), "dp", scatter_dimension=0, tiled=True
        ).astype(jnp.float32),
        lax.psum_scatter(
            summed[2].astype(jnp.bfloat16), "dp", scatter_dimension=0, tiled=True
        ).astype(jnp.float32),
        lax.psum_scatter(
            summed[3].astype(jnp.bfloat16), "dp", scatter_dimension=2, tiled=True
        ).astype(jnp.float32),
    )
    norm_new = adamw(norm_weight, norm_moment, norm_second, norm_sum, RATE_NORM)
    attend_new = adamw(attend_weight, attend_moment, attend_second, attend_sum, RATE_ATTEND)
    output_new = adamw(output_weight, output_moment, output_second, output_sum, RATE_OUTPUT)
    router_new = adamw(router_weight, router_moment, router_second, router_sum, RATE_ROUTER)
    expand_new = adamw(expand_weight, expand_moment, expand_second, expand_sum, RATE_EXPAND)
    reduce_new = adamw(reduce_weight, reduce_moment, reduce_second, reduce_sum, RATE_REDUCE)
    return (
        block_out,
        input_grad,
        norm_new[0],
        norm_new[1],
        norm_new[2],
        attend_new[0],
        attend_new[1],
        attend_new[2],
        output_new[0],
        output_new[1],
        output_new[2],
        router_new[0],
        router_new[1],
        router_new[2],
        expand_new[0],
        expand_new[1],
        expand_new[2],
        reduce_new[0],
        reduce_new[1],
        reduce_new[2],
    )


def solution(mesh):
    placed = (
        P("dp", "expert", None),
        P("dp", "expert", None),
        P("dp", None),
        P("dp", "expert"),
        P("dp", "expert", None),
        P(None, "dp"),
        P(None, "dp"),
        P(None, "dp"),
        P("dp", None),
        P("dp", None),
        P("dp", None),
        P("dp", None),
        P("dp", None),
        P("dp", None),
        P(None, None, "dp"),
        P(None, None, "dp"),
        P(None, None, "dp"),
        P("expert", None, None),
        P("expert", None, None),
        P("expert", None, None),
        P("expert", None, None),
        P("expert", None, None),
        P("expert", None, None),
    )
    fits = mesh.shape["dp"] == 8 and mesh.shape["expert"] == 4
    return jax.shard_map(
        fast_body if fits else body,
        mesh=mesh,
        in_specs=placed,
        out_specs=(
            P("dp", "expert", None),
            P("dp", "expert", None),
            P(None, "dp"),
            P(None, "dp"),
            P(None, "dp"),
            P("dp", None),
            P("dp", None),
            P("dp", None),
            P("dp", None),
            P("dp", None),
            P("dp", None),
            P(None, None, "dp"),
            P(None, None, "dp"),
            P(None, None, "dp"),
            P("expert", None, None),
            P("expert", None, None),
            P("expert", None, None),
            P("expert", None, None),
            P("expert", None, None),
            P("expert", None, None),
        ),
        check_vma=False,
    )
```
